32 devices in a mesh: tile: 4 (over y, core), pos: 8 (over z, x).
Axes of the slice: x: 2, y: 2, z: 4, core: 2. Of those that a mesh axis runs over, the one named last changes fastest.
Arguments:
- object_field: float32 [2048, 2, 512], P('tile'), may hold values from -5 to 5
- illumination: float32 [256, 2, 256], replicated, may hold values from -5 to 5
- amplitudes: bfloat16 [64, 256, 256], P(('tile', 'pos')), may hold values from 0.19921875 to 3
- row_offset: int32 [64], P(('tile', 'pos')), may hold values from 0 to 1792, as said below
- col_offset: int32 [64], P(('tile', 'pos')), may hold values from 0 to 256
Outputs:
- object_gradient: float32 [2048, 2, 512], P(('tile', 'pos'))
The draws below stay inside these ranges and needn't reach their ends.
Inputs may be any that keep to these rules, and one draw needn't show every extreme that they name: Position i lies in band b = i // 16: b * 512 <= row_offset[i] < (b + 1) * 512, and every window lies inside the object. Among the 2 positions of one device (an aligned block), at most 1 have row_offset[i] > (b + 1) * 512 - 256, so that their window reaches into band b + 1; in every draw some device has exactly 1 such positions; positions of the last band have none.
All inputs are finite; a program needn't handle non-finite values.
Results may differ from the reference program's by a relative error of at most 0.0003.
Values sent between devices are 32-bit elements; how exact they have to be, the bound alone decides.
No kernel may reach another device: no remote copies, remote signals or barrier semaphores. Data moves between devices by JAX's collectives and lax.ppermute only.
A program may use at most 64 MiB of HBM per device.

```python
import math
import jax
import jax.numpy as jnp
from jax import lax

WIN = 256
TH = 512
OW = 512
POS_DEV = 2
CROSS_MAX = 1
GROUP = 16
POSITIONS = 64
OH = 2048


def draw_row_offset(key, part):
    indices = jnp.arange(POSITIONS, dtype=jnp.int32)
    devices_total = POSITIONS // POS_DEV
    per_band = GROUP // POS_DEV
    band_count = POSITIONS // GROUP
    device_of = indices // POS_DEV
    slot_of = indices % POS_DEV
    band_of = indices // GROUP
    key_count, key_full, key_shift, key_low, key_high = jax.random.split(key, 5)
    crossing_count = jax.random.randint(key_count, (devices_total,), 0, CROSS_MAX + 1)
    chosen = jax.random.randint(key_full, (), 0, devices_total - per_band)
    device_ids = jnp.arange(devices_total, dtype=jnp.int32)
    crossing_count = jnp.where(device_ids == chosen, CROSS_MAX, crossing_count)
    crossing_count = jnp.where(device_ids // per_band == band_count - 1, 0, crossing_count)
    rotation = jax.random.randint(key_shift, (devices_total,), 0, POS_DEV)
    crosses = (slot_of + rotation[device_of]) % POS_DEV < crossing_count[device_of]
    inside = jax.random.randint(key_low, (POSITIONS,), 0, TH - WIN + 1)
    lowest_slot = (POS_DEV - 1 - rotation[0]) % POS_DEV
    inside = jnp.where(indices == lowest_slot, 0, inside)
    inside = jnp.where(indices == POSITIONS - 1, TH - WIN, inside)
    reaching = jax.random.randint(key_high, (POSITIONS,), TH - WIN + 1, TH)
    return (band_of * TH + jnp.where(crosses, reaching, inside)).astype(jnp.int32)


def with_ends(drawn, rng, smallest, top_value):
    spot = [jax.random.randint(jax.random.fold_in(rng, axis), (), 0, length) for axis, length in enumerate(drawn.shape)]
    widest = drawn.shape.index(max(drawn.shape))
    next_to = spot[:widest] + [(spot[widest] + 1) % drawn.shape[widest]] + spot[widest + 1:]
    return drawn.at[tuple(spot)].set(smallest).at[tuple(next_to)].set(top_value)


def block_scale(stream_key, dims, shards, least, top_value):
    factor_of = 1.0
    for dim, blocks in shards:
        steps = jax.random.uniform(jax.random.fold_in(jax.random.fold_in(stream_key, 6), dim), (blocks,), jnp.float32, least / len(shards), top_value / len(shards))
        factor_of = factor_of * jnp.repeat(jnp.exp(steps), dims[dim] // blocks).reshape((-1,) + (1,) * (len(dims) - 1 - dim))
    return factor_of


def scatter_about(rng, shape, scale, most, pieces=(), kind=jnp.bfloat16):
    drawn = jax.random.normal(rng, shape, jnp.float32) * scale
    if len(pieces) > 0:
        drawn = block_scale(rng, shape, pieces, -0.22, 0.18) * drawn
    return jnp.clip(drawn, min=-most, max=most).astype(kind)


def setup_inputs(seed: int = 0) -> dict:
    streams_of = jax.random.split(jax.random.key(seed), 6)
    object_field = scatter_about(streams_of[0], (OH, 2, OW), 0.7, 5.0, ((0, 4),), jnp.float32)
    illumination = scatter_about(streams_of[1], (WIN, 2, WIN), 0.7, 5.0, (), jnp.float32)
    amplitudes = jnp.clip(jnp.exp(math.log(3.0) - 2.7119641 * jax.random.uniform(streams_of[2], (POSITIONS, WIN, WIN), jnp.float32) ** block_scale(streams_of[2], (POSITIONS, WIN, WIN), ((0, 32),), -0.2, 0.2)), 0.19921875, 3.0).astype(jnp.bfloat16)
    row_offset = draw_row_offset(jax.random.fold_in(streams_of[5], 71), 0)
    col_offset = with_ends(jax.random.randint(streams_of[4], (POSITIONS,), 0, OW - WIN + 1), jax.random.fold_in(streams_of[4], 1), 0, OW - WIN).astype(jnp.int32)
    return dict(object_field=object_field, illumination=illumination, amplitudes=amplitudes, row_offset=row_offset, col_offset=col_offset)


def dft_tables(length):
    indices = jnp.arange(length, dtype=jnp.int32)
    product = indices[:, None] * indices[None, :] % length
    angles = product.astype(jnp.float32) * (2.0 * math.pi / length)
    factor = 1.0 / math.sqrt(length)
    return (jnp.cos(angles) * factor, jnp.sin(angles) * factor)

def apply_right(matrix, factor):
    return jnp.einsum('bij,jk->bik', matrix, factor, precision=lax.Precision.HIGHEST)

def apply_left(factor, matrix):
    return jnp.einsum('ij,bjk->bik', factor, matrix, precision=lax.Precision.HIGHEST)

def transform(real_part, imag_part, cos_table, sin_table, signum):
    mid_real = apply_right(real_part, cos_table) + signum * apply_right(imag_part, sin_table)
    mid_imag = apply_right(imag_part, cos_table) - signum * apply_right(real_part, sin_table)
    out_real = apply_left(cos_table, mid_real) + signum * apply_left(sin_table, mid_imag)
    out_imag = apply_left(cos_table, mid_imag) - signum * apply_left(sin_table, mid_real)
    return (out_real, out_imag)

def modulus(real_part, imag_part, amplitude):
    magnitude = jnp.sqrt(real_part * real_part + imag_part * imag_part)
    retain = 1.0 - amplitude.astype(jnp.float32) / jnp.maximum(magnitude, 0.25)
    return (real_part * retain, imag_part * retain)

def exit_wave(windows, illumination):
    obj_real = windows[:, :, 0, :]
    obj_imag = windows[:, :, 1, :]
    probe_real = illumination[:, 0, :]
    probe_imag = illumination[:, 1, :]
    return (probe_real * obj_real - probe_imag * obj_imag, probe_real * obj_imag + probe_imag * obj_real)

def far_gradient(exit_real, exit_imag, illumination, amplitude, cos_table, sin_table):
    far_real, far_imag = transform(exit_real, exit_imag, cos_table, sin_table, 1.0)
    diff_real, diff_imag = modulus(far_real, far_imag, amplitude)
    back_real, back_imag = transform(diff_real, diff_imag, cos_table, sin_table, -1.0)
    probe_real = illumination[:, 0, :]
    probe_imag = illumination[:, 1, :]
    grad_real = probe_real * back_real + probe_imag * back_imag
    grad_imag = probe_real * back_imag - probe_imag * back_real
    return jnp.stack([grad_real, grad_imag], axis=2)

def reference(object_field, illumination, amplitudes, row_offset, col_offset):
    cos_table, sin_table = dft_tables(WIN)
    block_count = POSITIONS // POS_DEV
    row_blocks = row_offset.reshape(block_count, POS_DEV)
    col_blocks = col_offset.reshape(block_count, POS_DEV)
    amp_blocks = amplitudes.reshape(block_count, POS_DEV, WIN, WIN)
    anchor = jnp.zeros((), jnp.int32)

    def extract(row_start, col_start):
        return lax.dynamic_slice(object_field, (row_start.astype(jnp.int32), anchor, col_start.astype(jnp.int32)), (WIN, 2, WIN))

    def advance(running, block):
        row_list, col_list, amp_list = block
        windows = jax.vmap(extract)(row_list, col_list)
        exit_real, exit_imag = exit_wave(windows, illumination)
        gradients = far_gradient(exit_real, exit_imag, illumination, amp_list, cos_table, sin_table)

        def add_one(position, buffer):
            corner = (row_list[position].astype(jnp.int32), anchor, col_list[position].astype(jnp.int32))
            updated = lax.dynamic_slice(buffer, corner, (WIN, 2, WIN)) + gradients[position]
            return lax.dynamic_update_slice(buffer, updated, corner)
        return (lax.fori_loop(0, POS_DEV, add_one, running), None)
    running, _ = lax.scan(advance, jnp.zeros(object_field.shape, jnp.float32), (row_blocks, col_blocks, amp_blocks))
    return running
```

```python
import functools
import math

import jax
import jax.numpy as jnp
import numpy as np
from jax import lax
from jax.experimental import pallas as pl
from jax.experimental.pallas import tpu as pltpu
from jax.sharding import PartitionSpec as P

LANES = 128
F32 = jnp.float32
BF16 = jnp.bfloat16


def shifted(block, axis, distance):
    devices = range(lax.axis_size(axis))
    route = [(i - distance, i) for i in devices if i - distance in devices]
    return lax.ppermute(block, axis, route)


def exchanged(block, axis, flip):
    return lax.ppermute(block, axis, [(i, i ^ flip) for i in range(lax.axis_size(axis))])


def split_tables(length):
    indices = np.arange(length, dtype=np.int64)
    angles = (indices[:, None] * indices[None, :] % length) * (2.0 * math.pi / length)
    factor = 1.0 / math.sqrt(length)
    whole = np.concatenate([np.cos(angles), np.sin(angles)], axis=0) * factor
    high = whole.astype(BF16)
    low = (whole - high.astype(np.float64)).astype(BF16)
    return jnp.asarray(np.concatenate([high, low], axis=0))


def linear(array):
    rows, parts, columns = array.shape
    tiles = columns // LANES
    return array.reshape(rows, parts, tiles, LANES).transpose(0, 2, 1, 3).reshape(rows * tiles * parts, LANES)


def unlinear(array, rows, columns):
    tiles = columns // LANES
    return array.reshape(rows, tiles, 2, LANES).transpose(0, 2, 1, 3).reshape(rows, 2, columns)


def halves(value):
    high = value.astype(BF16)
    return high, (value - high.astype(F32)).astype(BF16)


def dot3(high_left, low_left, high_right, low_right):
    dot = functools.partial(jnp.dot, preferred_element_type=F32)
    return dot(high_left, high_right) + (dot(low_left, high_right) + dot(high_left, low_right))


def rim_kernel(window, info, obj_ref, out_ref):
    offset = info[0]
    tiles = window // LANES
    shape = (window, 2 * tiles, LANES)
    column = lax.broadcasted_iota(jnp.int32, shape, 1) // 2 * LANES + lax.broadcasted_iota(jnp.int32, shape, 2)
    near = obj_ref[:, : 2 * tiles, :]
    beyond = obj_ref[:, 2 * tiles :, :]
    out_ref[...] = jnp.where(column < offset, beyond, near)


def wave_kernel(slot, window, classes, with_rim, *refs):
    info, obj_hbm, ill_hbm, amp_hbm, table_hbm = refs[:5]
    refs = refs[5:]
    if with_rim:
        rim_hbm, refs = refs[0], refs[1:]
    outs, refs = refs[:classes], refs[classes:]
    obj, ill, amp, table, probe, xh, xl, far, sem = refs[:9]
    rim = refs[9] if with_rim else None
    row, column, index, own = info[3 * slot], info[3 * slot + 1], info[3 * slot + 2], info[6]
    tiles = window // LANES
    ill_rows = window * 2 * tiles
    copies = [
        pltpu.make_async_copy(ill_hbm, ill.at[pl.ds(0, ill_rows)], sem.at[0]),
        pltpu.make_async_copy(ill_hbm, ill.at[pl.ds(ill_rows, ill_rows)], sem.at[1]),
        pltpu.make_async_copy(obj_hbm, obj, sem.at[2]),
        pltpu.make_async_copy(table_hbm, table, sem.at[3]),
        pltpu.make_async_copy(amp_hbm.at[index], amp, sem.at[4]),
    ]
    if with_rim:
        copies.append(pltpu.make_async_copy(rim_hbm, rim, sem.at[5]))
    for copy in copies:
        copy.start()
    for copy in copies:
        copy.wait()

    size = 32
    start = (window - lax.rem(row, window)) * (2 * tiles)

    def store_pair(first, real, imag):
        here = pl.ds(first, size)
        below = pl.ds(window + first, size)
        left, right = pl.ds(0, window), pl.ds(window, window)
        for part, ref in zip(range(2), (xh, xl)):
            r, i, n = (halves(v)[part] for v in (real, imag, -real))
            ref[here, left] = r
            ref[here, right] = i
            ref[below, left] = i
            ref[below, right] = n

    for first in range(0, window, size):
        place = lax.broadcasted_iota(jnp.int32, (size, window), 0) + first
        across = lax.broadcasted_iota(jnp.int32, (size, window), 1)
        pair = []
        for part in range(2):
            rolled = jnp.concatenate(
                [
                    ill[pl.ds(start + first * 2 * tiles + tile * 2 + part, size, stride=2 * tiles), :]
                    for tile in range(tiles)
                ],
                axis=1,
            )
            rolled = pltpu.roll(rolled, column, 1)
            probe[part, pl.ds(first, size), :] = rolled

            def block(base):
                def tile_at(tile):
                    return obj[pl.ds((base + first) * 4 * tiles + tile * 2 + part, size, stride=4 * tiles), :]

                near = jnp.concatenate([tile_at(t) for t in range(tiles)], axis=1)
                beyond = jnp.concatenate([tile_at(t + tiles) for t in range(tiles)], axis=1)
                return jnp.where(across < column, beyond, near)

            seen = jnp.where(place < row, block(window), block(0))
            if with_rim:
                edge = jnp.concatenate(
                    [
                        rim[pl.ds(first * 2 * tiles + tile * 2 + part, size, stride=2 * tiles), :]
                        for tile in range(tiles)
                    ],
                    axis=1,
                )
                seen = jnp.where(place + window < row, edge, seen)
            pair.append((rolled, seen))
        (probe_real, obj_real), (probe_imag, obj_imag) = pair
        store_pair(
            first,
            probe_real * obj_real - probe_imag * obj_imag,
            probe_real * obj_imag + probe_imag * obj_real,
        )

    high = table[pl.ds(0, 2 * window), :]
    low = table[pl.ds(2 * window, 2 * window), :]
    left_high = jnp.concatenate([table[pl.ds(0, window), :], table[pl.ds(window, window), :]], axis=1)
    left_low = jnp.concatenate([table[pl.ds(2 * window, window), :], table[pl.ds(3 * window, window), :]], axis=1)

    def both_sides():
        mid = dot3(xh[...], xl[...], high, low)
        for first in range(0, window, size):
            store_pair(first, mid[first : first + size], mid[window + first : window + first + size])
        far[...] = dot3(left_high, left_low, xh[...], xl[...])

    both_sides()
    for first in range(0, window, size):
        real = far[pl.ds(first, size), pl.ds(0, window)]
        imag = far[pl.ds(first, size), pl.ds(window, window)]
        inverse = jnp.minimum(lax.rsqrt(real * real + imag * imag), 4.0)
        scaled = amp[pl.ds(first, size), :].astype(F32) * inverse
        store_pair(first, real * (1.0 - scaled), imag * (scaled - 1.0))
    both_sides()

    share = window // classes
    for flip in range(classes):
        base = pl.multiple_of((own ^ flip) * share, share)
        here = pl.ds(base, share)
        real = far[here, pl.ds(0, window)]
        imag = far[here, pl.ds(window, window)]
        probe_real = probe[0, here, :]
        probe_imag = probe[1, here, :]
        outs[flip][pl.ds(0, share), :] = probe_real * real - probe_imag * imag
        outs[flip][pl.ds(share, share), :] = -(probe_real * imag + probe_imag * real)
        line = lax.broadcasted_iota(jnp.int32, (8, window), 0)
        outs[flip][pl.ds(2 * share, 8), :] = jnp.where(line == 0, row, column).astype(F32)


def wave(slot, window, classes, info, obj, ill, amp, table, rim=None):
    share = window // classes
    any_spec = pl.BlockSpec(memory_space=pl.ANY)
    ins = [obj, ill, amp, table] + ([rim] if rim is not None else [])
    out = jax.ShapeDtypeStruct((2 * share + 8, window), F32)
    scratch = [
        pltpu.VMEM(obj.shape, F32),
        pltpu.VMEM((2 * ill.shape[0], LANES), F32),
        pltpu.VMEM((window, window), BF16),
        pltpu.VMEM(table.shape, BF16),
        pltpu.VMEM((2, window, window), F32),
        pltpu.VMEM((2 * window, 2 * window), BF16),
        pltpu.VMEM((2 * window, 2 * window), BF16),
        pltpu.VMEM((window, 2 * window), F32),
        pltpu.SemaphoreType.DMA((6,)),
    ] + ([pltpu.VMEM(rim.shape, F32)] if rim is not None else [])
    return pl.pallas_call(
        functools.partial(wave_kernel, slot, window, classes, rim is not None),
        out_shape=[out] * classes,
        in_specs=[pl.BlockSpec(memory_space=pltpu.SMEM)] + [any_spec] * len(ins),
        out_specs=[pl.BlockSpec(memory_space=pltpu.VMEM)] * classes,
        scratch_shapes=scratch,
        cost_estimate=pl.CostEstimate(flops=96 * window**3, transcendentals=window**2, bytes_accessed=5 << 20),
        name="wave" + str(slot),
    )(info, *ins)


def placed(piece_ref, own, share, window):
    row = piece_ref[pl.ds(2 * share, 1), :]
    column = piece_ref[pl.ds(2 * share + 1, 1), :]
    place = (lax.broadcasted_iota(jnp.int32, (share, window), 0) + own * share).astype(F32)
    across = lax.broadcasted_iota(jnp.int32, (share, window), 1).astype(F32)
    upper = across < column
    below = place < row
    lowest = place + float(window) < row
    return upper, below, lowest


def first_sum_kernel(window, classes, info, *refs):
    pieces, acc = refs[:classes], refs[classes]
    share = window // classes
    for part in range(2):
        total = [[jnp.zeros((share, window), F32) for _ in range(2)] for _ in range(2)]
        for piece in pieces:
            upper, below, _ = placed(piece, info[6], share, window)
            value = piece[pl.ds(part * share, share), :]
            for k, wanted in enumerate((~below, below)):
                kept = jnp.where(wanted, value, 0.0)
                total[k][0] += jnp.where(upper, 0.0, kept)
                total[k][1] += jnp.where(upper, kept, 0.0)
        for k in range(2):
            for half in range(2):
                acc[k, part, :, pl.ds(half * window, window)] = total[k][half]


def second_sum_kernel(window, classes, info, acc, *refs):
    pieces, outs = refs[:classes], refs[classes:]
    share = window // classes
    tiles = window // LANES
    for part in range(2):
        total = [[acc[k, part, :, pl.ds(h * window, window)] for h in range(2)] for k in range(2)]
        total.append([jnp.zeros((share, window), F32) for _ in range(2)])
        for piece in pieces:
            upper, below, lowest = placed(piece, info[6], share, window)
            value = piece[pl.ds(part * share, share), :]
            for k, wanted in enumerate((~below, below & ~lowest, lowest)):
                kept = jnp.where(wanted, value, 0.0)
                total[k][0] += jnp.where(upper, 0.0, kept)
                total[k][1] += jnp.where(upper, kept, 0.0)
        for k in range(3):
            for half in range(2):
                for tile in range(tiles):
                    outs[k][pl.ds((half * tiles + tile) * 2 + part, share, stride=4 * tiles), :] = total[k][half][
                        :, tile * LANES : (tile + 1) * LANES
                    ]


def on_device(object_field, illumination, amplitudes, row_offset, col_offset):
    band_rows, _, columns = object_field.shape
    window = illumination.shape[0]
    ways = lax.axis_size("pos")
    assert band_rows == 2 * window and columns == 2 * window and row_offset.shape[0] == 2
    classes = ways // 2
    share = window // classes
    tiles = window // LANES
    pos = lax.axis_index("pos")
    tile = lax.axis_index("tile")
    own, upper = lax.rem(pos, classes), pos // classes
    table = split_tables(window)

    local = row_offset - tile * band_rows
    swap = local[0] > window
    first = swap.astype(jnp.int32)
    rows = jnp.where(swap, local[::-1], local)
    cols = jnp.where(swap, col_offset[::-1], col_offset)
    info = jnp.stack([rows[0], cols[0], first, rows[1], cols[1], 1 - first, own, upper])

    wanted = shifted(cols[1:], "tile", 1)
    obj = linear(object_field)
    ill = linear(illumination)
    obj_rows = obj.reshape(band_rows, 4 * tiles, LANES)
    smem = pl.BlockSpec(memory_space=pltpu.SMEM)
    vmem = pl.BlockSpec(memory_space=pltpu.VMEM)
    rim = pl.pallas_call(
        functools.partial(rim_kernel, window),
        grid_spec=pltpu.PrefetchScalarGridSpec(
            num_scalar_prefetch=1,
            grid=(1,),
            in_specs=[pl.BlockSpec((window, 4 * tiles, LANES), lambda i, s: (0, 0, 0))],
            out_specs=pl.BlockSpec((window, 2 * tiles, LANES), lambda i, s: (0, 0, 0)),
        ),
        out_shape=jax.ShapeDtypeStruct((window, 2 * tiles, LANES), F32),
        name="rim",
    )(wanted, obj_rows)
    rim = shifted(rim, "tile", -1).reshape(window * 2 * tiles, LANES)

    def spread(pieces):
        return [pieces[0]] + [exchanged(pieces[d], "pos", d) for d in range(1, classes)]

    near = spread(wave(0, window, classes, info, obj, ill, amplitudes, table))
    acc = pl.pallas_call(
        functools.partial(first_sum_kernel, window, classes),
        out_shape=jax.ShapeDtypeStruct((2, 2, share, columns), F32),
        in_specs=[smem] + [vmem] * classes,
        out_specs=vmem,
        name="sum0",
    )(info, *near)
    late = spread(wave(1, window, classes, info, obj, ill, amplitudes, table, rim))
    block = jax.ShapeDtypeStruct((share * 4 * tiles, LANES), F32)
    top, middle, spilled = pl.pallas_call(
        functools.partial(second_sum_kernel, window, classes),
        out_shape=[block] * 3,
        in_specs=[smem] + [vmem] * (classes + 1),
        out_specs=[vmem] * 3,
        name="sum1",
    )(info, acc, *late)
    top = top + shifted(spilled, "tile", 1)
    is_upper = upper == 1
    received = exchanged(jnp.where(is_upper, top, middle), "pos", classes)
    result = jnp.where(is_upper, middle, top) + received
    return unlinear(result, share, columns)


def solution(mesh):
    in_specs = (
        P("tile", None, None),
        P(),
        P(("tile", "pos"), None, None),
        P(("tile", "pos")),
        P(("tile", "pos")),
    )
    out_specs = P(("tile", "pos"), None, None)
    return jax.shard_map(
        on_device, mesh=mesh, in_specs=in_specs, out_specs=out_specs, check_vma=False
    )
```

```python
import functools
import math

import jax
import jax.numpy as jnp
import numpy as np
from jax import lax
from jax.experimental import pallas as pl
from jax.experimental.pallas import tpu as pltpu
from jax.sharding import PartitionSpec as P

LANES = 128
F32 = jnp.float32
BF16 = jnp.bfloat16


def shifted(block, axis, distance):
    devices = range(lax.axis_size(axis))
    route = [(i - distance, i) for i in devices if i - distance in devices]
    return lax.ppermute(block, axis, route)


def exchanged(block, axis, flip):
    return lax.ppermute(block, axis, [(i, i ^ flip) for i in range(lax.axis_size(axis))])


def split_tables(length):
    indices = np.arange(length, dtype=np.int64)
    angles = (indices[:, None] * indices[None, :] % length) * (2.0 * math.pi / length)
    factor = 1.0 / math.sqrt(length)
    whole = np.concatenate([np.cos(angles), np.sin(angles)], axis=0) * factor
    high = whole.astype(BF16)
    low = (whole - high.astype(np.float64)).astype(BF16)
    return jnp.asarray(np.concatenate([high, low], axis=0))


def linear(array):
    rows, parts, columns = array.shape
    tiles = columns // LANES
    return array.reshape(rows, parts, tiles, LANES).transpose(0, 2, 1, 3).reshape(rows * tiles * parts, LANES)


def unlinear(array, rows, columns):
    tiles = columns // LANES
    return array.reshape(rows, tiles, 2, LANES).transpose(0, 2, 1, 3).reshape(rows, 2, columns)


def halves(value):
    high = value.astype(BF16)
    return high, (value - high.astype(F32)).astype(BF16)


def dot3(high_left, low_left, high_right, low_right):
    left = jnp.concatenate([low_left, high_left, high_left], axis=1)
    right = jnp.concatenate([high_right, low_right, high_right], axis=0)
    return jnp.dot(left, right, preferred_element_type=F32)


def in_vmem(array):
    return pltpu.with_memory_space_constraint(array, pltpu.VMEM)


def kernel_call(body, name, out_shapes, scalars, arrays, scratch=(), flops=0):
    smem = pl.BlockSpec(memory_space=pltpu.SMEM)
    vmem = pl.BlockSpec(memory_space=pltpu.VMEM)
    moved = sum(4 * math.prod(shape) for shape in out_shapes)
    return pl.pallas_call(
        body,
        out_shape=[pltpu.VMEM(shape, F32) for shape in out_shapes],
        in_specs=[smem] * len(scalars) + [vmem] * len(arrays),
        out_specs=[vmem] * len(out_shapes),
        scratch_shapes=scratch,
        cost_estimate=pl.CostEstimate(flops=flops, transcendentals=0, bytes_accessed=2 * moved),
        compiler_params=pltpu.CompilerParams(vmem_limit_bytes=16 << 20),
        name=name,
    )(*scalars, *[in_vmem(array) for array in arrays])


def chosen(slot, rows, cols, band_start, window):
    crossing = (rows[0] - band_start > window).astype(jnp.int32)
    index = crossing if slot == 0 else 1 - crossing
    return rows[index] - band_start, cols[index], index


def rim_kernel(window, rows, cols, obj, out):
    band_start = (lax.axis_index("tile") - 1) * (2 * window)
    _, offset, _ = chosen(1, rows, cols, band_start, window)
    tiles = window // LANES
    for tile in range(tiles):
        column = lax.broadcasted_iota(jnp.int32, (window, LANES), 1) + tile * LANES
        for part in range(2):
            near = obj[pl.ds(tile * 2 + part, window, stride=4 * tiles), :]
            beyond = obj[pl.ds((tiles + tile) * 2 + part, window, stride=4 * tiles), :]
            out[part, :, pl.ds(tile * LANES, LANES)] = jnp.where(column < offset, beyond, near)


def wave_kernel(slot, window, classes, with_rim, rows, cols, obj, ill, amps, table, *refs):
    if with_rim:
        rim, refs = refs[0], refs[1:]
    outs, refs = refs[:classes], refs[classes:]
    doubled, probe, xh, xl, far = refs
    tiles = window // LANES
    row, column, index = chosen(slot, rows, cols, lax.axis_index("tile") * (2 * window), window)
    own = lax.rem(lax.axis_index("pos"), classes)
    size = 32
    step = 2 * tiles
    whole = window * step
    doubled[pl.ds(0, whole), :] = ill[...]
    doubled[pl.ds(whole, size * step), :] = ill[pl.ds(0, size * step), :]
    turn = lax.rem(row, window)

    def store_pair(first, real, imag):
        here = pl.ds(first, size)
        below = pl.ds(window + first, size)
        left, right = pl.ds(0, window), pl.ds(window, window)
        for part, ref in zip(range(2), (xh, xl)):
            r, i, n = (halves(v)[part] for v in (real, imag, -real))
            ref[here, left] = r
            ref[here, right] = i
            ref[below, left] = i
            ref[below, right] = n

    for first in range(0, window, size):
        place = lax.broadcasted_iota(jnp.int32, (size, window), 0) + first
        across = lax.broadcasted_iota(jnp.int32, (size, window), 1)
        start = lax.rem(first + window - turn, window) * step
        pair = []
        for part in range(2):
            rolled = jnp.concatenate(
                [doubled[pl.ds(start + tile * 2 + part, size, stride=step), :] for tile in range(tiles)],
                axis=1,
            )
            rolled = pltpu.roll(rolled, column, 1)
            probe[part, pl.ds(first, size), :] = rolled

            def block(base):
                def tile_at(tile):
                    return obj[pl.ds((base + first) * 2 * step + tile * 2 + part, size, stride=2 * step), :]

                near = jnp.concatenate([tile_at(t) for t in range(tiles)], axis=1)
                beyond = jnp.concatenate([tile_at(t + tiles) for t in range(tiles)], axis=1)
                return jnp.where(across < column, beyond, near)

            seen = jnp.where(place < row, block(window), block(0))
            if with_rim:
                seen = jnp.where(place + window < row, rim[part, pl.ds(first, size), :], seen)
            pair.append((rolled, seen))
        (probe_real, obj_real), (probe_imag, obj_imag) = pair
        store_pair(
            first,
            probe_real * obj_real - probe_imag * obj_imag,
            probe_real * obj_imag + probe_imag * obj_real,
        )

    high = table[pl.ds(0, 2 * window), :]
    low = table[pl.ds(2 * window, 2 * window), :]
    left_high = jnp.concatenate([table[pl.ds(0, window), :], table[pl.ds(window, window), :]], axis=1)
    left_low = jnp.concatenate([table[pl.ds(2 * window, window), :], table[pl.ds(3 * window, window), :]], axis=1)

    def both_sides():
        mid = dot3(xh[...], xl[...], high, low)
        for first in range(0, window, size):
            store_pair(first, mid[first : first + size], mid[window + first : window + first + size])
        far[...] = dot3(left_high, left_low, xh[...], xl[...])

    both_sides()
    for first in range(0, window, size):
        real = far[pl.ds(first, size), pl.ds(0, window)]
        imag = far[pl.ds(first, size), pl.ds(window, window)]
        inverse = jnp.minimum(lax.rsqrt(real * real + imag * imag), 4.0)
        scaled = amps[index, pl.ds(first, size), :].astype(F32) * inverse
        store_pair(first, real * (1.0 - scaled), imag * (scaled - 1.0))
    both_sides()

    share = window // classes
    for flip in range(classes):
        base = pl.multiple_of((own ^ flip) * share, share)
        here = pl.ds(base, share)
        real = far[here, pl.ds(0, window)]
        imag = far[here, pl.ds(window, window)]
        probe_real = probe[0, here, :]
        probe_imag = probe[1, here, :]
        outs[flip][pl.ds(0, share), :] = probe_real * real - probe_imag * imag
        outs[flip][pl.ds(share, share), :] = -(probe_real * imag + probe_imag * real)
        line = lax.broadcasted_iota(jnp.int32, (8, window), 0)
        outs[flip][pl.ds(2 * share, 8), :] = jnp.where(line == 0, row, column).astype(F32)


def wave(slot, window, classes, scalars, arrays):
    share = window // classes
    tiles = window // LANES
    scratch = [
        pltpu.VMEM(((window + 32) * 2 * tiles + 8, LANES), F32),
        pltpu.VMEM((2, window, window), F32),
        pltpu.VMEM((2 * window, 2 * window), BF16),
        pltpu.VMEM((2 * window, 2 * window), BF16),
        pltpu.VMEM((window, 2 * window), F32),
    ]
    return kernel_call(
        functools.partial(wave_kernel, slot, window, classes, len(arrays) == 5),
        "wave" + str(slot),
        [(2 * share + 8, window)] * classes,
        scalars,
        arrays,
        scratch,
        96 * window**3,
    )


def placed(piece, own, share, window):
    row = piece[pl.ds(2 * share, 1), :]
    column = piece[pl.ds(2 * share + 1, 1), :]
    place = (lax.broadcasted_iota(jnp.int32, (share, window), 0) + own * share).astype(F32)
    across = lax.broadcasted_iota(jnp.int32, (share, window), 1).astype(F32)
    return across < column, place < row, place + float(window) < row


def first_sum_kernel(window, classes, *refs):
    pieces, acc = refs[:classes], refs[classes]
    share = window // classes
    own = lax.rem(lax.axis_index("pos"), classes)
    for part in range(2):
        total = [[jnp.zeros((share, window), F32) for _ in range(2)] for _ in range(2)]
        for piece in pieces:
            upper, below, _ = placed(piece, own, share, window)
            value = piece[pl.ds(part * share, share), :]
            for k, wanted in enumerate((~below, below)):
                kept = jnp.where(wanted, value, 0.0)
                total[k][0] += jnp.where(upper, 0.0, kept)
                total[k][1] += jnp.where(upper, kept, 0.0)
        for k in range(2):
            for half in range(2):
                acc[k, part, :, pl.ds(half * window, window)] = total[k][half]


def second_sum_kernel(window, classes, acc, *refs):
    pieces, outs = refs[:classes], refs[classes:]
    share = window // classes
    tiles = window // LANES
    own = lax.rem(lax.axis_index("pos"), classes)
    for part in range(2):
        total = [[acc[k, part, :, pl.ds(h * window, window)] for h in range(2)] for k in range(2)]
        total.append([jnp.zeros((share, window), F32) for _ in range(2)])
        for piece in pieces:
            upper, below, lowest = placed(piece, own, share, window)
            value = piece[pl.ds(part * share, share), :]
            for k, wanted in enumerate((~below, below & ~lowest, lowest)):
                kept = jnp.where(wanted, value, 0.0)
                total[k][0] += jnp.where(upper, 0.0, kept)
                total[k][1] += jnp.where(upper, kept, 0.0)
        for k in range(3):
            for half in range(2):
                for tile in range(tiles):
                    outs[k][pl.ds((half * tiles + tile) * 2 + part, share, stride=4 * tiles), :] = total[k][half][
                        :, tile * LANES : (tile + 1) * LANES
                    ]


def on_device(object_field, illumination, amplitudes, row_offset, col_offset):
    band_rows, _, columns = object_field.shape
    window = illumination.shape[0]
    ways = lax.axis_size("pos")
    assert band_rows == 2 * window and columns == 2 * window and row_offset.shape[0] == 2
    classes = ways // 2
    share = window // classes
    tiles = window // LANES
    table = split_tables(window)
    obj = linear(object_field)
    ill = linear(illumination)
    scalars = (row_offset, col_offset)

    wanted = [shifted(scalar, "tile", 1) for scalar in scalars]
    (rim,) = kernel_call(functools.partial(rim_kernel, window), "rim", [(2, window, window)], wanted, [obj])
    rim = shifted(rim, "tile", -1)

    def spread(pieces):
        return [pieces[0]] + [exchanged(pieces[d], "pos", d) for d in range(1, classes)]

    near = spread(wave(0, window, classes, scalars, [obj, ill, amplitudes, table]))
    (acc,) = kernel_call(
        functools.partial(first_sum_kernel, window, classes), "sum0", [(2, 2, share, columns)], (), near
    )
    late = spread(wave(1, window, classes, scalars, [obj, ill, amplitudes, table, rim]))
    top, middle, spilled = kernel_call(
        functools.partial(second_sum_kernel, window, classes),
        "sum1",
        [(share * 4 * tiles, LANES)] * 3,
        (),
        [acc, *late],
    )
    top = top + shifted(spilled, "tile", 1)
    is_upper = lax.axis_index("pos") >= classes
    received = exchanged(jnp.where(is_upper, top, middle), "pos", classes)
    result = jnp.where(is_upper, middle, top) + received
    return unlinear(result, share, columns)


def solution(mesh):
    in_specs = (
        P("tile", None, None),
        P(),
        P(("tile", "pos"), None, None),
        P(("tile", "pos")),
        P(("tile", "pos")),
    )
    out_specs = P(("tile", "pos"), None, None)
    return jax.shard_map(
        on_device, mesh=mesh, in_specs=in_specs, out_specs=out_specs, check_vma=False
    )
```

```python
import functools
import math

import jax
import jax.numpy as jnp
import numpy as np
from jax import lax
from jax.experimental import pallas as pl
from jax.experimental.pallas import tpu as pltpu
from jax.sharding import PartitionSpec as P

LANES = 128
F32 = jnp.float32
BF16 = jnp.bfloat16


def shifted(block, axis, distance):
    devices = range(lax.axis_size(axis))
    route = [(i - distance, i) for i in devices if i - distance in devices]
    return lax.ppermute(block, axis, route)


def exchanged(block, axis, flip):
    return lax.ppermute(block, axis, [(i, i ^ flip) for i in range(lax.axis_size(axis))])


def split_tables(length):
    indices = np.arange(length, dtype=np.int64)
    angles = (indices[:, None] * indices[None, :] % length) * (2.0 * math.pi / length)
    factor = 1.0 / math.sqrt(length)
    whole = np.concatenate([np.cos(angles), np.sin(angles)], axis=0) * factor
    high = whole.astype(BF16)
    low = (whole - high.astype(np.float64)).astype(BF16)
    return jnp.asarray(np.concatenate([high, low], axis=0))


def linear(array):
    rows, parts, columns = array.shape
    tiles = columns // LANES
    return array.reshape(rows, parts, tiles, LANES).transpose(0, 2, 1, 3).reshape(rows * tiles * parts, LANES)


def unlinear(array, rows, columns):
    tiles = columns // LANES
    return array.reshape(rows, tiles, 2, LANES).transpose(0, 2, 1, 3).reshape(rows, 2, columns)


def halves(value):
    high = value.astype(BF16)
    return high, (value - high.astype(F32)).astype(BF16)


def dot3(high_left, low_left, high_right, low_right):
    left = jnp.concatenate([low_left, high_left, high_left], axis=1)
    right = jnp.concatenate([high_right, low_right, high_right], axis=0)
    return jnp.dot(left, right, preferred_element_type=F32)


def in_vmem(array):
    return pltpu.with_memory_space_constraint(array, pltpu.VMEM)


def kernel_call(body, name, out_shapes, scalars, arrays, scratch=(), flops=0):
    smem = pl.BlockSpec(memory_space=pltpu.SMEM)
    vmem = pl.BlockSpec(memory_space=pltpu.VMEM)
    moved = sum(4 * math.prod(shape) for shape in out_shapes)
    return pl.pallas_call(
        body,
        out_shape=[pltpu.VMEM(shape, F32) for shape in out_shapes],
        in_specs=[smem] * len(scalars) + [vmem] * len(arrays),
        out_specs=[vmem] * len(out_shapes),
        scratch_shapes=scratch,
        cost_estimate=pl.CostEstimate(flops=flops, transcendentals=0, bytes_accessed=2 * moved),
        compiler_params=pltpu.CompilerParams(vmem_limit_bytes=16 << 20),
        name=name,
    )(*scalars, *[in_vmem(array) for array in arrays])


def chosen(slot, rows, cols, band_start, window):
    crossing = (rows[0] - band_start > window).astype(jnp.int32)
    index = crossing if slot == 0 else 1 - crossing
    return rows[index] - band_start, cols[index], index


def load_kernel(number, *refs):
    sources, targets, sem = refs[:number], refs[number : 2 * number], refs[2 * number]
    copies = [pltpu.make_async_copy(a, b, sem.at[i]) for i, (a, b) in enumerate(zip(sources, targets))]
    for copy in copies:
        copy.start()
    for copy in copies:
        copy.wait()


def loaded(arrays):
    return pl.pallas_call(
        functools.partial(load_kernel, len(arrays)),
        out_shape=[pltpu.VMEM(array.shape, array.dtype) for array in arrays],
        in_specs=[pl.BlockSpec(memory_space=pl.ANY)] * len(arrays),
        out_specs=[pl.BlockSpec(memory_space=pltpu.VMEM)] * len(arrays),
        scratch_shapes=[pltpu.SemaphoreType.DMA((len(arrays),))],
        compiler_params=pltpu.CompilerParams(vmem_limit_bytes=16 << 20),
        name="load",
    )(*[pltpu.with_memory_space_constraint(array, pltpu.HBM) for array in arrays])


def rim_kernel(window, wanted, obj, out):
    offset = wanted[0]
    tiles = window // LANES
    for tile in range(tiles):
        column = lax.broadcasted_iota(jnp.int32, (window, LANES), 1) + tile * LANES
        for part in range(2):
            near = obj[pl.ds(tile * 2 + part, window, stride=4 * tiles), :]
            beyond = obj[pl.ds((tiles + tile) * 2 + part, window, stride=4 * tiles), :]
            out[part, :, pl.ds(tile * LANES, LANES)] = jnp.where(column < offset, beyond, near)


def wave_kernel(slot, window, classes, with_rim, rows, cols, obj, ill, amps, table, *refs):
    if with_rim:
        rim, refs = refs[0], refs[1:]
    outs, refs = refs[:classes], refs[classes:]
    doubled, probe, xh, xl, far = refs
    tiles = window // LANES
    row, column, index = chosen(slot, rows, cols, lax.axis_index("tile") * (2 * window), window)
    own = lax.rem(lax.axis_index("pos"), classes)
    size = 32
    step = 2 * tiles
    whole = window * step
    doubled[pl.ds(0, whole), :] = ill[...]
    doubled[pl.ds(whole, size * step), :] = ill[pl.ds(0, size * step), :]
    turn = lax.rem(row, window)

    def store_pair(first, real, imag):
        here = pl.ds(first, size)
        below = pl.ds(window + first, size)
        left, right = pl.ds(0, window), pl.ds(window, window)
        for part, ref in zip(range(2), (xh, xl)):
            r, i, n = (halves(v)[part] for v in (real, imag, -real))
            ref[here, left] = r
            ref[here, right] = i
            ref[below, left] = i
            ref[below, right] = n

    for first in range(0, window, size):
        place = lax.broadcasted_iota(jnp.int32, (size, window), 0) + first
        across = lax.broadcasted_iota(jnp.int32, (size, window), 1)
        start = lax.rem(first + window - turn, window) * step
        pair = []
        for part in range(2):
            rolled = jnp.concatenate(
                [doubled[pl.ds(start + tile * 2 + part, size, stride=step), :] for tile in range(tiles)],
                axis=1,
            )
            rolled = pltpu.roll(rolled, column, 1)
            probe[part, pl.ds(first, size), :] = rolled

            def block(base):
                def tile_at(tile):
                    return obj[pl.ds((base + first) * 2 * step + tile * 2 + part, size, stride=2 * step), :]

                near = jnp.concatenate([tile_at(t) for t in range(tiles)], axis=1)
                beyond = jnp.concatenate([tile_at(t + tiles) for t in range(tiles)], axis=1)
                return jnp.where(across < column, beyond, near)

            seen = jnp.where(place < row, block(window), block(0))
            if with_rim:
                seen = jnp.where(place + window < row, rim[part, pl.ds(first, size), :], seen)
            pair.append((rolled, seen))
        (probe_real, obj_real), (probe_imag, obj_imag) = pair
        store_pair(
            first,
            probe_real * obj_real - probe_imag * obj_imag,
            probe_real * obj_imag + probe_imag * obj_real,
        )

    high = table[pl.ds(0, 2 * window), :]
    low = table[pl.ds(2 * window, 2 * window), :]
    left_high = jnp.concatenate([table[pl.ds(0, window), :], table[pl.ds(window, window), :]], axis=1)
    left_low = jnp.concatenate([table[pl.ds(2 * window, window), :], table[pl.ds(3 * window, window), :]], axis=1)

    def both_sides():
        mid = dot3(xh[...], xl[...], high, low)
        for first in range(0, window, size):
            store_pair(first, mid[first : first + size], mid[window + first : window + first + size])
        far[...] = dot3(left_high, left_low, xh[...], xl[...])

    both_sides()
    for first in range(0, window, size):
        real = far[pl.ds(first, size), pl.ds(0, window)]
        imag = far[pl.ds(first, size), pl.ds(window, window)]
        inverse = jnp.minimum(lax.rsqrt(real * real + imag * imag), 4.0)
        scaled = amps[index, pl.ds(first, size), :].astype(F32) * inverse
        store_pair(first, real * (1.0 - scaled), imag * (scaled - 1.0))
    both_sides()

    share = window // classes
    for flip in range(classes):
        base = pl.multiple_of((own ^ flip) * share, share)
        here = pl.ds(base, share)
        real = far[here, pl.ds(0, window)]
        imag = far[here, pl.ds(window, window)]
        probe_real = probe[0, here, :]
        probe_imag = probe[1, here, :]
        outs[flip][pl.ds(0, share), :] = probe_real * real - probe_imag * imag
        outs[flip][pl.ds(share, share), :] = -(probe_real * imag + probe_imag * real)
        line = lax.broadcasted_iota(jnp.int32, (8, window), 0)
        outs[flip][pl.ds(2 * share, 8), :] = jnp.where(line == 0, row, column).astype(F32)


def wave(slot, window, classes, scalars, arrays):
    share = window // classes
    tiles = window // LANES
    scratch = [
        pltpu.VMEM(((window + 32) * 2 * tiles + 8, LANES), F32),
        pltpu.VMEM((2, window, window), F32),
        pltpu.VMEM((2 * window, 2 * window), BF16),
        pltpu.VMEM((2 * window, 2 * window), BF16),
        pltpu.VMEM((window, 2 * window), F32),
    ]
    return kernel_call(
        functools.partial(wave_kernel, slot, window, classes, len(arrays) == 5),
        "wave" + str(slot),
        [(2 * share + 8, window)] * classes,
        scalars,
        arrays,
        scratch,
        96 * window**3,
    )


def placed(piece, own, share, window):
    row = piece[pl.ds(2 * share, 1), :]
    column = piece[pl.ds(2 * share + 1, 1), :]
    place = (lax.broadcasted_iota(jnp.int32, (share, window), 0) + own * share).astype(F32)
    across = lax.broadcasted_iota(jnp.int32, (share, window), 1).astype(F32)
    return across < column, place < row, place + float(window) < row


def first_sum_kernel(window, classes, *refs):
    pieces, acc = refs[:classes], refs[classes]
    share = window // classes
    own = lax.rem(lax.axis_index("pos"), classes)
    for part in range(2):
        total = [[jnp.zeros((share, window), F32) for _ in range(2)] for _ in range(2)]
        for piece in pieces:
            upper, below, _ = placed(piece, own, share, window)
            value = piece[pl.ds(part * share, share), :]
            for k, wanted in enumerate((~below, below)):
                kept = jnp.where(wanted, value, 0.0)
                total[k][0] += jnp.where(upper, 0.0, kept)
                total[k][1] += jnp.where(upper, kept, 0.0)
        for k in range(2):
            for half in range(2):
                acc[k, part, :, pl.ds(half * window, window)] = total[k][half]


def second_sum_kernel(window, classes, acc, *refs):
    pieces, outs = refs[:classes], refs[classes:]
    share = window // classes
    tiles = window // LANES
    own = lax.rem(lax.axis_index("pos"), classes)
    for part in range(2):
        total = [[acc[k, part, :, pl.ds(h * window, window)] for h in range(2)] for k in range(2)]
        total.append([jnp.zeros((share, window), F32) for _ in range(2)])
        for piece in pieces:
            upper, below, lowest = placed(piece, own, share, window)
            value = piece[pl.ds(part * share, share), :]
            for k, wanted in enumerate((~below, below & ~lowest, lowest)):
                kept = jnp.where(wanted, value, 0.0)
                total[k][0] += jnp.where(upper, 0.0, kept)
                total[k][1] += jnp.where(upper, kept, 0.0)
        for k in range(3):
            for half in range(2):
                for tile in range(tiles):
                    outs[k][pl.ds((half * tiles + tile) * 2 + part, share, stride=4 * tiles), :] = total[k][half][
                        :, tile * LANES : (tile + 1) * LANES
                    ]


def on_device(object_field, illumination, amplitudes, row_offset, col_offset):
    band_rows, _, columns = object_field.shape
    window = illumination.shape[0]
    ways = lax.axis_size("pos")
    assert band_rows == 2 * window and columns == 2 * window and row_offset.shape[0] == 2
    classes = ways // 2
    share = window // classes
    tiles = window // LANES
    scalars = (row_offset, col_offset)

    crossing = row_offset[:1] - lax.axis_index("tile") * band_rows > window
    wanted = shifted(jnp.where(crossing, col_offset[:1], col_offset[1:]), "tile", 1)
    obj, ill, amps, table = loaded([linear(object_field), linear(illumination), amplitudes, split_tables(window)])
    (rim,) = kernel_call(functools.partial(rim_kernel, window), "rim", [(2, window, window)], [wanted], [obj])
    rim = shifted(rim, "tile", -1)

    def spread(pieces):
        moved = {d: exchanged(pieces[d], "pos", d) for d in reversed(range(1, classes))}
        return [pieces[0]] + [moved[d] for d in range(1, classes)]

    near = spread(wave(0, window, classes, scalars, [obj, ill, amps, table]))
    (acc,) = kernel_call(
        functools.partial(first_sum_kernel, window, classes), "sum0", [(2, 2, share, columns)], (), near
    )
    late = spread(wave(1, window, classes, scalars, [obj, ill, amps, table, rim]))
    top, middle, spilled = kernel_call(
        functools.partial(second_sum_kernel, window, classes),
        "sum1",
        [(share * 4 * tiles, LANES)] * 3,
        (),
        [acc, *late],
    )
    top = top + shifted(spilled, "tile", 1)
    is_upper = lax.axis_index("pos") >= classes
    received = exchanged(jnp.where(is_upper, top, middle), "pos", classes)
    result = jnp.where(is_upper, middle, top) + received
    return unlinear(result, share, columns)


def solution(mesh):
    in_specs = (
        P("tile", None, None),
        P(),
        P(("tile", "pos"), None, None),
        P(("tile", "pos")),
        P(("tile", "pos")),
    )
    out_specs = P(("tile", "pos"), None, None)
    return jax.shard_map(
        on_device, mesh=mesh, in_specs=in_specs, out_specs=out_specs, check_vma=False
    )
```

```python
import functools
import math

import jax
import jax.numpy as jnp
import numpy as np
from jax import lax
from jax.experimental import pallas as pl
from jax.experimental.pallas import tpu as pltpu
from jax.sharding import PartitionSpec as P


LANES = 128
F32 = jnp.float32
BF16 = jnp.bfloat16


def shifted(block, axis, distance):
    devices = range(lax.axis_size(axis))
    route = [(i - distance, i) for i in devices if i - distance in devices]
    return lax.ppermute(block, axis, route)


def exchanged(block, axis, flip):
    return lax.ppermute(block, axis, [(i, i ^ flip) for i in range(lax.axis_size(axis))])


def split_tables(length):
    indices = np.arange(length, dtype=np.int64)
    angles = (indices[:, None] * indices[None, :] % length) * (2.0 * math.pi / length)
    factor = 1.0 / math.sqrt(length)
    whole = np.concatenate([np.cos(angles), np.sin(angles)], axis=0) * factor
    high = whole.astype(BF16)
    low = (whole - high.astype(np.float64)).astype(BF16)
    return jnp.asarray(np.concatenate([high, low], axis=0))


def linear(array):
    rows, parts, columns = array.shape
    tiles = columns // LANES
    return array.reshape(rows, parts, tiles, LANES).transpose(0, 2, 1, 3).reshape(rows * tiles * parts, LANES)


def unlinear(array, rows, columns):
    tiles = columns // LANES
    return array.reshape(rows, tiles, 2, LANES).transpose(0, 2, 1, 3).reshape(rows, 2, columns)


def halves(value):
    high = value.astype(BF16)
    return high, (value - high.astype(F32)).astype(BF16)


def dot3(high_left, low_left, high_right, low_right):
    left = jnp.concatenate([low_left, high_left, high_left], axis=1)
    right = jnp.concatenate([high_right, low_right, high_right], axis=0)
    return jnp.dot(left, right, preferred_element_type=F32)


def in_vmem(array):
    return pltpu.with_memory_space_constraint(array, pltpu.VMEM)


def kernel_call(body, out_shapes, scalars, arrays, scratch=(), flops=0):
    smem = pl.BlockSpec(memory_space=pltpu.SMEM)
    vmem = pl.BlockSpec(memory_space=pltpu.VMEM)
    out_shapes = [shape if isinstance(shape, pl.MemoryRef) else pltpu.VMEM(shape, F32) for shape in out_shapes]
    moved = sum(4 * math.prod(shape.shape) for shape in out_shapes)
    return pl.pallas_call(
        body,
        out_shape=out_shapes,
        in_specs=[smem] * len(scalars) + [vmem] * len(arrays),
        out_specs=[vmem] * len(out_shapes),
        scratch_shapes=scratch,
        cost_estimate=pl.CostEstimate(flops=flops, transcendentals=0, bytes_accessed=2 * moved),
        compiler_params=pltpu.CompilerParams(vmem_limit_bytes=16 << 20),
    )(*scalars, *[in_vmem(array) for array in arrays])


def chosen(slot, rows, cols, band_start, window):
    crossing = (rows[0] - band_start > window).astype(jnp.int32)
    index = crossing if slot == 0 else 1 - crossing
    return rows[index] - band_start, cols[index], index


def load_kernel(number, *refs):
    sources, targets, sem = refs[:number], refs[number : 2 * number], refs[2 * number]
    copies = [pltpu.make_async_copy(a, b, sem.at[i]) for i, (a, b) in enumerate(zip(sources, targets))]
    for copy in copies:
        copy.start()
    for copy in copies:
        copy.wait()


def loaded(arrays):
    return pl.pallas_call(
        functools.partial(load_kernel, len(arrays)),
        out_shape=[pltpu.VMEM(array.shape, array.dtype) for array in arrays],
        in_specs=[pl.BlockSpec(memory_space=pl.ANY)] * len(arrays),
        out_specs=[pl.BlockSpec(memory_space=pltpu.VMEM)] * len(arrays),
        scratch_shapes=[pltpu.SemaphoreType.DMA((len(arrays),))],
        compiler_params=pltpu.CompilerParams(vmem_limit_bytes=16 << 20),
        name="load",
    )(*[pltpu.with_memory_space_constraint(array, pltpu.HBM) for array in arrays])


def pick_kernel(window, rows, cols, out):
    _, column, _ = chosen(1, rows, cols, lax.axis_index("tile") * (2 * window), window)
    out[...] = jnp.broadcast_to(column.astype(F32), out.shape)


def rim_kernel(window, wanted, obj, out):
    offset = wanted[pl.ds(0, 1), :]
    tiles = window // LANES
    for tile in range(tiles):
        column = (lax.broadcasted_iota(jnp.int32, (window, LANES), 1) + tile * LANES).astype(F32)
        for part in range(2):
            near = obj[pl.ds(tile * 2 + part, window, stride=4 * tiles), :]
            beyond = obj[pl.ds((tiles + tile) * 2 + part, window, stride=4 * tiles), :]
            out[part, :, pl.ds(tile * LANES, LANES)] = jnp.where(column < offset, beyond, near)


def wave_kernel(slot, window, classes, with_rim, rows, cols, obj, ill, amps, table, *refs):
    if with_rim:
        rim, refs = refs[0], refs[1:]
    outs, refs = refs[:classes], refs[classes:]
    if slot == 0:
        doubled, far, probe, xh, xl = refs
    else:
        probe, xh, xl, doubled, far = refs
    tiles = window // LANES
    row, column, index = chosen(slot, rows, cols, lax.axis_index("tile") * (2 * window), window)
    own = lax.rem(lax.axis_index("pos"), classes)
    size = 32
    step = 2 * tiles
    whole = window * step
    doubled[pl.ds(0, whole), :] = ill[...]
    doubled[pl.ds(whole, size * step), :] = ill[pl.ds(0, size * step), :]
    turn = lax.rem(row, window)

    def store_pair(first, real, imag):
        here = pl.ds(first, size)
        below = pl.ds(window + first, size)
        left, right = pl.ds(0, window), pl.ds(window, window)
        for part, ref in zip(range(2), (xh, xl)):
            r, i, n = (halves(v)[part] for v in (real, imag, -real))
            ref[here, left] = r
            ref[here, right] = i
            ref[below, left] = i
            ref[below, right] = n

    for first in range(0, window, size):
        place = lax.broadcasted_iota(jnp.int32, (size, window), 0) + first
        across = lax.broadcasted_iota(jnp.int32, (size, window), 1)
        start = lax.rem(first + window - turn, window) * step
        pair = []
        for part in range(2):
            rolled = jnp.concatenate(
                [doubled[pl.ds(start + tile * 2 + part, size, stride=step), :] for tile in range(tiles)],
                axis=1,
            )
            rolled = pltpu.roll(rolled, column, 1)
            probe[part, pl.ds(first, size), :] = rolled

            def block(base):
                def tile_at(tile):
                    return obj[pl.ds((base + first) * 2 * step + tile * 2 + part, size, stride=2 * step), :]

                near = jnp.concatenate([tile_at(t) for t in range(tiles)], axis=1)
                beyond = jnp.concatenate([tile_at(t + tiles) for t in range(tiles)], axis=1)
                return jnp.where(across < column, beyond, near)

            seen = jnp.where(place < row, block(window), block(0))
            if with_rim:
                seen = jnp.where(place + window < row, rim[part, pl.ds(first, size), :], seen)
            pair.append((rolled, seen))
        (probe_real, obj_real), (probe_imag, obj_imag) = pair
        store_pair(
            first,
            probe_real * obj_real - probe_imag * obj_imag,
            probe_real * obj_imag + probe_imag * obj_real,
        )

    high = table[pl.ds(0, 2 * window), :]
    low = table[pl.ds(2 * window, 2 * window), :]
    left_high = jnp.concatenate([table[pl.ds(0, window), :], table[pl.ds(window, window), :]], axis=1)
    left_low = jnp.concatenate([table[pl.ds(2 * window, window), :], table[pl.ds(3 * window, window), :]], axis=1)

    def right_side():
        mid = dot3(xh[...], xl[...], high, low)
        for first in range(0, window, size):
            store_pair(first, mid[first : first + size], mid[window + first : window + first + size])

    right_side()
    far[...] = dot3(left_high, left_low, xh[...], xl[...])
    for first in range(0, window, size):
        real = far[pl.ds(first, size), pl.ds(0, window)]
        imag = far[pl.ds(first, size), pl.ds(window, window)]
        inverse = jnp.minimum(lax.rsqrt(real * real + imag * imag), 4.0)
        scaled = amps[index, pl.ds(first, size), :].astype(F32) * inverse
        store_pair(first, real * (1.0 - scaled), imag * (scaled - 1.0))
    right_side()
    if slot == 0:
        finish(0, window, classes, row, column, table, probe, xh, xl, far, outs)
    else:
        finish(0, LANES, classes, row, column, table, probe, xh, xl, far, outs)


def finish(start, width, classes, row, column, table, probe, xh, xl, far, outs):
    window = probe.shape[1]
    share = window // classes
    own = lax.rem(lax.axis_index("pos"), classes)
    left_high = jnp.concatenate([table[pl.ds(0, window), :], table[pl.ds(window, window), :]], axis=1)
    left_low = jnp.concatenate([table[pl.ds(2 * window, window), :], table[pl.ds(3 * window, window), :]], axis=1)
    across = pl.ds(start, width)

    def columns_of(ref):
        return jnp.concatenate([ref[:, across], ref[:, pl.ds(window + start, width)]], axis=1)

    far[:, pl.ds(0, 2 * width)] = dot3(left_high, left_low, columns_of(xh), columns_of(xl))
    for flip in range(classes):
        base = pl.multiple_of((own ^ flip) * share, share)
        here = pl.ds(base, share)
        real = far[here, pl.ds(0, width)]
        imag = far[here, pl.ds(width, width)]
        probe_real = probe[0, here, across]
        probe_imag = probe[1, here, across]
        outs[flip][pl.ds(0, share), :] = probe_real * real - probe_imag * imag
        outs[flip][pl.ds(share, share), :] = -(probe_real * imag + probe_imag * real)
        line = lax.broadcasted_iota(jnp.int32, (8, width), 0)
        outs[flip][pl.ds(2 * share, 8), :] = jnp.where(line == 0, row, column).astype(F32)


def rest_kernel(start, window, classes, rows, cols, table, probe, xh, xl, *refs):
    outs, far = refs[:classes], refs[classes]
    row, column, _ = chosen(1, rows, cols, lax.axis_index("tile") * (2 * window), window)
    finish(start, LANES, classes, row, column, table, probe, xh, xl, far, outs)


def wave(slot, window, classes, scalars, arrays):
    share = window // classes
    tiles = window // LANES
    width = window if slot == 0 else LANES
    pieces = [pltpu.VMEM((2 * share + 8, width), F32)] * classes
    state = [
        pltpu.VMEM((2, window, window), F32),
        pltpu.VMEM((2 * window, 2 * window), BF16),
        pltpu.VMEM((2 * window, 2 * window), BF16),
    ]
    scratch = [
        pltpu.VMEM(((window + 32) * 2 * tiles + 8, LANES), F32),
        pltpu.VMEM((window, 2 * window), F32),
    ]
    return kernel_call(
        functools.partial(wave_kernel, slot, window, classes, slot == 1),
        pieces + (state if slot == 1 else []),
        scalars,
        arrays,
        scratch + (state if slot == 0 else []),
        96 * window**3,
    )


def rest(tile, window, classes, scalars, arrays):
    share = window // classes
    return kernel_call(
        functools.partial(rest_kernel, tile * LANES, window, classes),
        [pltpu.VMEM((2 * share + 8, LANES), F32)] * classes,
        scalars,
        arrays,
        [pltpu.VMEM((window, 2 * LANES), F32)],
        12 * window**3,
    )


def placed(piece, start, width, own, share, window):
    row = piece[pl.ds(2 * share, 1), :]
    column = piece[pl.ds(2 * share + 1, 1), :]
    place = (lax.broadcasted_iota(jnp.int32, (share, width), 0) + own * share).astype(F32)
    across = (lax.broadcasted_iota(jnp.int32, (share, width), 1) + start).astype(F32)
    return across < column, place < row, place + float(window) < row


def first_sum_kernel(window, classes, *refs):
    pieces, acc = refs[:classes], refs[classes]
    share = window // classes
    own = lax.rem(lax.axis_index("pos"), classes)
    for part in range(2):
        total = [[jnp.zeros((share, window), F32) for _ in range(2)] for _ in range(2)]
        for piece in pieces:
            upper, below, _ = placed(piece, 0, window, own, share, window)
            value = piece[pl.ds(part * share, share), :]
            for k, wanted in enumerate((~below, below)):
                kept = jnp.where(wanted, value, 0.0)
                total[k][0] += jnp.where(upper, 0.0, kept)
                total[k][1] += jnp.where(upper, kept, 0.0)
        for k in range(2):
            for half in range(2):
                acc[k, part, :, pl.ds(half * window, window)] = total[k][half]


def second_sum_kernel(start, window, classes, acc, *refs):
    pieces, outs = refs[:classes], refs[classes:]
    share = window // classes
    own = lax.rem(lax.axis_index("pos"), classes)
    for part in range(2):
        total = [[acc[k, part, :, pl.ds(h * window + start, LANES)] for h in range(2)] for k in range(2)]
        total.append([jnp.zeros((share, LANES), F32) for _ in range(2)])
        for piece in pieces:
            upper, below, lowest = placed(piece, start, LANES, own, share, window)
            value = piece[pl.ds(part * share, share), :]
            for k, wanted in enumerate((~below, below & ~lowest, lowest)):
                kept = jnp.where(wanted, value, 0.0)
                total[k][0] += jnp.where(upper, 0.0, kept)
                total[k][1] += jnp.where(upper, kept, 0.0)
        for k in range(3):
            for half in range(2):
                outs[k][pl.ds((half * 2 + part) * share, share), :] = total[k][half]


def final_kernel(tiles, share, *refs):
    kept, received, out = refs[:tiles], refs[tiles : 2 * tiles], refs[2 * tiles]
    for tile in range(tiles):
        for half in range(2):
            for part in range(2):
                here = pl.ds((half * 2 + part) * share, share)
                line = (half * tiles + tile) * 2 + part
                out[pl.ds(line, share, stride=4 * tiles), :] = kept[tile][here, :] + received[tile][here, :]


def on_device(object_field, illumination, amplitudes, row_offset, col_offset):
    band_rows, _, columns = object_field.shape
    window = illumination.shape[0]
    ways = lax.axis_size("pos")
    assert band_rows == 2 * window and columns == 2 * window and row_offset.shape[0] == 2
    classes = ways // 2
    share = window // classes
    tiles = window // LANES
    scalars = (row_offset, col_offset)

    remote = tuple(pltpu.with_memory_space_constraint(scalar, pltpu.HBM) for scalar in scalars)
    (wanted,) = kernel_call(functools.partial(pick_kernel, window), [(8, LANES)], remote, [])
    wanted = shifted(wanted, "tile", 1)
    obj, ill, amps, table = loaded([linear(object_field), linear(illumination), amplitudes, split_tables(window)])
    (rim,) = kernel_call(functools.partial(rim_kernel, window), [(2, window, window)], (), [wanted, obj])
    rim = shifted(rim, "tile", -1)

    def spread(pieces):
        moved = {d: exchanged(pieces[d], "pos", d) for d in reversed(range(1, classes))}
        return [pieces[0]] + [moved[d] for d in range(1, classes)]

    near = spread(wave(0, window, classes, scalars, [obj, ill, amps, table]))
    (acc,) = kernel_call(functools.partial(first_sum_kernel, window, classes), [(2, 2, share, columns)], (), near)
    *pieces, probe, xh, xl = wave(1, window, classes, scalars, [obj, ill, amps, table, rim])
    late = [spread(pieces)]
    for lane_tile in range(1, tiles):
        pieces = rest(lane_tile, window, classes, scalars, [table, probe, xh, xl])
        late.append(spread(pieces))
    is_upper = lax.axis_index("pos") >= classes
    kept, received = [], []
    for lane_tile in range(tiles):
        top, middle, spilled = kernel_call(
            functools.partial(second_sum_kernel, lane_tile * LANES, window, classes),
            [(4 * share, LANES)] * 3,
            (),
            [acc, *late[lane_tile]],
        )
        spilled = shifted(spilled, "tile", 1)
        top = top + spilled
        outgoing = jnp.where(is_upper, top, middle)
        received.append(exchanged(outgoing, "pos", classes))
        kept.append(jnp.where(is_upper, middle, top))
    result = pl.pallas_call(
        functools.partial(final_kernel, tiles, share),
        out_shape=jax.ShapeDtypeStruct((share * 4 * tiles, LANES), F32),
        in_specs=[pl.BlockSpec(memory_space=pltpu.VMEM)] * (2 * tiles),
        out_specs=pl.BlockSpec(memory_space=pltpu.VMEM),
        compiler_params=pltpu.CompilerParams(vmem_limit_bytes=16 << 20),
        name="final",
    )(*[in_vmem(array) for array in kept + received])
    return unlinear(result, share, columns)


def solution(mesh):
    in_specs = (
        P("tile", None, None),
        P(),
        P(("tile", "pos"), None, None),
        P(("tile", "pos")),
        P(("tile", "pos")),
    )
    out_specs = P(("tile", "pos"), None, None)

    return jax.shard_map(on_device, mesh=mesh, in_specs=in_specs, out_specs=out_specs, check_vma=False)
```

```python
import functools
import math

import jax
import jax.numpy as jnp
import numpy as np
from jax import lax
from jax.experimental import pallas as pl
from jax.experimental.pallas import tpu as pltpu
from jax.sharding import PartitionSpec as P

LANES = 128
F32 = jnp.float32
BF16 = jnp.bfloat16


def shifted(block, axis, distance):
    devices = range(lax.axis_size(axis))
    route = [(i - distance, i) for i in devices if i - distance in devices]
    return lax.ppermute(block, axis, route)


def exchanged(block, axis, flip):
    return lax.ppermute(block, axis, [(i, i ^ flip) for i in range(lax.axis_size(axis))])


def split_tables(length):
    indices = np.arange(length, dtype=np.int64)
    angles = (indices[:, None] * indices[None, :] % length) * (2.0 * math.pi / length)
    factor = 1.0 / math.sqrt(length)
    whole = np.concatenate([np.cos(angles), np.sin(angles)], axis=0) * factor
    high = whole.astype(BF16)
    low = (whole - high.astype(np.float64)).astype(BF16)
    return jnp.asarray(np.concatenate([high, low], axis=0))


def linear(array):
    rows, parts, columns = array.shape
    tiles = columns // LANES
    return array.reshape(rows, parts, tiles, LANES).transpose(0, 2, 1, 3).reshape(rows * tiles * parts, LANES)


def unlinear(array, rows, columns):
    tiles = columns // LANES
    return array.reshape(rows, tiles, 2, LANES).transpose(0, 2, 1, 3).reshape(rows, 2, columns)


def halves(value):
    high = value.astype(BF16)
    return high, (value - high.astype(F32)).astype(BF16)


def dot3(high_left, low_left, high_right, low_right):
    left = jnp.concatenate([low_left, high_left, high_left], axis=1)
    right = jnp.concatenate([high_right, low_right, high_right], axis=0)
    return jnp.dot(left, right, preferred_element_type=F32)


def in_vmem(array):
    return pltpu.with_memory_space_constraint(array, pltpu.VMEM)


def kernel_call(body, name, out_shapes, scalars, arrays, scratch=(), flops=0):
    smem = pl.BlockSpec(memory_space=pltpu.SMEM)
    vmem = pl.BlockSpec(memory_space=pltpu.VMEM)
    moved = sum(4 * math.prod(shape) for shape in out_shapes)
    return pl.pallas_call(
        body,
        out_shape=[pltpu.VMEM(shape, F32) for shape in out_shapes],
        in_specs=[smem] * len(scalars) + [vmem] * len(arrays),
        out_specs=[vmem] * len(out_shapes),
        scratch_shapes=scratch,
        cost_estimate=pl.CostEstimate(flops=flops, transcendentals=0, bytes_accessed=2 * moved),
        compiler_params=pltpu.CompilerParams(vmem_limit_bytes=16 << 20),
        name=name,
    )(*scalars, *[in_vmem(array) for array in arrays])


def chosen(slot, rows, cols, band_start, window):
    crossing = (rows[0] - band_start > window).astype(jnp.int32)
    index = crossing if slot == 0 else 1 - crossing
    return rows[index] - band_start, cols[index], index


def load_kernel(number, *refs):
    sources, targets, sem = refs[:number], refs[number : 2 * number], refs[2 * number]
    copies = [pltpu.make_async_copy(a, b, sem.at[i]) for i, (a, b) in enumerate(zip(sources, targets))]
    for copy in copies:
        copy.start()
    for copy in copies:
        copy.wait()


def loaded(arrays):
    return pl.pallas_call(
        functools.partial(load_kernel, len(arrays)),
        out_shape=[pltpu.VMEM(array.shape, array.dtype) for array in arrays],
        in_specs=[pl.BlockSpec(memory_space=pl.ANY)] * len(arrays),
        out_specs=[pl.BlockSpec(memory_space=pltpu.VMEM)] * len(arrays),
        scratch_shapes=[pltpu.SemaphoreType.DMA((len(arrays),))],
        compiler_params=pltpu.CompilerParams(vmem_limit_bytes=16 << 20),
        name="load",
    )(*[pltpu.with_memory_space_constraint(array, pltpu.HBM) for array in arrays])


def pick_kernel(window, rows, cols, out):
    _, column, _ = chosen(1, rows, cols, lax.axis_index("tile") * (2 * window), window)
    out[...] = jnp.broadcast_to(column.astype(F32), out.shape)


def rim_kernel(window, wanted, obj, out):
    offset = wanted[pl.ds(0, 1), :]
    tiles = window // LANES
    for tile in range(tiles):
        column = (lax.broadcasted_iota(jnp.int32, (window, LANES), 1) + tile * LANES).astype(F32)
        for part in range(2):
            near = obj[pl.ds(tile * 2 + part, window, stride=4 * tiles), :]
            beyond = obj[pl.ds((tiles + tile) * 2 + part, window, stride=4 * tiles), :]
            out[part, :, pl.ds(tile * LANES, LANES)] = jnp.where(column < offset, beyond, near)


def wave_kernel(slot, window, classes, with_rim, rows, cols, obj, ill, amps, table, *refs):
    if with_rim:
        rim, refs = refs[0], refs[1:]
    outs, refs = refs[:classes], refs[classes:]
    doubled, probe, xh, xl, far = refs
    tiles = window // LANES
    row, column, index = chosen(slot, rows, cols, lax.axis_index("tile") * (2 * window), window)
    own = lax.rem(lax.axis_index("pos"), classes)
    size = 32
    step = 2 * tiles
    whole = window * step
    doubled[pl.ds(0, whole), :] = ill[...]
    doubled[pl.ds(whole, size * step), :] = ill[pl.ds(0, size * step), :]
    turn = lax.rem(row, window)

    def store_pair(first, real, imag):
        here = pl.ds(first, size)
        below = pl.ds(window + first, size)
        left, right = pl.ds(0, window), pl.ds(window, window)
        for part, ref in zip(range(2), (xh, xl)):
            r, i, n = (halves(v)[part] for v in (real, imag, -real))
            ref[here, left] = r
            ref[here, right] = i
            ref[below, left] = i
            ref[below, right] = n

    for first in range(0, window, size):
        place = lax.broadcasted_iota(jnp.int32, (size, window), 0) + first
        across = lax.broadcasted_iota(jnp.int32, (size, window), 1)
        start = lax.rem(first + window - turn, window) * step
        pair = []
        for part in range(2):
            rolled = jnp.concatenate(
                [doubled[pl.ds(start + tile * 2 + part, size, stride=step), :] for tile in range(tiles)],
                axis=1,
            )
            rolled = pltpu.roll(rolled, column, 1)
            probe[part, pl.ds(first, size), :] = rolled

            def block(base):
                def tile_at(tile):
                    return obj[pl.ds((base + first) * 2 * step + tile * 2 + part, size, stride=2 * step), :]

                near = jnp.concatenate([tile_at(t) for t in range(tiles)], axis=1)
                beyond = jnp.concatenate([tile_at(t + tiles) for t in range(tiles)], axis=1)
                return jnp.where(across < column, beyond, near)

            seen = jnp.where(place < row, block(window), block(0))
            if with_rim:
                seen = jnp.where(place + window < row, rim[part, pl.ds(first, size), :], seen)
            pair.append((rolled, seen))
        (probe_real, obj_real), (probe_imag, obj_imag) = pair
        store_pair(
            first,
            probe_real * obj_real - probe_imag * obj_imag,
            probe_real * obj_imag + probe_imag * obj_real,
        )

    high = table[pl.ds(0, 2 * window), :]
    low = table[pl.ds(2 * window, 2 * window), :]
    left_high = jnp.concatenate([table[pl.ds(0, window), :], table[pl.ds(window, window), :]], axis=1)
    left_low = jnp.concatenate([table[pl.ds(2 * window, window), :], table[pl.ds(3 * window, window), :]], axis=1)

    def both_sides():
        mid = dot3(xh[...], xl[...], high, low)
        for first in range(0, window, size):
            store_pair(first, mid[first : first + size], mid[window + first : window + first + size])
        far[...] = dot3(left_high, left_low, xh[...], xl[...])

    both_sides()
    for first in range(0, window, size):
        real = far[pl.ds(first, size), pl.ds(0, window)]
        imag = far[pl.ds(first, size), pl.ds(window, window)]
        inverse = jnp.minimum(lax.rsqrt(real * real + imag * imag), 4.0)
        scaled = amps[index, pl.ds(first, size), :].astype(F32) * inverse
        store_pair(first, real * (1.0 - scaled), imag * (scaled - 1.0))
    both_sides()

    share = window // classes
    for flip in range(classes):
        base = pl.multiple_of((own ^ flip) * share, share)
        here = pl.ds(base, share)
        real = far[here, pl.ds(0, window)]
        imag = far[here, pl.ds(window, window)]
        probe_real = probe[0, here, :]
        probe_imag = probe[1, here, :]
        outs[flip][pl.ds(0, share), :] = probe_real * real - probe_imag * imag
        outs[flip][pl.ds(share, share), :] = -(probe_real * imag + probe_imag * real)
        line = lax.broadcasted_iota(jnp.int32, (8, window), 0)
        outs[flip][pl.ds(2 * share, 8), :] = jnp.where(line == 0, row, column).astype(F32)


def wave(slot, window, classes, scalars, arrays):
    share = window // classes
    tiles = window // LANES
    scratch = [
        pltpu.VMEM(((window + 32) * 2 * tiles + 8, LANES), F32),
        pltpu.VMEM((2, window, window), F32),
        pltpu.VMEM((2 * window, 2 * window), BF16),
        pltpu.VMEM((2 * window, 2 * window), BF16),
        pltpu.VMEM((window, 2 * window), F32),
    ]
    return kernel_call(
        functools.partial(wave_kernel, slot, window, classes, len(arrays) == 5),
        "wave" + str(slot),
        [(2 * share + 8, window)] * classes,
        scalars,
        arrays,
        scratch,
        96 * window**3,
    )


def placed(piece, own, share, window):
    row = piece[pl.ds(2 * share, 1), :]
    column = piece[pl.ds(2 * share + 1, 1), :]
    place = (lax.broadcasted_iota(jnp.int32, (share, window), 0) + own * share).astype(F32)
    across = lax.broadcasted_iota(jnp.int32, (share, window), 1).astype(F32)
    return across < column, place < row, place + float(window) < row


def first_sum_kernel(window, classes, *refs):
    pieces, acc = refs[:classes], refs[classes]
    share = window // classes
    own = lax.rem(lax.axis_index("pos"), classes)
    for part in range(2):
        total = [[jnp.zeros((share, window), F32) for _ in range(2)] for _ in range(2)]
        for piece in pieces:
            upper, below, _ = placed(piece, own, share, window)
            value = piece[pl.ds(part * share, share), :]
            for k, wanted in enumerate((~below, below)):
                kept = jnp.where(wanted, value, 0.0)
                total[k][0] += jnp.where(upper, 0.0, kept)
                total[k][1] += jnp.where(upper, kept, 0.0)
        for k in range(2):
            for half in range(2):
                acc[k, part, :, pl.ds(half * window, window)] = total[k][half]


def second_sum_kernel(window, classes, acc, *refs):
    pieces, outs = refs[:classes], refs[classes:]
    share = window // classes
    tiles = window // LANES
    own = lax.rem(lax.axis_index("pos"), classes)
    for part in range(2):
        total = [[acc[k, part, :, pl.ds(h * window, window)] for h in range(2)] for k in range(2)]
        total.append([jnp.zeros((share, window), F32) for _ in range(2)])
        for piece in pieces:
            upper, below, lowest = placed(piece, own, share, window)
            value = piece[pl.ds(part * share, share), :]
            for k, wanted in enumerate((~below, below & ~lowest, lowest)):
                kept = jnp.where(wanted, value, 0.0)
                total[k][0] += jnp.where(upper, 0.0, kept)
                total[k][1] += jnp.where(upper, kept, 0.0)
        for k in range(3):
            for half in range(2):
                for tile in range(tiles):
                    outs[k][pl.ds((half * tiles + tile) * 2 + part, share, stride=4 * tiles), :] = total[k][half][
                        :, tile * LANES : (tile + 1) * LANES
                    ]


def on_device(object_field, illumination, amplitudes, row_offset, col_offset):
    band_rows, _, columns = object_field.shape
    window = illumination.shape[0]
    ways = lax.axis_size("pos")
    assert band_rows == 2 * window and columns == 2 * window and row_offset.shape[0] == 2
    classes = ways // 2
    share = window // classes
    tiles = window // LANES
    scalars = (row_offset, col_offset)

    remote = tuple(pltpu.with_memory_space_constraint(scalar, pltpu.HBM) for scalar in scalars)
    (wanted,) = kernel_call(functools.partial(pick_kernel, window), "pick", [(8, LANES)], remote, [])
    wanted = shifted(wanted, "tile", 1)
    obj, ill, amps, table = loaded([linear(object_field), linear(illumination), amplitudes, split_tables(window)])
    (rim,) = kernel_call(functools.partial(rim_kernel, window), "rim", [(2, window, window)], (), [wanted, obj])
    rim = shifted(rim, "tile", -1)

    def spread(pieces):
        moved = {d: exchanged(pieces[d], "pos", d) for d in reversed(range(1, classes))}
        return [pieces[0]] + [moved[d] for d in range(1, classes)]

    near = spread(wave(0, window, classes, scalars, [obj, ill, amps, table]))
    (acc,) = kernel_call(
        functools.partial(first_sum_kernel, window, classes), "sum0", [(2, 2, share, columns)], (), near
    )
    late = spread(wave(1, window, classes, scalars, [obj, ill, amps, table, rim]))
    top, middle, spilled = kernel_call(
        functools.partial(second_sum_kernel, window, classes),
        "sum1",
        [(share * 4 * tiles, LANES)] * 3,
        (),
        [acc, *late],
    )
    top = top + shifted(spilled, "tile", 1)
    is_upper = lax.axis_index("pos") >= classes
    received = exchanged(jnp.where(is_upper, top, middle), "pos", classes)
    result = jnp.where(is_upper, middle, top) + received
    return unlinear(result, share, columns)


def solution(mesh):
    in_specs = (
        P("tile", None, None),
        P(),
        P(("tile", "pos"), None, None),
        P(("tile", "pos")),
        P(("tile", "pos")),
    )
    out_specs = P(("tile", "pos"), None, None)
    return jax.shard_map(
        on_device, mesh=mesh, in_specs=in_specs, out_specs=out_specs, check_vma=False
    )
```

```python
import functools
import math

import jax
import jax.numpy as jnp
import numpy as np
from jax import lax
from jax.experimental import pallas as pl
from jax.experimental.pallas import tpu as pltpu
from jax.sharding import PartitionSpec as P

LANES = 128
F32 = jnp.float32
BF16 = jnp.bfloat16


def shifted(block, axis, distance):
    devices = range(lax.axis_size(axis))
    route = [(i - distance, i) for i in devices if i - distance in devices]
    return lax.ppermute(block, axis, route)


def exchanged(block, axis, flip):
    return lax.ppermute(block, axis, [(i, i ^ flip) for i in range(lax.axis_size(axis))])


def split_tables(length):
    half = length // 2
    n = np.arange(half, dtype=np.int64)
    even = 2 * n[:, None] * n[None, :]
    odd = n[:, None] * (2 * n[None, :] + 1)
    rows = []
    for product in (even, odd, odd.T):
        angles = (product % length) * (2.0 * math.pi / length)
        real, imag = np.cos(angles) / math.sqrt(length), -np.sin(angles) / math.sqrt(length)
        whole = np.concatenate([real, imag, -imag], axis=1)
        high = whole.astype(BF16)
        rows += [high, (whole - high.astype(np.float64)).astype(BF16)]
    return jnp.asarray(np.concatenate(rows, axis=0))


def linear(array):
    rows, parts, columns = array.shape
    tiles = columns // LANES
    return array.reshape(rows, parts, tiles, LANES).transpose(0, 2, 1, 3).reshape(rows * tiles * parts, LANES)


def unlinear(array, rows, columns):
    tiles = columns // LANES
    return array.reshape(rows, tiles, 2, LANES).transpose(0, 2, 1, 3).reshape(rows, 2, columns)


def halves(value):
    high = value.astype(BF16)
    return high, (value - high.astype(F32)).astype(BF16)


def dot3(high_left, low_left, high_right, low_right):
    left = jnp.concatenate([low_left, high_left, high_left], axis=1)
    right = jnp.concatenate([high_right, low_right, high_right], axis=0)
    return jnp.dot(left, right, preferred_element_type=F32)


def in_vmem(array):
    return pltpu.with_memory_space_constraint(array, pltpu.VMEM)


def kernel_call(body, name, out_shapes, scalars, arrays, scratch=(), flops=0):
    smem = pl.BlockSpec(memory_space=pltpu.SMEM)
    vmem = pl.BlockSpec(memory_space=pltpu.VMEM)
    moved = sum(4 * math.prod(shape) for shape in out_shapes)
    return pl.pallas_call(
        body,
        out_shape=[pltpu.VMEM(shape, F32) for shape in out_shapes],
        in_specs=[smem] * len(scalars) + [vmem] * len(arrays),
        out_specs=[vmem] * len(out_shapes),
        scratch_shapes=scratch,
        cost_estimate=pl.CostEstimate(flops=flops, transcendentals=0, bytes_accessed=2 * moved),
        compiler_params=pltpu.CompilerParams(vmem_limit_bytes=16 << 20),
        name=name,
    )(*scalars, *[in_vmem(array) for array in arrays])


def chosen(slot, rows, cols, band_start, window):
    crossing = (rows[0] - band_start > window).astype(jnp.int32)
    index = crossing if slot == 0 else 1 - crossing
    return rows[index] - band_start, cols[index], index


def load_kernel(number, *refs):
    sources, targets, sem = refs[:number], refs[number : 2 * number], refs[2 * number]
    copies = [pltpu.make_async_copy(a, b, sem.at[i]) for i, (a, b) in enumerate(zip(sources, targets))]
    for copy in copies:
        copy.start()
    for copy in copies:
        copy.wait()


def loaded(arrays):
    return pl.pallas_call(
        functools.partial(load_kernel, len(arrays)),
        out_shape=[pltpu.VMEM(array.shape, array.dtype) for array in arrays],
        in_specs=[pl.BlockSpec(memory_space=pl.ANY)] * len(arrays),
        out_specs=[pl.BlockSpec(memory_space=pltpu.VMEM)] * len(arrays),
        scratch_shapes=[pltpu.SemaphoreType.DMA((len(arrays),))],
        compiler_params=pltpu.CompilerParams(vmem_limit_bytes=16 << 20),
        name="load",
    )(*[pltpu.with_memory_space_constraint(array, pltpu.HBM) for array in arrays])


def pick_kernel(window, rows, cols, out):
    _, column, _ = chosen(1, rows, cols, lax.axis_index("tile") * (2 * window), window)
    out[...] = jnp.broadcast_to(column.astype(F32), out.shape)


def rim_kernel(window, wanted, obj, out):
    offset = wanted[pl.ds(0, 1), :]
    tiles = window // LANES
    for tile in range(tiles):
        column = (lax.broadcasted_iota(jnp.int32, (window, LANES), 1) + tile * LANES).astype(F32)
        for part in range(2):
            near = obj[pl.ds(tile * 2 + part, window, stride=4 * tiles), :]
            beyond = obj[pl.ds((tiles + tile) * 2 + part, window, stride=4 * tiles), :]
            out[part, :, pl.ds(tile * LANES, LANES)] = jnp.where(column < offset, beyond, near)


def wave_kernel(slot, window, classes, with_rim, rows, cols, obj, ill, amps, table, *refs):
    if with_rim:
        rim, refs = refs[0], refs[1:]
    outs, refs = refs[:classes], refs[classes:]
    doubled, probe, xh, xl, yh, yl, far, ordered = refs
    tiles = window // LANES
    half = window // 2
    row, column, index = chosen(slot, rows, cols, lax.axis_index("tile") * (2 * window), window)
    own = lax.rem(lax.axis_index("pos"), classes)
    size = 32
    step = 2 * tiles
    whole = window * step
    doubled[pl.ds(0, whole), :] = ill[...]
    doubled[pl.ds(whole, size * step), :] = ill[pl.ds(0, size * step), :]
    turn = lax.rem(row, window)

    below = lax.broadcasted_iota(jnp.int32, (window, window), 0)
    beside = lax.broadcasted_iota(jnp.int32, (window, window), 1)

    def picks(frequency, place):
        wanted = jnp.where(place < half, 2 * place, 2 * (place - half) + 1)
        return jnp.where(frequency == wanted, 1.0, 0.0).astype(BF16)

    by_column = jnp.dot(amps[index], picks(below, beside), preferred_element_type=F32).astype(BF16)
    ordered[...] = jnp.dot(picks(beside, below), by_column, preferred_element_type=F32)

    def block_of(matrix, part, low):
        return table[pl.ds((2 * matrix + low) * half, half), pl.ds(part * half, half)]

    def factor(matrix, order):
        return [
            jnp.concatenate(
                [
                    jnp.concatenate([block_of(matrix, part, low) for part in line], axis=1)
                    for line in order
                ],
                axis=0,
            )
            for low in range(2)
        ]

    def from_right(first, matrix):
        across = pl.ds(first, window)
        return dot3(xh[:, across], xl[:, across], *factor(matrix, ((0, 1), (2, 0))))

    def from_left(matrix, first):
        down = pl.ds(first, window)
        return dot3(*factor(matrix, ((0, 2), (1, 0))), yh[down, :], yl[down, :])

    def keep(high_ref, low_ref, here, across, value):
        high, low = halves(value)
        high_ref[here, across] = high
        low_ref[here, across] = low

    for first in range(0, window, size):
        place = lax.broadcasted_iota(jnp.int32, (size, window), 0) + first
        across = lax.broadcasted_iota(jnp.int32, (size, window), 1)
        start = lax.rem(first + window - turn, window) * step
        pair = []
        for part in range(2):
            rolled = jnp.concatenate(
                [doubled[pl.ds(start + tile * 2 + part, size, stride=step), :] for tile in range(tiles)],
                axis=1,
            )
            rolled = pltpu.roll(rolled, column, 1)
            probe[part, pl.ds(first, size), :] = rolled

            def block(base):
                def tile_at(tile):
                    return obj[pl.ds((base + first) * 2 * step + tile * 2 + part, size, stride=2 * step), :]

                near = jnp.concatenate([tile_at(t) for t in range(tiles)], axis=1)
                beyond = jnp.concatenate([tile_at(t + tiles) for t in range(tiles)], axis=1)
                return jnp.where(across < column, beyond, near)

            seen = jnp.where(place < row, block(window), block(0))
            if with_rim:
                seen = jnp.where(place + window < row, rim[part, pl.ds(first, size), :], seen)
            pair.append((rolled, seen))
        (probe_real, obj_real), (probe_imag, obj_imag) = pair
        exits = (
            probe_real * obj_real - probe_imag * obj_imag,
            probe_real * obj_imag + probe_imag * obj_real,
        )
        here = pl.ds(first, size)
        for part, value in enumerate(exits):
            left, right = value[:, :half], value[:, half:]
            keep(xh, xl, here, pl.ds(part * half, half), left + right)
            keep(xh, xl, here, pl.ds(window + part * half, half), left - right)

    for parity in range(2):
        mid = from_right(parity * window, parity)
        across = pl.ds(parity * half, half)
        for first in range(0, half, size):
            top, bottom = mid[first : first + size], mid[half + first : half + first + size]
            for line, value in enumerate((top + bottom, top - bottom)):
                for part in range(2):
                    here = pl.ds((2 * line + part) * half + first, size)
                    keep(yh, yl, here, across, value[:, part * half : (part + 1) * half])
    far[pl.ds(0, window), :] = from_left(0, 0)
    far[pl.ds(window, window), :] = from_left(2, window)

    for parity in range(2):
        for first in range(0, half, size):
            real = far[pl.ds(parity * window + first, size), :]
            imag = far[pl.ds(parity * window + half + first, size), :]
            here = pl.ds(parity * half + first, size)
            inverse = jnp.minimum(lax.rsqrt(real * real + imag * imag), 4.0)
            scaled = ordered[here, :] * inverse
            for part, value in enumerate((real * (1.0 - scaled), imag * (scaled - 1.0))):
                for side in range(2):
                    across = pl.ds(side * window + part * half, half)
                    keep(xh, xl, here, across, value[:, side * half : (side + 1) * half])

    even, odd = from_right(0, 0), from_right(window, 2)
    for first in range(0, window, size):
        near, beyond = even[first : first + size], odd[first : first + size]
        parity, place = first // half, first % half
        for side, value in enumerate((near + beyond, near - beyond)):
            for part in range(2):
                here = pl.ds((2 * parity + part) * half + place, size)
                keep(yh, yl, here, pl.ds(side * half, half), value[:, part * half : (part + 1) * half])
    far[pl.ds(0, window), :] = from_left(0, 0)
    far[pl.ds(window, window), :] = from_left(1, window)

    share = window // classes
    for flip in range(classes):
        base = pl.multiple_of((own ^ flip) * share, share)
        place = pl.multiple_of(lax.rem(base, half), share)
        sign = jnp.where(base < half, 1.0, -1.0)
        real, imag = (
            far[pl.ds(part * half + place, share), :] + sign * far[pl.ds(window + part * half + place, share), :]
            for part in range(2)
        )
        here = pl.ds(base, share)
        probe_real = probe[0, here, :]
        probe_imag = probe[1, here, :]
        outs[flip][pl.ds(0, share), :] = probe_real * real - probe_imag * imag
        outs[flip][pl.ds(share, share), :] = -(probe_real * imag + probe_imag * real)
        line = lax.broadcasted_iota(jnp.int32, (8, window), 0)
        outs[flip][pl.ds(2 * share, 8), :] = jnp.where(line == 0, row, column).astype(F32)


def wave(slot, window, classes, scalars, arrays):
    share = window // classes
    tiles = window // LANES
    scratch = [
        pltpu.VMEM(((window + 32) * 2 * tiles + 8, LANES), F32),
        pltpu.VMEM((2, window, window), F32),
        pltpu.VMEM((window, 2 * window), BF16),
        pltpu.VMEM((window, 2 * window), BF16),
        pltpu.VMEM((2 * window, window), BF16),
        pltpu.VMEM((2 * window, window), BF16),
        pltpu.VMEM((2 * window, window), F32),
        pltpu.VMEM((window, window), F32),
    ]
    return kernel_call(
        functools.partial(wave_kernel, slot, window, classes, len(arrays) == 5),
        "wave" + str(slot),
        [(2 * share + 8, window)] * classes,
        scalars,
        arrays,
        scratch,
        48 * window**3,
    )


def placed(piece, own, share, window):
    row = piece[pl.ds(2 * share, 1), :]
    column = piece[pl.ds(2 * share + 1, 1), :]
    place = (lax.broadcasted_iota(jnp.int32, (share, window), 0) + own * share).astype(F32)
    across = lax.broadcasted_iota(jnp.int32, (share, window), 1).astype(F32)
    return across < column, place < row, place + float(window) < row


def first_sum_kernel(window, classes, *refs):
    pieces, acc = refs[:classes], refs[classes]
    share = window // classes
    own = lax.rem(lax.axis_index("pos"), classes)
    for part in range(2):
        total = [[jnp.zeros((share, window), F32) for _ in range(2)] for _ in range(2)]
        for piece in pieces:
            upper, below, _ = placed(piece, own, share, window)
            value = piece[pl.ds(part * share, share), :]
            for k, wanted in enumerate((~below, below)):
                kept = jnp.where(wanted, value, 0.0)
                total[k][0] += jnp.where(upper, 0.0, kept)
                total[k][1] += jnp.where(upper, kept, 0.0)
        for k in range(2):
            for half in range(2):
                acc[k, part, :, pl.ds(half * window, window)] = total[k][half]


def second_sum_kernel(window, classes, acc, *refs):
    pieces, outs = refs[:classes], refs[classes:]
    share = window // classes
    tiles = window // LANES
    own = lax.rem(lax.axis_index("pos"), classes)
    for part in range(2):
        total = [[acc[k, part, :, pl.ds(h * window, window)] for h in range(2)] for k in range(2)]
        total.append([jnp.zeros((share, window), F32) for _ in range(2)])
        for piece in pieces:
            upper, below, lowest = placed(piece, own, share, window)
            value = piece[pl.ds(part * share, share), :]
            for k, wanted in enumerate((~below, below & ~lowest, lowest)):
                kept = jnp.where(wanted, value, 0.0)
                total[k][0] += jnp.where(upper, 0.0, kept)
                total[k][1] += jnp.where(upper, kept, 0.0)
        for k in range(3):
            for half in range(2):
                for tile in range(tiles):
                    outs[k][pl.ds((half * tiles + tile) * 2 + part, share, stride=4 * tiles), :] = total[k][half][
                        :, tile * LANES : (tile + 1) * LANES
                    ]


def on_device(object_field, illumination, amplitudes, row_offset, col_offset):
    band_rows, _, columns = object_field.shape
    window = illumination.shape[0]
    ways = lax.axis_size("pos")
    assert band_rows == 2 * window and columns == 2 * window and row_offset.shape[0] == 2
    classes = ways // 2
    share = window // classes
    tiles = window // LANES
    scalars = (row_offset, col_offset)

    remote = tuple(pltpu.with_memory_space_constraint(scalar, pltpu.HBM) for scalar in scalars)
    (wanted,) = kernel_call(functools.partial(pick_kernel, window), "pick", [(8, LANES)], remote, [])
    wanted = shifted(wanted, "tile", 1)
    obj, ill, amps, table = loaded([linear(object_field), linear(illumination), amplitudes, split_tables(window)])
    (rim,) = kernel_call(functools.partial(rim_kernel, window), "rim", [(2, window, window)], (), [wanted, obj])
    rim = shifted(rim, "tile", -1)

    def spread(pieces):
        moved = {d: exchanged(pieces[d], "pos", d) for d in reversed(range(1, classes))}
        return [pieces[0]] + [moved[d] for d in range(1, classes)]

    near = spread(wave(0, window, classes, scalars, [obj, ill, amps, table]))
    (acc,) = kernel_call(
        functools.partial(first_sum_kernel, window, classes), "sum0", [(2, 2, share, columns)], (), near
    )
    late = spread(wave(1, window, classes, scalars, [obj, ill, amps, table, rim]))
    top, middle, spilled = kernel_call(
        functools.partial(second_sum_kernel, window, classes),
        "sum1",
        [(share * 4 * tiles, LANES)] * 3,
        (),
        [acc, *late],
    )
    top = top + shifted(spilled, "tile", 1)
    is_upper = lax.axis_index("pos") >= classes
    received = exchanged(jnp.where(is_upper, top, middle), "pos", classes)
    result = jnp.where(is_upper, middle, top) + received
    return unlinear(result, share, columns)


def solution(mesh):
    in_specs = (
        P("tile", None, None),
        P(),
        P(("tile", "pos"), None, None),
        P(("tile", "pos")),
        P(("tile", "pos")),
    )
    out_specs = P(("tile", "pos"), None, None)
    return jax.shard_map(
        on_device, mesh=mesh, in_specs=in_specs, out_specs=out_specs, check_vma=False
    )
```

```python
import functools
import math

import jax
import jax.numpy as jnp
import numpy as np
from jax import lax
from jax.experimental import pallas as pl
from jax.experimental.pallas import tpu as pltpu
from jax.sharding import PartitionSpec as P


LANES = 128
F32 = jnp.float32
BF16 = jnp.bfloat16


def shifted(block, axis, distance):
    devices = range(lax.axis_size(axis))
    route = [(i - distance, i) for i in devices if i - distance in devices]
    return lax.ppermute(block, axis, route)


def exchanged(block, axis, flip):
    return lax.ppermute(block, axis, [(i, i ^ flip) for i in range(lax.axis_size(axis))])


def split_tables(length):
    half = length // 2
    n = np.arange(half, dtype=np.int64)
    even = 2 * n[:, None] * n[None, :]
    odd = n[:, None] * (2 * n[None, :] + 1)
    rows = []
    for product in (even, odd, odd.T):
        angles = (product % length) * (2.0 * math.pi / length)
        real, imag = np.cos(angles) / math.sqrt(length), -np.sin(angles) / math.sqrt(length)
        whole = np.concatenate([real, imag, -imag], axis=1)
        high = whole.astype(BF16)
        rows += [high, (whole - high.astype(np.float64)).astype(BF16)]
    return jnp.asarray(np.concatenate(rows, axis=0))


def linear(array):
    rows, parts, columns = array.shape
    tiles = columns // LANES
    return array.reshape(rows, parts, tiles, LANES).transpose(0, 2, 1, 3).reshape(rows * tiles * parts, LANES)


def unlinear(array, rows, columns):
    tiles = columns // LANES
    return array.reshape(rows, tiles, 2, LANES).transpose(0, 2, 1, 3).reshape(rows, 2, columns)


def halves(value):
    high = value.astype(BF16)
    return high, (value - high.astype(F32)).astype(BF16)


def dot3(high_left, low_left, high_right, low_right):
    left = jnp.concatenate([low_left, high_left, high_left], axis=1)
    right = jnp.concatenate([high_right, low_right, high_right], axis=0)
    return jnp.dot(left, right, preferred_element_type=F32)


def in_vmem(array):
    return pltpu.with_memory_space_constraint(array, pltpu.VMEM)


def kernel_call(body, out_shapes, scalars, arrays, scratch=(), flops=0):
    smem = pl.BlockSpec(memory_space=pltpu.SMEM)
    vmem = pl.BlockSpec(memory_space=pltpu.VMEM)
    moved = sum(4 * math.prod(shape) for shape in out_shapes)
    return pl.pallas_call(
        body,
        out_shape=[pltpu.VMEM(shape, F32) for shape in out_shapes],
        in_specs=[smem] * len(scalars) + [vmem] * len(arrays),
        out_specs=[vmem] * len(out_shapes),
        scratch_shapes=scratch,
        cost_estimate=pl.CostEstimate(flops=flops, transcendentals=0, bytes_accessed=2 * moved),
        compiler_params=pltpu.CompilerParams(vmem_limit_bytes=16 << 20),
    )(*scalars, *[in_vmem(array) for array in arrays])


def chosen(slot, rows, cols, band_start, window):
    crossing = (rows[0] - band_start > window).astype(jnp.int32)
    index = crossing if slot == 0 else 1 - crossing
    return rows[index] - band_start, cols[index], index


def load_kernel(number, *refs):
    sources, targets, sem = refs[:number], refs[number : 2 * number], refs[2 * number]
    copies = [pltpu.make_async_copy(a, b, sem.at[i]) for i, (a, b) in enumerate(zip(sources, targets))]
    for copy in copies:
        copy.start()
    for copy in copies:
        copy.wait()


def loaded(arrays):
    return pl.pallas_call(
        functools.partial(load_kernel, len(arrays)),
        out_shape=[pltpu.VMEM(array.shape, array.dtype) for array in arrays],
        in_specs=[pl.BlockSpec(memory_space=pl.ANY)] * len(arrays),
        out_specs=[pl.BlockSpec(memory_space=pltpu.VMEM)] * len(arrays),
        scratch_shapes=[pltpu.SemaphoreType.DMA((len(arrays),))],
        compiler_params=pltpu.CompilerParams(vmem_limit_bytes=16 << 20),
        name="load",
    )(*[pltpu.with_memory_space_constraint(array, pltpu.HBM) for array in arrays])


def pick_kernel(window, rows, cols, out):
    _, column, _ = chosen(1, rows, cols, lax.axis_index("tile") * (2 * window), window)
    out[...] = jnp.broadcast_to(column.astype(F32), out.shape)


def rim_kernel(window, wanted, obj, out):
    offset = wanted[pl.ds(0, 1), :]
    tiles = window // LANES
    for tile in range(tiles):
        column = (lax.broadcasted_iota(jnp.int32, (window, LANES), 1) + tile * LANES).astype(F32)
        for part in range(2):
            near = obj[pl.ds(tile * 2 + part, window, stride=4 * tiles), :]
            beyond = obj[pl.ds((tiles + tile) * 2 + part, window, stride=4 * tiles), :]
            out[part, :, pl.ds(tile * LANES, LANES)] = jnp.where(column < offset, beyond, near)


def wave_kernel(slot, window, classes, with_rim, rows, cols, obj, ill, amps, table, *refs):
    if with_rim:
        rim, refs = refs[0], refs[1:]
    outs, refs = refs[:classes], refs[classes:]
    doubled, probe, xh, xl, yh, yl, far, ordered = refs
    tiles = window // LANES
    half = window // 2
    row, column, index = chosen(slot, rows, cols, lax.axis_index("tile") * (2 * window), window)
    own = lax.rem(lax.axis_index("pos"), classes)
    size = 32
    step = 2 * tiles
    whole = window * step
    doubled[pl.ds(0, whole), :] = ill[...]
    doubled[pl.ds(whole, size * step), :] = ill[pl.ds(0, size * step), :]
    turn = lax.rem(row, window)

    below = lax.broadcasted_iota(jnp.int32, (window, window), 0)
    beside = lax.broadcasted_iota(jnp.int32, (window, window), 1)

    def picks(frequency, place):
        wanted = jnp.where(place < half, 2 * place, 2 * (place - half) + 1)
        return jnp.where(frequency == wanted, 1.0, 0.0).astype(BF16)

    by_column = jnp.dot(amps[index], picks(below, beside), preferred_element_type=F32).astype(BF16)
    ordered[...] = jnp.dot(picks(beside, below), by_column, preferred_element_type=F32)

    def block_of(matrix, part, low):
        return table[pl.ds((2 * matrix + low) * half, half), pl.ds(part * half, half)]

    def factor(matrix, order):
        return [
            jnp.concatenate(
                [
                    jnp.concatenate([block_of(matrix, part, low) for part in line], axis=1)
                    for line in order
                ],
                axis=0,
            )
            for low in range(2)
        ]

    def from_right(first, matrix):
        across = pl.ds(first, window)
        return dot3(xh[:, across], xl[:, across], *factor(matrix, ((0, 1), (2, 0))))

    def from_left(matrix, first):
        down = pl.ds(first, window)
        return dot3(*factor(matrix, ((0, 2), (1, 0))), yh[down, :], yl[down, :])

    def keep(high_ref, low_ref, here, across, value):
        high, low = halves(value)
        high_ref[here, across] = high
        low_ref[here, across] = low

    for first in range(0, window, size):
        place = lax.broadcasted_iota(jnp.int32, (size, window), 0) + first
        across = lax.broadcasted_iota(jnp.int32, (size, window), 1)
        start = lax.rem(first + window - turn, window) * step
        pair = []
        for part in range(2):
            rolled = jnp.concatenate(
                [doubled[pl.ds(start + tile * 2 + part, size, stride=step), :] for tile in range(tiles)],
                axis=1,
            )
            rolled = pltpu.roll(rolled, column, 1)
            probe[part, pl.ds(first, size), :] = rolled

            def block(base):
                def tile_at(tile):
                    return obj[pl.ds((base + first) * 2 * step + tile * 2 + part, size, stride=2 * step), :]

                near = jnp.concatenate([tile_at(t) for t in range(tiles)], axis=1)
                beyond = jnp.concatenate([tile_at(t + tiles) for t in range(tiles)], axis=1)
                return jnp.where(across < column, beyond, near)

            seen = jnp.where(place < row, block(window), block(0))
            if with_rim:
                seen = jnp.where(place + window < row, rim[part, pl.ds(first, size), :], seen)
            pair.append((rolled, seen))
        (probe_real, obj_real), (probe_imag, obj_imag) = pair
        exits = (
            probe_real * obj_real - probe_imag * obj_imag,
            probe_real * obj_imag + probe_imag * obj_real,
        )
        here = pl.ds(first, size)
        for part, value in enumerate(exits):
            left, right = value[:, :half], value[:, half:]
            keep(xh, xl, here, pl.ds(part * half, half), left + right)
            keep(xh, xl, here, pl.ds(window + part * half, half), left - right)

    for parity in range(2):
        mid = from_right(parity * window, parity)
        across = pl.ds(parity * half, half)
        for first in range(0, half, size):
            top, bottom = mid[first : first + size], mid[half + first : half + first + size]
            for line, value in enumerate((top + bottom, top - bottom)):
                for part in range(2):
                    here = pl.ds((2 * line + part) * half + first, size)
                    keep(yh, yl, here, across, value[:, part * half : (part + 1) * half])
    far[pl.ds(0, window), :] = from_left(0, 0)
    far[pl.ds(window, window), :] = from_left(2, window)

    for parity in range(2):
        for first in range(0, half, size):
            real = far[pl.ds(parity * window + first, size), :]
            imag = far[pl.ds(parity * window + half + first, size), :]
            here = pl.ds(parity * half + first, size)
            inverse = jnp.minimum(lax.rsqrt(real * real + imag * imag), 4.0)
            scaled = ordered[here, :] * inverse
            for part, value in enumerate((real * (1.0 - scaled), imag * (scaled - 1.0))):
                for side in range(2):
                    across = pl.ds(side * window + part * half, half)
                    keep(xh, xl, here, across, value[:, side * half : (side + 1) * half])

    even, odd = from_right(0, 0), from_right(window, 2)
    for first in range(0, window, size):
        near, beyond = even[first : first + size], odd[first : first + size]
        parity, place = first // half, first % half
        for side, value in enumerate((near + beyond, near - beyond)):
            for part in range(2):
                here = pl.ds((2 * parity + part) * half + place, size)
                keep(yh, yl, here, pl.ds(side * half, half), value[:, part * half : (part + 1) * half])
    far[pl.ds(0, window), :] = from_left(0, 0)
    far[pl.ds(window, window), :] = from_left(1, window)

    share = window // classes
    for flip in range(classes):
        base = pl.multiple_of((own ^ flip) * share, share)
        place = pl.multiple_of(lax.rem(base, half), share)
        sign = jnp.where(base < half, 1.0, -1.0)
        real, imag = (
            far[pl.ds(part * half + place, share), :] + sign * far[pl.ds(window + part * half + place, share), :]
            for part in range(2)
        )
        here = pl.ds(base, share)
        probe_real = probe[0, here, :]
        probe_imag = probe[1, here, :]
        outs[flip][pl.ds(0, share), :] = probe_real * real - probe_imag * imag
        outs[flip][pl.ds(share, share), :] = -(probe_real * imag + probe_imag * real)
        line = lax.broadcasted_iota(jnp.int32, (8, window), 0)
        outs[flip][pl.ds(2 * share, 8), :] = jnp.where(line == 0, row, column).astype(F32)


def wave(slot, window, classes, scalars, arrays):
    share = window // classes
    tiles = window // LANES
    scratch = [
        pltpu.VMEM(((window + 32) * 2 * tiles + 8, LANES), F32),
        pltpu.VMEM((2, window, window), F32),
        pltpu.VMEM((window, 2 * window), BF16),
        pltpu.VMEM((window, 2 * window), BF16),
        pltpu.VMEM((2 * window, window), BF16),
        pltpu.VMEM((2 * window, window), BF16),
        pltpu.VMEM((2 * window, window), F32),
        pltpu.VMEM((window, window), F32),
    ]
    return kernel_call(
        functools.partial(wave_kernel, slot, window, classes, len(arrays) == 5),
        [(2 * share + 8, window)] * classes,
        scalars,
        arrays,
        scratch,
        48 * window**3,
    )


def placed(piece, own, share, window):
    row = piece[pl.ds(2 * share, 1), :]
    column = piece[pl.ds(2 * share + 1, 1), :]
    place = (lax.broadcasted_iota(jnp.int32, (share, window), 0) + own * share).astype(F32)
    across = lax.broadcasted_iota(jnp.int32, (share, window), 1).astype(F32)
    return across < column, place < row, place + float(window) < row


def first_sum_kernel(window, classes, *refs):
    pieces, acc = refs[:classes], refs[classes]
    share = window // classes
    own = lax.rem(lax.axis_index("pos"), classes)
    for part in range(2):
        total = [[jnp.zeros((share, window), F32) for _ in range(2)] for _ in range(2)]
        for piece in pieces:
            upper, below, _ = placed(piece, own, share, window)
            value = piece[pl.ds(part * share, share), :]
            for k, wanted in enumerate((~below, below)):
                kept = jnp.where(wanted, value, 0.0)
                total[k][0] += jnp.where(upper, 0.0, kept)
                total[k][1] += jnp.where(upper, kept, 0.0)
        for k in range(2):
            for half in range(2):
                acc[k, part, :, pl.ds(half * window, window)] = total[k][half]


def second_sum_kernel(window, classes, acc, *refs):
    pieces, outs = refs[:classes], refs[classes:]
    share = window // classes
    tiles = window // LANES
    own = lax.rem(lax.axis_index("pos"), classes)
    for part in range(2):
        total = [[acc[k, part, :, pl.ds(h * window, window)] for h in range(2)] for k in range(2)]
        total.append([jnp.zeros((share, window), F32) for _ in range(2)])
        for piece in pieces:
            upper, below, lowest = placed(piece, own, share, window)
            value = piece[pl.ds(part * share, share), :]
            for k, wanted in enumerate((~below, below & ~lowest, lowest)):
                kept = jnp.where(wanted, value, 0.0)
                total[k][0] += jnp.where(upper, 0.0, kept)
                total[k][1] += jnp.where(upper, kept, 0.0)
        for k in range(3):
            for half in range(2):
                for tile in range(tiles):
                    outs[k][pl.ds((half * tiles + tile) * 2 + part, share, stride=4 * tiles), :] = total[k][half][
                        :, tile * LANES : (tile + 1) * LANES
                    ]


def on_device(object_field, illumination, amplitudes, row_offset, col_offset):
    band_rows, _, columns = object_field.shape
    window = illumination.shape[0]
    ways = lax.axis_size("pos")
    assert band_rows == 2 * window and columns == 2 * window and row_offset.shape[0] == 2
    classes = ways // 2
    share = window // classes
    tiles = window // LANES
    scalars = (row_offset, col_offset)

    remote = tuple(pltpu.with_memory_space_constraint(scalar, pltpu.HBM) for scalar in scalars)
    (wanted,) = kernel_call(functools.partial(pick_kernel, window), [(8, LANES)], remote, [])
    wanted = shifted(wanted, "tile", 1)
    obj, ill, amps, table = loaded([linear(object_field), linear(illumination), amplitudes, split_tables(window)])
    (rim,) = kernel_call(functools.partial(rim_kernel, window), [(2, window, window)], (), [wanted, obj])
    rim = shifted(rim, "tile", -1)

    def spread(pieces):
        moved = {d: exchanged(pieces[d], "pos", d) for d in reversed(range(1, classes))}
        return [pieces[0]] + [moved[d] for d in range(1, classes)]

    near = spread(wave(0, window, classes, scalars, [obj, ill, amps, table]))
    (acc,) = kernel_call(functools.partial(first_sum_kernel, window, classes), [(2, 2, share, columns)], (), near)
    late = spread(wave(1, window, classes, scalars, [obj, ill, amps, table, rim]))
    top, middle, spilled = kernel_call(
        functools.partial(second_sum_kernel, window, classes), [(share * 4 * tiles, LANES)] * 3, (), [acc, *late]
    )
    is_upper = lax.axis_index("pos") >= classes
    bands = range(lax.axis_size("tile"))
    arrived = 0.0
    for group in ((0, 3), (1, 2)):
        members = [band for band in bands if band % 4 in group]
        top = top + lax.ppermute(spilled, "tile", [(band - 1, band) for band in members if band > 0])
        outgoing = jnp.where(is_upper, top, middle)
        outgoing, spilled = lax.optimization_barrier((outgoing, spilled))
        route = [(band * ways + i, band * ways + (i ^ classes)) for band in members for i in range(ways)]
        arrived = arrived + lax.ppermute(outgoing, ("tile", "pos"), route)
    result = jnp.where(is_upper, middle, top) + arrived
    return unlinear(result, share, columns)


def solution(mesh):
    in_specs = (
        P("tile", None, None),
        P(),
        P(("tile", "pos"), None, None),
        P(("tile", "pos")),
        P(("tile", "pos")),
    )
    out_specs = P(("tile", "pos"), None, None)

    return jax.shard_map(on_device, mesh=mesh, in_specs=in_specs, out_specs=out_specs, check_vma=False)
```

```python
import functools
import math

import jax
import jax.numpy as jnp
import numpy as np
from jax import lax
from jax.experimental import pallas as pl
from jax.experimental.pallas import tpu as pltpu
from jax.sharding import PartitionSpec as P

LANES = 128
F32 = jnp.float32
BF16 = jnp.bfloat16


def shifted(block, axis, distance):
    devices = lax.axis_size(axis)
    return lax.ppermute(block, axis, [((i - distance) % devices, i) for i in range(devices)])


def exchanged(block, axis, flip):
    return lax.ppermute(block, axis, [(i, i ^ flip) for i in range(lax.axis_size(axis))])


def split_tables(length):
    half = length // 2
    n = np.arange(half, dtype=np.int64)
    even = 2 * n[:, None] * n[None, :]
    odd = n[:, None] * (2 * n[None, :] + 1)
    rows = []
    for product in (even, odd, odd.T):
        angles = (product % length) * (2.0 * math.pi / length)
        real, imag = np.cos(angles) / math.sqrt(length), -np.sin(angles) / math.sqrt(length)
        whole = np.concatenate([real, imag, -imag], axis=1)
        high = whole.astype(BF16)
        rows += [high, (whole - high.astype(np.float64)).astype(BF16)]
    return jnp.asarray(np.concatenate(rows, axis=0))


def linear(array):
    rows, parts, columns = array.shape
    tiles = columns // LANES
    return array.reshape(rows, parts, tiles, LANES).transpose(0, 2, 1, 3).reshape(rows * tiles * parts, LANES)


def unlinear(array, rows, columns):
    tiles = columns // LANES
    return array.reshape(rows, tiles, 2, LANES).transpose(0, 2, 1, 3).reshape(rows, 2, columns)


def halves(value):
    high = value.astype(BF16)
    return high, (value - high.astype(F32)).astype(BF16)


def dot3(high_left, low_left, high_right, low_right):
    left = jnp.concatenate([low_left, high_left, high_left], axis=1)
    right = jnp.concatenate([high_right, low_right, high_right], axis=0)
    return jnp.dot(left, right, preferred_element_type=F32)


def in_vmem(array):
    return pltpu.with_memory_space_constraint(array, pltpu.VMEM)


def kernel_call(body, name, out_shapes, scalars, arrays, scratch=(), flops=0):
    smem = pl.BlockSpec(memory_space=pltpu.SMEM)
    vmem = pl.BlockSpec(memory_space=pltpu.VMEM)
    moved = sum(4 * math.prod(shape) for shape in out_shapes)
    return pl.pallas_call(
        body,
        out_shape=[pltpu.VMEM(shape, F32) for shape in out_shapes],
        in_specs=[smem] * len(scalars) + [vmem] * len(arrays),
        out_specs=[vmem] * len(out_shapes),
        scratch_shapes=scratch,
        cost_estimate=pl.CostEstimate(flops=flops, transcendentals=0, bytes_accessed=2 * moved),
        compiler_params=pltpu.CompilerParams(vmem_limit_bytes=16 << 20),
        name=name,
    )(*scalars, *[in_vmem(array) for array in arrays])


def chosen(slot, rows, cols, band_start, window):
    crossing = (rows[0] - band_start > window).astype(jnp.int32)
    index = crossing if slot == 0 else 1 - crossing
    return rows[index] - band_start, cols[index], index


def load_kernel(number, *refs):
    sources, targets, sem = refs[:number], refs[number : 2 * number], refs[2 * number]
    copies = [pltpu.make_async_copy(a, b, sem.at[i]) for i, (a, b) in enumerate(zip(sources, targets))]
    for copy in copies:
        copy.start()
    for copy in copies:
        copy.wait()


def loaded(arrays):
    return pl.pallas_call(
        functools.partial(load_kernel, len(arrays)),
        out_shape=[pltpu.VMEM(array.shape, array.dtype) for array in arrays],
        in_specs=[pl.BlockSpec(memory_space=pl.ANY)] * len(arrays),
        out_specs=[pl.BlockSpec(memory_space=pltpu.VMEM)] * len(arrays),
        scratch_shapes=[pltpu.SemaphoreType.DMA((len(arrays),))],
        compiler_params=pltpu.CompilerParams(vmem_limit_bytes=16 << 20),
        name="load",
    )(*[pltpu.with_memory_space_constraint(array, pltpu.HBM) for array in arrays])


def pick_kernel(window, rows, cols, out):
    _, column, _ = chosen(1, rows, cols, lax.axis_index("tile") * (2 * window), window)
    out[...] = jnp.broadcast_to(column.astype(F32), out.shape)


def rim_kernel(window, wanted, obj, out):
    offset = wanted[pl.ds(0, 1), :]
    tiles = window // LANES
    for tile in range(tiles):
        column = (lax.broadcasted_iota(jnp.int32, (window, LANES), 1) + tile * LANES).astype(F32)
        for part in range(2):
            near = obj[pl.ds(tile * 2 + part, window, stride=4 * tiles), :]
            beyond = obj[pl.ds((tiles + tile) * 2 + part, window, stride=4 * tiles), :]
            out[part, :, pl.ds(tile * LANES, LANES)] = jnp.where(column < offset, beyond, near)


def wave_kernel(slot, window, classes, with_rim, rows, cols, obj, ill, amps, table, *refs):
    if with_rim:
        rim, refs = refs[0], refs[1:]
    outs, refs = refs[:classes], refs[classes:]
    doubled, probe, xh, xl, yh, yl, far, ordered = refs
    tiles = window // LANES
    half = window // 2
    row, column, index = chosen(slot, rows, cols, lax.axis_index("tile") * (2 * window), window)
    own = lax.rem(lax.axis_index("pos"), classes)
    size = 32
    step = 2 * tiles
    whole = window * step
    doubled[pl.ds(0, whole), :] = ill[...]
    doubled[pl.ds(whole, size * step), :] = ill[pl.ds(0, size * step), :]
    turn = lax.rem(row, window)

    below = lax.broadcasted_iota(jnp.int32, (window, window), 0)
    beside = lax.broadcasted_iota(jnp.int32, (window, window), 1)

    def picks(frequency, place):
        wanted = jnp.where(place < half, 2 * place, 2 * (place - half) + 1)
        return jnp.where(frequency == wanted, 1.0, 0.0).astype(BF16)

    by_column = jnp.dot(amps[index], picks(below, beside), preferred_element_type=F32).astype(BF16)
    ordered[...] = jnp.dot(picks(beside, below), by_column, preferred_element_type=F32)

    def block_of(matrix, part, low):
        return table[pl.ds((2 * matrix + low) * half, half), pl.ds(part * half, half)]

    def factor(matrix, order):
        return [
            jnp.concatenate(
                [
                    jnp.concatenate([block_of(matrix, part, low) for part in line], axis=1)
                    for line in order
                ],
                axis=0,
            )
            for low in range(2)
        ]

    def from_right(first, matrix):
        across = pl.ds(first, window)
        return dot3(xh[:, across], xl[:, across], *factor(matrix, ((0, 1), (2, 0))))

    def from_left(matrix, first):
        down = pl.ds(first, window)
        return dot3(*factor(matrix, ((0, 2), (1, 0))), yh[down, :], yl[down, :])

    def keep(high_ref, low_ref, here, across, value):
        high, low = halves(value)
        high_ref[here, across] = high
        low_ref[here, across] = low

    for first in range(0, window, size):
        place = lax.broadcasted_iota(jnp.int32, (size, window), 0) + first
        across = lax.broadcasted_iota(jnp.int32, (size, window), 1)
        start = lax.rem(first + window - turn, window) * step
        pair = []
        for part in range(2):
            rolled = jnp.concatenate(
                [doubled[pl.ds(start + tile * 2 + part, size, stride=step), :] for tile in range(tiles)],
                axis=1,
            )
            rolled = pltpu.roll(rolled, column, 1)
            probe[part, pl.ds(first, size), :] = rolled

            def block(base):
                def tile_at(tile):
                    return obj[pl.ds((base + first) * 2 * step + tile * 2 + part, size, stride=2 * step), :]

                near = jnp.concatenate([tile_at(t) for t in range(tiles)], axis=1)
                beyond = jnp.concatenate([tile_at(t + tiles) for t in range(tiles)], axis=1)
                return jnp.where(across < column, beyond, near)

            seen = jnp.where(place < row, block(window), block(0))
            if with_rim:
                seen = jnp.where(place + window < row, rim[part, pl.ds(first, size), :], seen)
            pair.append((rolled, seen))
        (probe_real, obj_real), (probe_imag, obj_imag) = pair
        exits = (
            probe_real * obj_real - probe_imag * obj_imag,
            probe_real * obj_imag + probe_imag * obj_real,
        )
        here = pl.ds(first, size)
        for part, value in enumerate(exits):
            left, right = value[:, :half], value[:, half:]
            keep(xh, xl, here, pl.ds(part * half, half), left + right)
            keep(xh, xl, here, pl.ds(window + part * half, half), left - right)

    for parity in range(2):
        mid = from_right(parity * window, parity)
        across = pl.ds(parity * half, half)
        for first in range(0, half, size):
            top, bottom = mid[first : first + size], mid[half + first : half + first + size]
            for line, value in enumerate((top + bottom, top - bottom)):
                for part in range(2):
                    here = pl.ds((2 * line + part) * half + first, size)
                    keep(yh, yl, here, across, value[:, part * half : (part + 1) * half])
    far[pl.ds(0, window), :] = from_left(0, 0)
    far[pl.ds(window, window), :] = from_left(2, window)

    for parity in range(2):
        for first in range(0, half, size):
            real = far[pl.ds(parity * window + first, size), :]
            imag = far[pl.ds(parity * window + half + first, size), :]
            here = pl.ds(parity * half + first, size)
            inverse = jnp.minimum(lax.rsqrt(real * real + imag * imag), 4.0)
            scaled = ordered[here, :] * inverse
            for part, value in enumerate((real * (1.0 - scaled), imag * (scaled - 1.0))):
                for side in range(2):
                    across = pl.ds(side * window + part * half, half)
                    keep(xh, xl, here, across, value[:, side * half : (side + 1) * half])

    even, odd = from_right(0, 0), from_right(window, 2)
    for first in range(0, window, size):
        near, beyond = even[first : first + size], odd[first : first + size]
        parity, place = first // half, first % half
        for side, value in enumerate((near + beyond, near - beyond)):
            for part in range(2):
                here = pl.ds((2 * parity + part) * half + place, size)
                keep(yh, yl, here, pl.ds(side * half, half), value[:, part * half : (part + 1) * half])
    far[pl.ds(0, window), :] = from_left(0, 0)
    far[pl.ds(window, window), :] = from_left(1, window)

    share = window // classes
    for flip in range(classes):
        base = pl.multiple_of((own ^ flip) * share, share)
        place = pl.multiple_of(lax.rem(base, half), share)
        sign = jnp.where(base < half, 1.0, -1.0)
        real, imag = (
            far[pl.ds(part * half + place, share), :] + sign * far[pl.ds(window + part * half + place, share), :]
            for part in range(2)
        )
        here = pl.ds(base, share)
        probe_real = probe[0, here, :]
        probe_imag = probe[1, here, :]
        outs[flip][pl.ds(0, share), :] = probe_real * real - probe_imag * imag
        outs[flip][pl.ds(share, share), :] = -(probe_real * imag + probe_imag * real)
        line = lax.broadcasted_iota(jnp.int32, (8, window), 0)
        outs[flip][pl.ds(2 * share, 8), :] = jnp.where(line == 0, row, column).astype(F32)


def wave(slot, window, classes, scalars, arrays):
    share = window // classes
    tiles = window // LANES
    scratch = [
        pltpu.VMEM(((window + 32) * 2 * tiles + 8, LANES), F32),
        pltpu.VMEM((2, window, window), F32),
        pltpu.VMEM((window, 2 * window), BF16),
        pltpu.VMEM((window, 2 * window), BF16),
        pltpu.VMEM((2 * window, window), BF16),
        pltpu.VMEM((2 * window, window), BF16),
        pltpu.VMEM((2 * window, window), F32),
        pltpu.VMEM((window, window), F32),
    ]
    return kernel_call(
        functools.partial(wave_kernel, slot, window, classes, len(arrays) == 5),
        "wave" + str(slot),
        [(2 * share + 8, window)] * classes,
        scalars,
        arrays,
        scratch,
        48 * window**3,
    )


def placed(piece, own, share, window):
    row = piece[pl.ds(2 * share, 1), :]
    column = piece[pl.ds(2 * share + 1, 1), :]
    place = (lax.broadcasted_iota(jnp.int32, (share, window), 0) + own * share).astype(F32)
    across = lax.broadcasted_iota(jnp.int32, (share, window), 1).astype(F32)
    return across < column, place < row, place + float(window) < row


def first_sum_kernel(window, classes, *refs):
    pieces, acc = refs[:classes], refs[classes]
    share = window // classes
    own = lax.rem(lax.axis_index("pos"), classes)
    for part in range(2):
        total = [[jnp.zeros((share, window), F32) for _ in range(2)] for _ in range(2)]
        for piece in pieces:
            upper, below, _ = placed(piece, own, share, window)
            value = piece[pl.ds(part * share, share), :]
            for k, wanted in enumerate((~below, below)):
                kept = jnp.where(wanted, value, 0.0)
                total[k][0] += jnp.where(upper, 0.0, kept)
                total[k][1] += jnp.where(upper, kept, 0.0)
        for k in range(2):
            for half in range(2):
                acc[k, part, :, pl.ds(half * window, window)] = total[k][half]


def second_sum_kernel(window, classes, acc, *refs):
    pieces, outs = refs[:classes], refs[classes:]
    share = window // classes
    tiles = window // LANES
    own = lax.rem(lax.axis_index("pos"), classes)
    for part in range(2):
        total = [[acc[k, part, :, pl.ds(h * window, window)] for h in range(2)] for k in range(2)]
        total.append([jnp.zeros((share, window), F32) for _ in range(2)])
        for piece in pieces:
            upper, below, lowest = placed(piece, own, share, window)
            value = piece[pl.ds(part * share, share), :]
            for k, wanted in enumerate((~below, below & ~lowest, lowest)):
                kept = jnp.where(wanted, value, 0.0)
                total[k][0] += jnp.where(upper, 0.0, kept)
                total[k][1] += jnp.where(upper, kept, 0.0)
        for k in range(3):
            for half in range(2):
                for tile in range(tiles):
                    outs[k][pl.ds((half * tiles + tile) * 2 + part, share, stride=4 * tiles), :] = total[k][half][
                        :, tile * LANES : (tile + 1) * LANES
                    ]


def on_device(object_field, illumination, amplitudes, row_offset, col_offset):
    band_rows, _, columns = object_field.shape
    window = illumination.shape[0]
    ways = lax.axis_size("pos")
    assert band_rows == 2 * window and columns == 2 * window and row_offset.shape[0] == 2
    classes = ways // 2
    share = window // classes
    tiles = window // LANES
    scalars = (row_offset, col_offset)

    remote = tuple(pltpu.with_memory_space_constraint(scalar, pltpu.HBM) for scalar in scalars)
    (wanted,) = kernel_call(functools.partial(pick_kernel, window), "pick", [(8, LANES)], remote, [])
    wanted = shifted(wanted, "tile", 1)
    obj, ill, amps, table = loaded([linear(object_field), linear(illumination), amplitudes, split_tables(window)])
    (rim,) = kernel_call(functools.partial(rim_kernel, window), "rim", [(2, window, window)], (), [wanted, obj])
    rim = shifted(rim, "tile", -1)

    def spread(pieces):
        moved = {d: exchanged(pieces[d], "pos", d) for d in reversed(range(1, classes))}
        return [pieces[0]] + [moved[d] for d in range(1, classes)]

    near = spread(wave(0, window, classes, scalars, [obj, ill, amps, table]))
    (acc,) = kernel_call(
        functools.partial(first_sum_kernel, window, classes), "sum0", [(2, 2, share, columns)], (), near
    )
    late = spread(wave(1, window, classes, scalars, [obj, ill, amps, table, rim]))
    top, middle, spilled = kernel_call(
        functools.partial(second_sum_kernel, window, classes),
        "sum1",
        [(share * 4 * tiles, LANES)] * 3,
        (),
        [acc, *late],
    )
    top = top + shifted(spilled, "tile", 1)
    is_upper = lax.axis_index("pos") >= classes
    received = exchanged(jnp.where(is_upper, top, middle), "pos", classes)
    result = jnp.where(is_upper, middle, top) + received
    return unlinear(result, share, columns)


def solution(mesh):
    in_specs = (
        P("tile", None, None),
        P(),
        P(("tile", "pos"), None, None),
        P(("tile", "pos")),
        P(("tile", "pos")),
    )
    out_specs = P(("tile", "pos"), None, None)
    return jax.shard_map(
        on_device, mesh=mesh, in_specs=in_specs, out_specs=out_specs, check_vma=False
    )
```

```python
import functools
import math

import jax
import jax.numpy as jnp
import numpy as np
from jax import lax
from jax.experimental import pallas as pl
from jax.experimental.pallas import tpu as pltpu
from jax.sharding import PartitionSpec as P

LANES = 128
F32 = jnp.float32
BF16 = jnp.bfloat16


def shifted(block, axis, distance):
    devices = lax.axis_size(axis)
    return lax.ppermute(block, axis, [((i - distance) % devices, i) for i in range(devices)])


def exchanged(block, axis, flip):
    return lax.ppermute(block, axis, [(i, i ^ flip) for i in range(lax.axis_size(axis))])


def split_tables(length):
    half = length // 2
    n = np.arange(half, dtype=np.int64)
    even = 2 * n[:, None] * n[None, :]
    odd = n[:, None] * (2 * n[None, :] + 1)
    rows = []
    for product in (even, odd, odd.T):
        angles = (product % length) * (2.0 * math.pi / length)
        real, imag = np.cos(angles) / math.sqrt(length), -np.sin(angles) / math.sqrt(length)
        whole = np.concatenate([real, imag, -imag], axis=1)
        high = whole.astype(BF16)
        rows += [high, (whole - high.astype(np.float64)).astype(BF16)]
    return jnp.asarray(np.concatenate(rows, axis=0))


def linear(array):
    rows, parts, columns = array.shape
    tiles = columns // LANES
    return array.reshape(rows, parts, tiles, LANES).transpose(0, 2, 1, 3).reshape(rows * tiles * parts, LANES)


def unlinear(array, rows, columns):
    tiles = columns // LANES
    return array.reshape(rows, tiles, 2, LANES).transpose(0, 2, 1, 3).reshape(rows, 2, columns)


def halves(value):
    high = value.astype(BF16)
    return high, (value - high.astype(F32)).astype(BF16)


def dot3(high_left, low_left, high_right, low_right):
    left = jnp.concatenate([low_left, high_left, high_left], axis=1)
    right = jnp.concatenate([high_right, low_right, high_right], axis=0)
    return jnp.dot(left, right, preferred_element_type=F32)


def in_vmem(array):
    return pltpu.with_memory_space_constraint(array, pltpu.VMEM)


def kernel_call(body, name, out_shapes, scalars, arrays, scratch=(), flops=0):
    smem = pl.BlockSpec(memory_space=pltpu.SMEM)
    vmem = pl.BlockSpec(memory_space=pltpu.VMEM)
    moved = sum(4 * math.prod(shape) for shape in out_shapes)
    return pl.pallas_call(
        body,
        out_shape=[pltpu.VMEM(shape, F32) for shape in out_shapes],
        in_specs=[smem] * len(scalars) + [vmem] * len(arrays),
        out_specs=[vmem] * len(out_shapes),
        scratch_shapes=scratch,
        cost_estimate=pl.CostEstimate(flops=flops, transcendentals=0, bytes_accessed=2 * moved),
        compiler_params=pltpu.CompilerParams(vmem_limit_bytes=16 << 20),
        name=name,
    )(*scalars, *[in_vmem(array) for array in arrays])


def chosen(slot, rows, cols, band_start, window):
    crossing = (rows[0] - band_start > window).astype(jnp.int32)
    index = crossing if slot == 0 else 1 - crossing
    return rows[index] - band_start, cols[index], index


def load_kernel(window, number, rows, cols, *refs):
    sources, targets = refs[:number], refs[number : 2 * number]
    wanted, sem = refs[2 * number :]
    copies = [pltpu.make_async_copy(a, b, sem.at[i]) for i, (a, b) in enumerate(zip(sources, targets))]
    for copy in copies:
        copy.start()
    _, column, _ = chosen(1, rows, cols, lax.axis_index("tile") * (2 * window), window)
    wanted[...] = jnp.broadcast_to(column.astype(F32), wanted.shape)
    for copy in copies:
        copy.wait()


def loaded(window, scalars, arrays):
    smem = pl.BlockSpec(memory_space=pltpu.SMEM)
    vmem = pl.BlockSpec(memory_space=pltpu.VMEM)
    return pl.pallas_call(
        functools.partial(load_kernel, window, len(arrays)),
        out_shape=[pltpu.VMEM(array.shape, array.dtype) for array in arrays] + [pltpu.VMEM((8, LANES), F32)],
        in_specs=[smem] * len(scalars) + [pl.BlockSpec(memory_space=pl.ANY)] * len(arrays),
        out_specs=[vmem] * (len(arrays) + 1),
        scratch_shapes=[pltpu.SemaphoreType.DMA((len(arrays),))],
        compiler_params=pltpu.CompilerParams(vmem_limit_bytes=16 << 20),
        name="load",
    )(*[pltpu.with_memory_space_constraint(array, pltpu.HBM) for array in (*scalars, *arrays)])


def rim_kernel(window, wanted, obj, out):
    offset = wanted[pl.ds(0, 1), :]
    tiles = window // LANES
    for tile in range(tiles):
        column = (lax.broadcasted_iota(jnp.int32, (window, LANES), 1) + tile * LANES).astype(F32)
        for part in range(2):
            near = obj[pl.ds(tile * 2 + part, window, stride=4 * tiles), :]
            beyond = obj[pl.ds((tiles + tile) * 2 + part, window, stride=4 * tiles), :]
            out[part, :, pl.ds(tile * LANES, LANES)] = jnp.where(column < offset, beyond, near)


def wave_kernel(slot, window, classes, with_rim, rows, cols, obj, ill, amps, table, *refs):
    if with_rim:
        rim, refs = refs[0], refs[1:]
    outs, refs = refs[:classes], refs[classes:]
    doubled, probe, xh, xl, yh, yl, far, ordered = refs
    tiles = window // LANES
    half = window // 2
    row, column, index = chosen(slot, rows, cols, lax.axis_index("tile") * (2 * window), window)
    own = lax.rem(lax.axis_index("pos"), classes)
    size = 32
    step = 2 * tiles
    whole = window * step
    doubled[pl.ds(0, whole), :] = ill[...]
    doubled[pl.ds(whole, size * step), :] = ill[pl.ds(0, size * step), :]
    turn = lax.rem(row, window)

    below = lax.broadcasted_iota(jnp.int32, (window, window), 0)
    beside = lax.broadcasted_iota(jnp.int32, (window, window), 1)

    def picks(frequency, place):
        wanted = jnp.where(place < half, 2 * place, 2 * (place - half) + 1)
        return jnp.where(frequency == wanted, 1.0, 0.0).astype(BF16)

    by_column = jnp.dot(amps[index], picks(below, beside), preferred_element_type=F32).astype(BF16)
    ordered[...] = jnp.dot(picks(beside, below), by_column, preferred_element_type=F32)

    def block_of(matrix, part, low):
        return table[pl.ds((2 * matrix + low) * half, half), pl.ds(part * half, half)]

    def factor(matrix, order):
        return [
            jnp.concatenate(
                [
                    jnp.concatenate([block_of(matrix, part, low) for part in line], axis=1)
                    for line in order
                ],
                axis=0,
            )
            for low in range(2)
        ]

    def from_right(first, matrix):
        across = pl.ds(first, window)
        return dot3(xh[:, across], xl[:, across], *factor(matrix, ((0, 1), (2, 0))))

    def from_left(matrix, first):
        down = pl.ds(first, window)
        return dot3(*factor(matrix, ((0, 2), (1, 0))), yh[down, :], yl[down, :])

    def keep(high_ref, low_ref, here, across, value):
        high, low = halves(value)
        high_ref[here, across] = high
        low_ref[here, across] = low

    for first in range(0, window, size):
        place = lax.broadcasted_iota(jnp.int32, (size, window), 0) + first
        across = lax.broadcasted_iota(jnp.int32, (size, window), 1)
        start = lax.rem(first + window - turn, window) * step
        pair = []
        for part in range(2):
            rolled = jnp.concatenate(
                [doubled[pl.ds(start + tile * 2 + part, size, stride=step), :] for tile in range(tiles)],
                axis=1,
            )
            rolled = pltpu.roll(rolled, column, 1)
            probe[part, pl.ds(first, size), :] = rolled

            def block(base):
                def tile_at(tile):
                    return obj[pl.ds((base + first) * 2 * step + tile * 2 + part, size, stride=2 * step), :]

                near = jnp.concatenate([tile_at(t) for t in range(tiles)], axis=1)
                beyond = jnp.concatenate([tile_at(t + tiles) for t in range(tiles)], axis=1)
                return jnp.where(across < column, beyond, near)

            seen = jnp.where(place < row, block(window), block(0))
            if with_rim:
                seen = jnp.where(place + window < row, rim[part, pl.ds(first, size), :], seen)
            pair.append((rolled, seen))
        (probe_real, obj_real), (probe_imag, obj_imag) = pair
        exits = (
            probe_real * obj_real - probe_imag * obj_imag,
            probe_real * obj_imag + probe_imag * obj_real,
        )
        here = pl.ds(first, size)
        for part, value in enumerate(exits):
            left, right = value[:, :half], value[:, half:]
            keep(xh, xl, here, pl.ds(part * half, half), left + right)
            keep(xh, xl, here, pl.ds(window + part * half, half), left - right)

    for parity in range(2):
        mid = from_right(parity * window, parity)
        across = pl.ds(parity * half, half)
        for first in range(0, half, size):
            top, bottom = mid[first : first + size], mid[half + first : half + first + size]
            for line, value in enumerate((top + bottom, top - bottom)):
                for part in range(2):
                    here = pl.ds((2 * line + part) * half + first, size)
                    keep(yh, yl, here, across, value[:, part * half : (part + 1) * half])
    far[pl.ds(0, window), :] = from_left(0, 0)
    far[pl.ds(window, window), :] = from_left(2, window)

    for parity in range(2):
        for first in range(0, half, size):
            real = far[pl.ds(parity * window + first, size), :]
            imag = far[pl.ds(parity * window + half + first, size), :]
            here = pl.ds(parity * half + first, size)
            inverse = jnp.minimum(lax.rsqrt(real * real + imag * imag), 4.0)
            scaled = ordered[here, :] * inverse
            for part, value in enumerate((real * (1.0 - scaled), imag * (scaled - 1.0))):
                for side in range(2):
                    across = pl.ds(side * window + part * half, half)
                    keep(xh, xl, here, across, value[:, side * half : (side + 1) * half])

    even, odd = from_right(0, 0), from_right(window, 2)
    for first in range(0, window, size):
        near, beyond = even[first : first + size], odd[first : first + size]
        parity, place = first // half, first % half
        for side, value in enumerate((near + beyond, near - beyond)):
            for part in range(2):
                here = pl.ds((2 * parity + part) * half + place, size)
                keep(yh, yl, here, pl.ds(side * half, half), value[:, part * half : (part + 1) * half])
    far[pl.ds(0, window), :] = from_left(0, 0)
    far[pl.ds(window, window), :] = from_left(1, window)

    share = window // classes
    for flip in range(classes):
        base = pl.multiple_of((own ^ flip) * share, share)
        place = pl.multiple_of(lax.rem(base, half), share)
        sign = jnp.where(base < half, 1.0, -1.0)
        real, imag = (
            far[pl.ds(part * half + place, share), :] + sign * far[pl.ds(window + part * half + place, share), :]
            for part in range(2)
        )
        here = pl.ds(base, share)
        probe_real = probe[0, here, :]
        probe_imag = probe[1, here, :]
        outs[flip][pl.ds(0, share), :] = probe_real * real - probe_imag * imag
        outs[flip][pl.ds(share, share), :] = -(probe_real * imag + probe_imag * real)
        line = lax.broadcasted_iota(jnp.int32, (8, window), 0)
        outs[flip][pl.ds(2 * share, 8), :] = jnp.where(line == 0, row, column).astype(F32)


def wave(slot, window, classes, scalars, arrays):
    share = window // classes
    tiles = window // LANES
    scratch = [
        pltpu.VMEM(((window + 32) * 2 * tiles + 8, LANES), F32),
        pltpu.VMEM((2, window, window), F32),
        pltpu.VMEM((window, 2 * window), BF16),
        pltpu.VMEM((window, 2 * window), BF16),
        pltpu.VMEM((2 * window, window), BF16),
        pltpu.VMEM((2 * window, window), BF16),
        pltpu.VMEM((2 * window, window), F32),
        pltpu.VMEM((window, window), F32),
    ]
    return kernel_call(
        functools.partial(wave_kernel, slot, window, classes, len(arrays) == 5),
        "wave" + str(slot),
        [(2 * share + 8, window)] * classes,
        scalars,
        arrays,
        scratch,
        48 * window**3,
    )


def placed(piece, own, share, window):
    row = piece[pl.ds(2 * share, 1), :]
    column = piece[pl.ds(2 * share + 1, 1), :]
    place = (lax.broadcasted_iota(jnp.int32, (share, window), 0) + own * share).astype(F32)
    across = lax.broadcasted_iota(jnp.int32, (share, window), 1).astype(F32)
    return across < column, place < row, place + float(window) < row


def first_sum_kernel(window, classes, *refs):
    pieces, acc = refs[:classes], refs[classes]
    share = window // classes
    own = lax.rem(lax.axis_index("pos"), classes)
    for part in range(2):
        total = [[jnp.zeros((share, window), F32) for _ in range(2)] for _ in range(2)]
        for piece in pieces:
            upper, below, _ = placed(piece, own, share, window)
            value = piece[pl.ds(part * share, share), :]
            for k, wanted in enumerate((~below, below)):
                kept = jnp.where(wanted, value, 0.0)
                total[k][0] += jnp.where(upper, 0.0, kept)
                total[k][1] += jnp.where(upper, kept, 0.0)
        for k in range(2):
            for half in range(2):
                acc[k, part, :, pl.ds(half * window, window)] = total[k][half]


def second_sum_kernel(window, classes, acc, *refs):
    pieces, outs = refs[:classes], refs[classes:]
    share = window // classes
    tiles = window // LANES
    own = lax.rem(lax.axis_index("pos"), classes)
    for part in range(2):
        total = [[acc[k, part, :, pl.ds(h * window, window)] for h in range(2)] for k in range(2)]
        total.append([jnp.zeros((share, window), F32) for _ in range(2)])
        for piece in pieces:
            upper, below, lowest = placed(piece, own, share, window)
            value = piece[pl.ds(part * share, share), :]
            for k, wanted in enumerate((~below, below & ~lowest, lowest)):
                kept = jnp.where(wanted, value, 0.0)
                total[k][0] += jnp.where(upper, 0.0, kept)
                total[k][1] += jnp.where(upper, kept, 0.0)
        for k in range(3):
            for half in range(2):
                for tile in range(tiles):
                    outs[3 * tile + k][pl.ds((half * 2 + part) * share, share), :] = total[k][half][
                        :, tile * LANES : (tile + 1) * LANES
                    ]


def final_kernel(tiles, share, *refs):
    kept, received, out = refs[:tiles], refs[tiles : 2 * tiles], refs[2 * tiles]
    for tile in range(tiles):
        for half in range(2):
            for part in range(2):
                here = pl.ds((half * 2 + part) * share, share)
                line = (half * tiles + tile) * 2 + part
                out[pl.ds(line, share, stride=4 * tiles), :] = kept[tile][here, :] + received[tile][here, :]


def on_device(object_field, illumination, amplitudes, row_offset, col_offset):
    band_rows, _, columns = object_field.shape
    window = illumination.shape[0]
    ways = lax.axis_size("pos")
    assert band_rows == 2 * window and columns == 2 * window and row_offset.shape[0] == 2
    classes = ways // 2
    share = window // classes
    tiles = window // LANES
    scalars = (row_offset, col_offset)

    arrays = [linear(object_field), linear(illumination), amplitudes, split_tables(window)]
    obj, ill, amps, table, wanted = loaded(window, scalars, arrays)
    wanted = shifted(wanted, "tile", 1)
    (rim,) = kernel_call(functools.partial(rim_kernel, window), "rim", [(2, window, window)], (), [wanted, obj])
    rim = shifted(rim, "tile", -1)

    def spread(pieces):
        moved = {d: exchanged(pieces[d], "pos", d) for d in reversed(range(1, classes))}
        return [pieces[0]] + [moved[d] for d in range(1, classes)]

    near = spread(wave(0, window, classes, scalars, [obj, ill, amps, table]))
    (acc,) = kernel_call(
        functools.partial(first_sum_kernel, window, classes), "sum0", [(2, 2, share, columns)], (), near
    )
    late = spread(wave(1, window, classes, scalars, [obj, ill, amps, table, rim]))
    sums = kernel_call(
        functools.partial(second_sum_kernel, window, classes),
        "sum1",
        [(4 * share, LANES)] * (3 * tiles),
        (),
        [acc, *late],
    )
    is_upper = lax.axis_index("pos") >= classes
    kept, received = [], []
    for chunk in range(tiles):
        top, middle, spilled = sums[3 * chunk : 3 * chunk + 3]
        with jax.named_scope("spill_" + str(chunk)):
            top = top + shifted(spilled, "tile", 1)
        outgoing = jnp.where(is_upper, top, middle)
        with jax.named_scope("halves_" + str(chunk)):
            received.append(exchanged(outgoing, "pos", classes))
        kept.append(jnp.where(is_upper, middle, top))
    result = pl.pallas_call(
        functools.partial(final_kernel, tiles, share),
        out_shape=jax.ShapeDtypeStruct((share * 4 * tiles, LANES), F32),
        in_specs=[pl.BlockSpec(memory_space=pltpu.VMEM)] * (2 * tiles),
        out_specs=pl.BlockSpec(memory_space=pltpu.VMEM),
        compiler_params=pltpu.CompilerParams(vmem_limit_bytes=16 << 20),
        name="final",
    )(*[in_vmem(array) for array in kept + received])
    return unlinear(result, share, columns)


def solution(mesh):
    in_specs = (
        P("tile", None, None),
        P(),
        P(("tile", "pos"), None, None),
        P(("tile", "pos")),
        P(("tile", "pos")),
    )
    out_specs = P(("tile", "pos"), None, None)
    return jax.shard_map(
        on_device, mesh=mesh, in_specs=in_specs, out_specs=out_specs, check_vma=False
    )
```

```python
import functools
import math

import jax
import jax.numpy as jnp
import numpy as np
from jax import lax
from jax.experimental import pallas as pl
from jax.experimental.pallas import tpu as pltpu
from jax.sharding import PartitionSpec as P

LANES = 128
F32 = jnp.float32
BF16 = jnp.bfloat16


def shifted(block, axis, distance):
    devices = lax.axis_size(axis)
    return lax.ppermute(block, axis, [((i - distance) % devices, i) for i in range(devices)])


def exchanged(block, axis, flip):
    return lax.ppermute(block, axis, [(i, i ^ flip) for i in range(lax.axis_size(axis))])


def split_tables(length):
    half = length // 2
    n = np.arange(half, dtype=np.int64)
    even = 2 * n[:, None] * n[None, :]
    odd = n[:, None] * (2 * n[None, :] + 1)
    rows = []
    for product in (even, odd, odd.T):
        angles = (product % length) * (2.0 * math.pi / length)
        real, imag = np.cos(angles) / math.sqrt(length), -np.sin(angles) / math.sqrt(length)
        whole = np.concatenate([real, imag, -imag], axis=1)
        high = whole.astype(BF16)
        rows += [high, (whole - high.astype(np.float64)).astype(BF16)]
    return jnp.asarray(np.concatenate(rows, axis=0))


def linear(array):
    rows, parts, columns = array.shape
    tiles = columns // LANES
    return array.reshape(rows, parts, tiles, LANES).transpose(0, 2, 1, 3).reshape(rows * tiles * parts, LANES)


def unlinear(array, rows, columns):
    tiles = columns // LANES
    return array.reshape(rows, tiles, 2, LANES).transpose(0, 2, 1, 3).reshape(rows, 2, columns)


def halves(value):
    high = value.astype(BF16)
    return high, (value - high.astype(F32)).astype(BF16)


def dot3(high_left, low_left, high_right, low_right):
    left = jnp.concatenate([low_left, high_left, high_left], axis=1)
    right = jnp.concatenate([high_right, low_right, high_right], axis=0)
    return jnp.dot(left, right, preferred_element_type=F32)


def in_vmem(array):
    return pltpu.with_memory_space_constraint(array, pltpu.VMEM)


def kernel_call(body, name, out_shapes, scalars, arrays, scratch=(), flops=0):
    smem = pl.BlockSpec(memory_space=pltpu.SMEM)
    vmem = pl.BlockSpec(memory_space=pltpu.VMEM)
    moved = sum(4 * math.prod(shape) for shape in out_shapes)
    return pl.pallas_call(
        body,
        out_shape=[pltpu.VMEM(shape, F32) for shape in out_shapes],
        in_specs=[smem] * len(scalars) + [vmem] * len(arrays),
        out_specs=[vmem] * len(out_shapes),
        scratch_shapes=scratch,
        cost_estimate=pl.CostEstimate(flops=flops, transcendentals=0, bytes_accessed=2 * moved),
        compiler_params=pltpu.CompilerParams(vmem_limit_bytes=16 << 20),
        name=name,
    )(*scalars, *[in_vmem(array) for array in arrays])


def chosen(slot, rows, cols, band_start, window):
    crossing = (rows[0] - band_start > window).astype(jnp.int32)
    index = crossing if slot == 0 else 1 - crossing
    return rows[index] - band_start, cols[index], index


def load_kernel(number, *refs):
    sources, targets, sem = refs[:number], refs[number : 2 * number], refs[2 * number]
    copies = [pltpu.make_async_copy(a, b, sem.at[i]) for i, (a, b) in enumerate(zip(sources, targets))]
    for copy in copies:
        copy.start()
    for copy in copies:
        copy.wait()


def loaded(arrays):
    return pl.pallas_call(
        functools.partial(load_kernel, len(arrays)),
        out_shape=[pltpu.VMEM(array.shape, array.dtype) for array in arrays],
        in_specs=[pl.BlockSpec(memory_space=pl.ANY)] * len(arrays),
        out_specs=[pl.BlockSpec(memory_space=pltpu.VMEM)] * len(arrays),
        scratch_shapes=[pltpu.SemaphoreType.DMA((len(arrays),))],
        compiler_params=pltpu.CompilerParams(vmem_limit_bytes=16 << 20),
        name="load",
    )(*[pltpu.with_memory_space_constraint(array, pltpu.HBM) for array in arrays])


def pick_kernel(window, rows, cols, out):
    _, column, _ = chosen(1, rows, cols, lax.axis_index("tile") * (2 * window), window)
    out[...] = jnp.broadcast_to(column.astype(F32), out.shape)


def rim_kernel(window, wanted, obj, out):
    offset = wanted[pl.ds(0, 1), :]
    tiles = window // LANES
    for tile in range(tiles):
        column = (lax.broadcasted_iota(jnp.int32, (window, LANES), 1) + tile * LANES).astype(F32)
        for part in range(2):
            near = obj[pl.ds(tile * 2 + part, window, stride=4 * tiles), :]
            beyond = obj[pl.ds((tiles + tile) * 2 + part, window, stride=4 * tiles), :]
            out[part, :, pl.ds(tile * LANES, LANES)] = jnp.where(column < offset, beyond, near)


def prepare(slot, window, rows, cols, obj, ill, amps, doubled, probe, ordered, emit):
    tiles = window // LANES
    half = window // 2
    row, column, index = chosen(slot, rows, cols, lax.axis_index("tile") * (2 * window), window)
    size = 32
    step = 2 * tiles
    whole = window * step
    doubled[pl.ds(0, whole), :] = ill[...]
    doubled[pl.ds(whole, size * step), :] = ill[pl.ds(0, size * step), :]
    turn = lax.rem(row, window)

    below = lax.broadcasted_iota(jnp.int32, (window, window), 0)
    beside = lax.broadcasted_iota(jnp.int32, (window, window), 1)

    def picks(frequency, place):
        wanted = jnp.where(place < half, 2 * place, 2 * (place - half) + 1)
        return jnp.where(frequency == wanted, 1.0, 0.0).astype(BF16)

    by_column = jnp.dot(amps[index], picks(below, beside), preferred_element_type=F32).astype(BF16)
    ordered[...] = jnp.dot(picks(beside, below), by_column, preferred_element_type=F32)

    for first in range(0, window, size):
        place = lax.broadcasted_iota(jnp.int32, (size, window), 0) + first
        across = lax.broadcasted_iota(jnp.int32, (size, window), 1)
        start = lax.rem(first + window - turn, window) * step
        pair = []
        for part in range(2):
            rolled = jnp.concatenate(
                [doubled[pl.ds(start + tile * 2 + part, size, stride=step), :] for tile in range(tiles)],
                axis=1,
            )
            rolled = pltpu.roll(rolled, column, 1)
            probe[part, pl.ds(first, size), :] = rolled

            def block(base):
                def tile_at(tile):
                    return obj[pl.ds((base + first) * 2 * step + tile * 2 + part, size, stride=2 * step), :]

                near = jnp.concatenate([tile_at(t) for t in range(tiles)], axis=1)
                beyond = jnp.concatenate([tile_at(t + tiles) for t in range(tiles)], axis=1)
                return jnp.where(across < column, beyond, near)

            pair.append((rolled, jnp.where(place < row, block(window), block(0))))
        emit(first, size, product(*pair))


def product(real_pair, imag_pair):
    (probe_real, obj_real), (probe_imag, obj_imag) = real_pair, imag_pair
    return (
        probe_real * obj_real - probe_imag * obj_imag,
        probe_real * obj_imag + probe_imag * obj_real,
    )


def keep(high_ref, low_ref, here, across, value):
    high, low = halves(value)
    high_ref[here, across] = high
    low_ref[here, across] = low


def keep_exit(xh, xl, first, size, exits):
    here = pl.ds(first, size)
    window = exits[0].shape[1]
    half = window // 2
    for part, value in enumerate(exits):
        left, right = value[:, :half], value[:, half:]
        keep(xh, xl, here, pl.ds(part * half, half), left + right)
        keep(xh, xl, here, pl.ds(window + part * half, half), left - right)


def transforms(window, classes, table, probe, ordered, xh, xl, yh, yl, far, outs):
    half = window // 2
    own = lax.rem(lax.axis_index("pos"), classes)
    size = 32

    def block_of(matrix, part, low):
        return table[pl.ds((2 * matrix + low) * half, half), pl.ds(part * half, half)]

    def factor(matrix, order):
        return [
            jnp.concatenate(
                [
                    jnp.concatenate([block_of(matrix, part, low) for part in line], axis=1)
                    for line in order
                ],
                axis=0,
            )
            for low in range(2)
        ]

    def from_right(first, matrix):
        across = pl.ds(first, window)
        return dot3(xh[:, across], xl[:, across], *factor(matrix, ((0, 1), (2, 0))))

    def from_left(matrix, first):
        down = pl.ds(first, window)
        return dot3(*factor(matrix, ((0, 2), (1, 0))), yh[down, :], yl[down, :])

    for parity in range(2):
        mid = from_right(parity * window, parity)
        across = pl.ds(parity * half, half)
        for first in range(0, half, size):
            top, bottom = mid[first : first + size], mid[half + first : half + first + size]
            for line, value in enumerate((top + bottom, top - bottom)):
                for part in range(2):
                    here = pl.ds((2 * line + part) * half + first, size)
                    keep(yh, yl, here, across, value[:, part * half : (part + 1) * half])
    far[pl.ds(0, window), :] = from_left(0, 0)
    far[pl.ds(window, window), :] = from_left(2, window)

    for parity in range(2):
        for first in range(0, half, size):
            real = far[pl.ds(parity * window + first, size), :]
            imag = far[pl.ds(parity * window + half + first, size), :]
            here = pl.ds(parity * half + first, size)
            inverse = jnp.minimum(lax.rsqrt(real * real + imag * imag), 4.0)
            scaled = ordered[here, :] * inverse
            for part, value in enumerate((real * (1.0 - scaled), imag * (scaled - 1.0))):
                for side in range(2):
                    across = pl.ds(side * window + part * half, half)
                    keep(xh, xl, here, across, value[:, side * half : (side + 1) * half])

    even, odd = from_right(0, 0), from_right(window, 2)
    for first in range(0, window, size):
        near, beyond = even[first : first + size], odd[first : first + size]
        parity, place = first // half, first % half
        for side, value in enumerate((near + beyond, near - beyond)):
            for part in range(2):
                here = pl.ds((2 * parity + part) * half + place, size)
                keep(yh, yl, here, pl.ds(side * half, half), value[:, part * half : (part + 1) * half])
    far[pl.ds(0, window), :] = from_left(0, 0)
    far[pl.ds(window, window), :] = from_left(1, window)

    share = window // classes
    for flip in range(classes):
        base = pl.multiple_of((own ^ flip) * share, share)
        place = pl.multiple_of(lax.rem(base, half), share)
        sign = jnp.where(base < half, 1.0, -1.0)
        real, imag = (
            far[pl.ds(part * half + place, share), :] + sign * far[pl.ds(window + part * half + place, share), :]
            for part in range(2)
        )
        here = pl.ds(base, share)
        probe_real = probe[0, here, :]
        probe_imag = probe[1, here, :]
        outs[flip][pl.ds(0, share), :] = probe_real * real - probe_imag * imag
        outs[flip][pl.ds(share, share), :] = -(probe_real * imag + probe_imag * real)


def first_wave_kernel(window, classes, rows, cols, obj, ill, amps, table, *refs):
    outs = refs[:classes]
    doubled, probe, ordered, xh, xl, yh, yl, far = refs[classes:]
    emit = functools.partial(keep_exit, xh, xl)
    prepare(0, window, rows, cols, obj, ill, amps, doubled, probe, ordered, emit)
    transforms(window, classes, table, probe, ordered, xh, xl, yh, yl, far, outs)
    share = window // classes
    line = lax.broadcasted_iota(jnp.int32, (8, window), 0)
    head = jnp.zeros((8, window), jnp.int32)
    for slot in range(2):
        row, column, _ = chosen(slot, rows, cols, lax.axis_index("tile") * (2 * window), window)
        head = jnp.where(line == 2 * slot, row, jnp.where(line == 2 * slot + 1, column, head))
    for out in outs:
        out[pl.ds(2 * share, 8), :] = head.astype(F32)


def second_start_kernel(window, rows, cols, obj, ill, amps, probe, ordered, exits, doubled):
    def emit(first, size, values):
        for part in range(2):
            exits[part, pl.ds(first, size), :] = values[part]

    prepare(1, window, rows, cols, obj, ill, amps, doubled, probe, ordered, emit)


def second_wave_kernel(window, classes, rows, cols, probe, ordered, exits, table, rim, *refs):
    outs = refs[:classes]
    xh, xl, yh, yl, far = refs[classes:]
    row, _, _ = chosen(1, rows, cols, lax.axis_index("tile") * (2 * window), window)
    size = 32
    for first in range(0, window, size):
        here = pl.ds(first, size)
        beyond = lax.broadcasted_iota(jnp.int32, (size, window), 0) + (first + window) < row
        edge = product(*[(probe[part, here, :], rim[part, here, :]) for part in range(2)])
        values = [jnp.where(beyond, edge[part], exits[part, here, :]) for part in range(2)]
        keep_exit(xh, xl, first, size, values)
    transforms(window, classes, table, probe, ordered, xh, xl, yh, yl, far, outs)


def scratch_of(window):
    tiles = window // LANES
    roll = [pltpu.VMEM(((window + 32) * 2 * tiles + 8, LANES), F32)]
    state = [pltpu.VMEM((2, window, window), F32), pltpu.VMEM((window, window), F32)]
    work = [
        pltpu.VMEM((window, 2 * window), BF16),
        pltpu.VMEM((window, 2 * window), BF16),
        pltpu.VMEM((2 * window, window), BF16),
        pltpu.VMEM((2 * window, window), BF16),
        pltpu.VMEM((2 * window, window), F32),
    ]
    return roll, state, work


def placed(slot, piece, own, share, window):
    row = piece[pl.ds(2 * share + 2 * slot, 1), :]
    column = piece[pl.ds(2 * share + 2 * slot + 1, 1), :]
    place = (lax.broadcasted_iota(jnp.int32, (share, window), 0) + own * share).astype(F32)
    across = lax.broadcasted_iota(jnp.int32, (share, window), 1).astype(F32)
    return across < column, place < row, place + float(window) < row


def first_sum_kernel(window, classes, *refs):
    pieces, acc = refs[:classes], refs[classes]
    share = window // classes
    own = lax.rem(lax.axis_index("pos"), classes)
    for part in range(2):
        total = [[jnp.zeros((share, window), F32) for _ in range(2)] for _ in range(2)]
        for piece in pieces:
            upper, below, _ = placed(0, piece, own, share, window)
            value = piece[pl.ds(part * share, share), :]
            for k, wanted in enumerate((~below, below)):
                kept = jnp.where(wanted, value, 0.0)
                total[k][0] += jnp.where(upper, 0.0, kept)
                total[k][1] += jnp.where(upper, kept, 0.0)
        for k in range(2):
            for half in range(2):
                acc[k, part, :, pl.ds(half * window, window)] = total[k][half]


def second_sum_kernel(window, classes, acc, *refs):
    heads, pieces, outs = refs[:classes], refs[classes : 2 * classes], refs[2 * classes :]
    share = window // classes
    tiles = window // LANES
    own = lax.rem(lax.axis_index("pos"), classes)
    for part in range(2):
        total = [[acc[k, part, :, pl.ds(h * window, window)] for h in range(2)] for k in range(2)]
        total.append([jnp.zeros((share, window), F32) for _ in range(2)])
        for head, piece in zip(heads, pieces):
            upper, below, lowest = placed(1, head, own, share, window)
            value = piece[pl.ds(part * share, share), :]
            for k, wanted in enumerate((~below, below & ~lowest, lowest)):
                kept = jnp.where(wanted, value, 0.0)
                total[k][0] += jnp.where(upper, 0.0, kept)
                total[k][1] += jnp.where(upper, kept, 0.0)
        for k in range(3):
            for half in range(2):
                for tile in range(tiles):
                    outs[3 * tile + k][pl.ds((half * 2 + part) * share, share), :] = total[k][half][
                        :, tile * LANES : (tile + 1) * LANES
                    ]


def final_kernel(tiles, share, *refs):
    kept, received, out = refs[:tiles], refs[tiles : 2 * tiles], refs[2 * tiles]
    for tile in range(tiles):
        for half in range(2):
            for part in range(2):
                here = pl.ds((half * 2 + part) * share, share)
                line = (half * tiles + tile) * 2 + part
                out[pl.ds(line, share, stride=4 * tiles), :] = kept[tile][here, :] + received[tile][here, :]


def on_device(object_field, illumination, amplitudes, row_offset, col_offset):
    band_rows, _, columns = object_field.shape
    window = illumination.shape[0]
    ways = lax.axis_size("pos")
    assert band_rows == 2 * window and columns == 2 * window and row_offset.shape[0] == 2
    classes = ways // 2
    share = window // classes
    tiles = window // LANES
    scalars = (row_offset, col_offset)

    arrays = [linear(object_field), linear(illumination), amplitudes, split_tables(window)]
    remote = tuple(pltpu.with_memory_space_constraint(scalar, pltpu.HBM) for scalar in scalars)
    (wanted,) = kernel_call(functools.partial(pick_kernel, window), "pick", [(8, LANES)], remote, [])
    wanted = shifted(wanted, "tile", 1)
    obj, ill, amps, table = loaded(arrays)
    (rim,) = kernel_call(functools.partial(rim_kernel, window), "rim", [(2, window, window)], (), [wanted, obj])
    rim = shifted(rim, "tile", -1)

    def spread(pieces):
        moved = {d: exchanged(pieces[d], "pos", d) for d in reversed(range(1, classes))}
        return [pieces[0]] + [moved[d] for d in range(1, classes)]

    roll, state, work = scratch_of(window)
    near = spread(
        kernel_call(
            functools.partial(first_wave_kernel, window, classes),
            "wave0",
            [(2 * share + 8, window)] * classes,
            scalars,
            [obj, ill, amps, table],
            roll + state + work,
            48 * window**3,
        )
    )
    with jax.named_scope("start"):
        probe, ordered, exits = kernel_call(
            functools.partial(second_start_kernel, window),
            "start1",
            [(2, window, window), (window, window), (2, window, window)],
            scalars,
            [obj, ill, amps],
            roll,
        )
    (acc,) = kernel_call(
        functools.partial(first_sum_kernel, window, classes), "sum0", [(2, 2, share, columns)], (), near
    )
    late = spread(
        kernel_call(
            functools.partial(second_wave_kernel, window, classes),
            "wave1",
            [(2 * share, window)] * classes,
            scalars,
            [probe, ordered, exits, table, rim],
            work,
            48 * window**3,
        )
    )
    sums = kernel_call(
        functools.partial(second_sum_kernel, window, classes),
        "sum1",
        [(4 * share, LANES)] * (3 * tiles),
        (),
        [acc, *near, *late],
    )
    is_upper = lax.axis_index("pos") >= classes
    kept, received = [], []
    for chunk in range(tiles):
        top, middle, spilled = sums[3 * chunk : 3 * chunk + 3]
        with jax.named_scope("spill_" + str(chunk)):
            top = top + shifted(spilled, "tile", 1)
        outgoing = jnp.where(is_upper, top, middle)
        with jax.named_scope("halves_" + str(chunk)):
            received.append(exchanged(outgoing, "pos", classes))
        kept.append(jnp.where(is_upper, middle, top))
    result = pl.pallas_call(
        functools.partial(final_kernel, tiles, share),
        out_shape=jax.ShapeDtypeStruct((share * 4 * tiles, LANES), F32),
        in_specs=[pl.BlockSpec(memory_space=pltpu.VMEM)] * (2 * tiles),
        out_specs=pl.BlockSpec(memory_space=pltpu.VMEM),
        compiler_params=pltpu.CompilerParams(vmem_limit_bytes=16 << 20),
        name="final",
    )(*[in_vmem(array) for array in kept + received])
    return unlinear(result, share, columns)


def solution(mesh):
    in_specs = (
        P("tile", None, None),
        P(),
        P(("tile", "pos"), None, None),
        P(("tile", "pos")),
        P(("tile", "pos")),
    )
    out_specs = P(("tile", "pos"), None, None)
    return jax.shard_map(
        on_device, mesh=mesh, in_specs=in_specs, out_specs=out_specs, check_vma=False
    )
```

```python
import functools
import math

import jax
import jax.numpy as jnp
import numpy as np
from jax import lax
from jax.experimental import pallas as pl
from jax.experimental.pallas import tpu as pltpu
from jax.sharding import PartitionSpec as P

LANES = 128
F32 = jnp.float32
BF16 = jnp.bfloat16


def shifted(block, axis, distance):
    devices = lax.axis_size(axis)
    return lax.ppermute(block, axis, [((i - distance) % devices, i) for i in range(devices)])


def exchanged(block, axis, flip):
    return lax.ppermute(block, axis, [(i, i ^ flip) for i in range(lax.axis_size(axis))])


def split_tables(length):
    half = length // 2
    n = np.arange(half, dtype=np.int64)
    even = 2 * n[:, None] * n[None, :]
    odd = n[:, None] * (2 * n[None, :] + 1)
    rows = []
    for product in (even, odd, odd.T):
        angles = (product % length) * (2.0 * math.pi / length)
        real, imag = np.cos(angles) / math.sqrt(length), -np.sin(angles) / math.sqrt(length)
        whole = np.concatenate([real, imag, -imag], axis=1)
        high = whole.astype(BF16)
        rows += [high, (whole - high.astype(np.float64)).astype(BF16)]
    return jnp.asarray(np.concatenate(rows, axis=0))


def linear(array):
    rows, parts, columns = array.shape
    tiles = columns // LANES
    return array.reshape(rows, parts, tiles, LANES).transpose(0, 2, 1, 3).reshape(rows * tiles * parts, LANES)


def unlinear(array, rows, columns):
    tiles = columns // LANES
    return array.reshape(rows, tiles, 2, LANES).transpose(0, 2, 1, 3).reshape(rows, 2, columns)


def halves(value):
    high = value.astype(BF16)
    return high, (value - high.astype(F32)).astype(BF16)


def dot3(high_left, low_left, high_right, low_right):
    left = jnp.concatenate([low_left, high_left, high_left], axis=1)
    right = jnp.concatenate([high_right, low_right, high_right], axis=0)
    return jnp.dot(left, right, preferred_element_type=F32)


def in_vmem(array):
    return pltpu.with_memory_space_constraint(array, pltpu.VMEM)


def kernel_call(body, name, out_shapes, scalars, arrays, scratch=(), flops=0):
    smem = pl.BlockSpec(memory_space=pltpu.SMEM)
    vmem = pl.BlockSpec(memory_space=pltpu.VMEM)
    moved = sum(4 * math.prod(shape) for shape in out_shapes)
    return pl.pallas_call(
        body,
        out_shape=[pltpu.VMEM(shape, F32) for shape in out_shapes],
        in_specs=[smem] * len(scalars) + [vmem] * len(arrays),
        out_specs=[vmem] * len(out_shapes),
        scratch_shapes=scratch,
        cost_estimate=pl.CostEstimate(flops=flops, transcendentals=0, bytes_accessed=2 * moved),
        compiler_params=pltpu.CompilerParams(vmem_limit_bytes=16 << 20),
        name=name,
    )(*scalars, *[in_vmem(array) for array in arrays])


def chosen(slot, rows, cols, band_start, window):
    crossing = (rows[0] - band_start > window).astype(jnp.int32)
    index = crossing if slot == 0 else 1 - crossing
    return rows[index] - band_start, cols[index], index


def load_kernel(number, *refs):
    sources, targets, sem = refs[:number], refs[number : 2 * number], refs[2 * number]
    copies = [pltpu.make_async_copy(a, b, sem.at[i]) for i, (a, b) in enumerate(zip(sources, targets))]
    for copy in copies:
        copy.start()
    for copy in copies:
        copy.wait()


def loaded(arrays):
    return pl.pallas_call(
        functools.partial(load_kernel, len(arrays)),
        out_shape=[pltpu.VMEM(array.shape, array.dtype) for array in arrays],
        in_specs=[pl.BlockSpec(memory_space=pl.ANY)] * len(arrays),
        out_specs=[pl.BlockSpec(memory_space=pltpu.VMEM)] * len(arrays),
        scratch_shapes=[pltpu.SemaphoreType.DMA((len(arrays),))],
        compiler_params=pltpu.CompilerParams(vmem_limit_bytes=16 << 20),
        name="load",
    )(*[pltpu.with_memory_space_constraint(array, pltpu.HBM) for array in arrays])


def pick_kernel(window, rows, cols, out):
    _, column, _ = chosen(1, rows, cols, lax.axis_index("tile") * (2 * window), window)
    out[...] = jnp.broadcast_to(column.astype(F32), out.shape)


def rim_kernel(window, wanted, obj, out):
    offset = wanted[pl.ds(0, 1), :]
    tiles = window // LANES
    for tile in range(tiles):
        column = (lax.broadcasted_iota(jnp.int32, (window, LANES), 1) + tile * LANES).astype(F32)
        for part in range(2):
            near = obj[pl.ds(tile * 2 + part, window, stride=4 * tiles), :]
            beyond = obj[pl.ds((tiles + tile) * 2 + part, window, stride=4 * tiles), :]
            out[part, :, pl.ds(tile * LANES, LANES)] = jnp.where(column < offset, beyond, near)


def prepare(slot, window, rows, cols, obj, ill, amps, doubled, probe, ordered, emit):
    tiles = window // LANES
    half = window // 2
    row, column, index = chosen(slot, rows, cols, lax.axis_index("tile") * (2 * window), window)
    size = 32
    step = 2 * tiles
    whole = window * step
    doubled[pl.ds(0, whole), :] = ill[...]
    doubled[pl.ds(whole, size * step), :] = ill[pl.ds(0, size * step), :]
    turn = lax.rem(row, window)

    below = lax.broadcasted_iota(jnp.int32, (window, window), 0)
    beside = lax.broadcasted_iota(jnp.int32, (window, window), 1)

    def picks(frequency, place):
        wanted = jnp.where(place < half, 2 * place, 2 * (place - half) + 1)
        return jnp.where(frequency == wanted, 1.0, 0.0).astype(BF16)

    by_column = jnp.dot(amps[index], picks(below, beside), preferred_element_type=F32).astype(BF16)
    ordered[...] = jnp.dot(picks(beside, below), by_column, preferred_element_type=F32)

    for first in range(0, window, size):
        place = lax.broadcasted_iota(jnp.int32, (size, window), 0) + first
        across = lax.broadcasted_iota(jnp.int32, (size, window), 1)
        start = lax.rem(first + window - turn, window) * step
        pair = []
        for part in range(2):
            rolled = jnp.concatenate(
                [doubled[pl.ds(start + tile * 2 + part, size, stride=step), :] for tile in range(tiles)],
                axis=1,
            )
            rolled = pltpu.roll(rolled, column, 1)
            probe[part, pl.ds(first, size), :] = rolled

            def block(base):
                def tile_at(tile):
                    return obj[pl.ds((base + first) * 2 * step + tile * 2 + part, size, stride=2 * step), :]

                near = jnp.concatenate([tile_at(t) for t in range(tiles)], axis=1)
                beyond = jnp.concatenate([tile_at(t + tiles) for t in range(tiles)], axis=1)
                return jnp.where(across < column, beyond, near)

            pair.append((rolled, jnp.where(place < row, block(window), block(0))))
        emit(first, size, product(*pair))


def product(real_pair, imag_pair):
    (probe_real, obj_real), (probe_imag, obj_imag) = real_pair, imag_pair
    return (
        probe_real * obj_real - probe_imag * obj_imag,
        probe_real * obj_imag + probe_imag * obj_real,
    )


def keep(high_ref, low_ref, here, across, value):
    high, low = halves(value)
    high_ref[here, across] = high
    low_ref[here, across] = low


def keep_exit(xh, xl, first, size, exits):
    here = pl.ds(first, size)
    window = exits[0].shape[1]
    half = window // 2
    for part, value in enumerate(exits):
        left, right = value[:, :half], value[:, half:]
        keep(xh, xl, here, pl.ds(part * half, half), left + right)
        keep(xh, xl, here, pl.ds(window + part * half, half), left - right)


def transforms(window, classes, table, probe, ordered, xh, xl, yh, yl, far, outs):
    half = window // 2
    own = lax.rem(lax.axis_index("pos"), classes)
    size = 32

    def block_of(matrix, part, low):
        return table[pl.ds((2 * matrix + low) * half, half), pl.ds(part * half, half)]

    def factor(matrix, order):
        return [
            jnp.concatenate(
                [
                    jnp.concatenate([block_of(matrix, part, low) for part in line], axis=1)
                    for line in order
                ],
                axis=0,
            )
            for low in range(2)
        ]

    def from_right(first, matrix):
        across = pl.ds(first, window)
        return dot3(xh[:, across], xl[:, across], *factor(matrix, ((0, 1), (2, 0))))

    def from_left(matrix, first):
        down = pl.ds(first, window)
        return dot3(*factor(matrix, ((0, 2), (1, 0))), yh[down, :], yl[down, :])

    for parity in range(2):
        mid = from_right(parity * window, parity)
        across = pl.ds(parity * half, half)
        for first in range(0, half, size):
            top, bottom = mid[first : first + size], mid[half + first : half + first + size]
            for line, value in enumerate((top + bottom, top - bottom)):
                for part in range(2):
                    here = pl.ds((2 * line + part) * half + first, size)
                    keep(yh, yl, here, across, value[:, part * half : (part + 1) * half])
    far[pl.ds(0, window), :] = from_left(0, 0)
    far[pl.ds(window, window), :] = from_left(2, window)

    for parity in range(2):
        for first in range(0, half, size):
            real = far[pl.ds(parity * window + first, size), :]
            imag = far[pl.ds(parity * window + half + first, size), :]
            here = pl.ds(parity * half + first, size)
            inverse = jnp.minimum(lax.rsqrt(real * real + imag * imag), 4.0)
            scaled = ordered[here, :] * inverse
            for part, value in enumerate((real * (1.0 - scaled), imag * (scaled - 1.0))):
                for side in range(2):
                    across = pl.ds(side * window + part * half, half)
                    keep(xh, xl, here, across, value[:, side * half : (side + 1) * half])

    even, odd = from_right(0, 0), from_right(window, 2)
    for first in range(0, window, size):
        near, beyond = even[first : first + size], odd[first : first + size]
        parity, place = first // half, first % half
        for side, value in enumerate((near + beyond, near - beyond)):
            for part in range(2):
                here = pl.ds((2 * parity + part) * half + place, size)
                keep(yh, yl, here, pl.ds(side * half, half), value[:, part * half : (part + 1) * half])
    far[pl.ds(0, window), :] = from_left(0, 0)
    far[pl.ds(window, window), :] = from_left(1, window)

    share = window // classes
    for flip in range(classes):
        base = pl.multiple_of((own ^ flip) * share, share)
        place = pl.multiple_of(lax.rem(base, half), share)
        sign = jnp.where(base < half, 1.0, -1.0)
        real, imag = (
            far[pl.ds(part * half + place, share), :] + sign * far[pl.ds(window + part * half + place, share), :]
            for part in range(2)
        )
        here = pl.ds(base, share)
        probe_real = probe[0, here, :]
        probe_imag = probe[1, here, :]
        outs[flip][pl.ds(0, share), :] = probe_real * real - probe_imag * imag
        outs[flip][pl.ds(share, share), :] = -(probe_real * imag + probe_imag * real)


def first_wave_kernel(window, classes, rows, cols, obj, ill, amps, table, *refs):
    outs = refs[:classes]
    doubled, probe, ordered, xh, xl, yh, yl, far = refs[classes:]
    emit = functools.partial(keep_exit, xh, xl)
    prepare(0, window, rows, cols, obj, ill, amps, doubled, probe, ordered, emit)
    transforms(window, classes, table, probe, ordered, xh, xl, yh, yl, far, outs)
    share = window // classes
    line = lax.broadcasted_iota(jnp.int32, (8, window), 0)
    head = jnp.zeros((8, window), jnp.int32)
    for slot in range(2):
        row, column, _ = chosen(slot, rows, cols, lax.axis_index("tile") * (2 * window), window)
        head = jnp.where(line == 2 * slot, row, jnp.where(line == 2 * slot + 1, column, head))
    for out in outs:
        out[pl.ds(2 * share, 8), :] = head.astype(F32)


def second_start_kernel(window, rows, cols, obj, ill, amps, probe, ordered, exits, doubled):
    def emit(first, size, values):
        for part in range(2):
            exits[part, pl.ds(first, size), :] = values[part]

    prepare(1, window, rows, cols, obj, ill, amps, doubled, probe, ordered, emit)


def second_wave_kernel(window, classes, rows, cols, probe, ordered, exits, table, rim, *refs):
    outs = refs[:classes]
    xh, xl, yh, yl, far = refs[classes:]
    row, _, _ = chosen(1, rows, cols, lax.axis_index("tile") * (2 * window), window)
    size = 32
    for first in range(0, window, size):
        here = pl.ds(first, size)
        beyond = lax.broadcasted_iota(jnp.int32, (size, window), 0) + (first + window) < row
        edge = product(*[(probe[part, here, :], rim[part, here, :]) for part in range(2)])
        values = [jnp.where(beyond, edge[part], exits[part, here, :]) for part in range(2)]
        keep_exit(xh, xl, first, size, values)
    transforms(window, classes, table, probe, ordered, xh, xl, yh, yl, far, outs)


def scratch_of(window):
    tiles = window // LANES
    roll = [pltpu.VMEM(((window + 32) * 2 * tiles + 8, LANES), F32)]
    state = [pltpu.VMEM((2, window, window), F32), pltpu.VMEM((window, window), F32)]
    work = [
        pltpu.VMEM((window, 2 * window), BF16),
        pltpu.VMEM((window, 2 * window), BF16),
        pltpu.VMEM((2 * window, window), BF16),
        pltpu.VMEM((2 * window, window), BF16),
        pltpu.VMEM((2 * window, window), F32),
    ]
    return roll, state, work


def placed(slot, piece, own, share, window):
    row = piece[pl.ds(2 * share + 2 * slot, 1), :]
    column = piece[pl.ds(2 * share + 2 * slot + 1, 1), :]
    place = (lax.broadcasted_iota(jnp.int32, (share, window), 0) + own * share).astype(F32)
    across = lax.broadcasted_iota(jnp.int32, (share, window), 1).astype(F32)
    return across < column, place < row, place + float(window) < row


def first_sum_kernel(window, classes, *refs):
    pieces, acc = refs[:classes], refs[classes]
    share = window // classes
    own = lax.rem(lax.axis_index("pos"), classes)
    for part in range(2):
        total = [[jnp.zeros((share, window), F32) for _ in range(2)] for _ in range(2)]
        for piece in pieces:
            upper, below, _ = placed(0, piece, own, share, window)
            value = piece[pl.ds(part * share, share), :]
            for k, wanted in enumerate((~below, below)):
                kept = jnp.where(wanted, value, 0.0)
                total[k][0] += jnp.where(upper, 0.0, kept)
                total[k][1] += jnp.where(upper, kept, 0.0)
        for k in range(2):
            for half in range(2):
                acc[k, part, :, pl.ds(half * window, window)] = total[k][half]


def second_sum_kernel(window, classes, acc, *refs):
    heads, pieces, outs = refs[:classes], refs[classes : 2 * classes], refs[2 * classes :]
    share = window // classes
    tiles = window // LANES
    own = lax.rem(lax.axis_index("pos"), classes)
    for part in range(2):
        total = [[acc[k, part, :, pl.ds(h * window, window)] for h in range(2)] for k in range(2)]
        total.append([jnp.zeros((share, window), F32) for _ in range(2)])
        for head, piece in zip(heads, pieces):
            upper, below, lowest = placed(1, head, own, share, window)
            value = piece[pl.ds(part * share, share), :]
            for k, wanted in enumerate((~below, below & ~lowest, lowest)):
                kept = jnp.where(wanted, value, 0.0)
                total[k][0] += jnp.where(upper, 0.0, kept)
                total[k][1] += jnp.where(upper, kept, 0.0)
        for k in range(3):
            for half in range(2):
                for tile in range(tiles):
                    outs[3 * (2 * tile + part) + k][pl.ds(half * share, share), :] = total[k][half][
                        :, tile * LANES : (tile + 1) * LANES
                    ]


def final_kernel(tiles, share, *refs):
    chunks = 2 * tiles
    kept, received, out = refs[:chunks], refs[chunks : 2 * chunks], refs[2 * chunks]
    for chunk in range(chunks):
        for half in range(2):
            here = pl.ds(half * share, share)
            line = half * chunks + chunk
            out[pl.ds(line, share, stride=4 * tiles), :] = kept[chunk][here, :] + received[chunk][here, :]


def on_device(object_field, illumination, amplitudes, row_offset, col_offset):
    band_rows, _, columns = object_field.shape
    window = illumination.shape[0]
    ways = lax.axis_size("pos")
    assert band_rows == 2 * window and columns == 2 * window and row_offset.shape[0] == 2
    classes = ways // 2
    share = window // classes
    tiles = window // LANES
    scalars = (row_offset, col_offset)

    arrays = [linear(object_field), linear(illumination), amplitudes, split_tables(window)]
    remote = tuple(pltpu.with_memory_space_constraint(scalar, pltpu.HBM) for scalar in scalars)
    (wanted,) = kernel_call(functools.partial(pick_kernel, window), "pick", [(8, LANES)], remote, [])
    wanted = shifted(wanted, "tile", 1)
    obj, ill, amps, table = loaded(arrays)
    (rim,) = kernel_call(functools.partial(rim_kernel, window), "rim", [(2, window, window)], (), [wanted, obj])
    rim = shifted(rim, "tile", -1)

    def spread(pieces):
        moved = {d: exchanged(pieces[d], "pos", d) for d in reversed(range(1, classes))}
        return [pieces[0]] + [moved[d] for d in range(1, classes)]

    roll, state, work = scratch_of(window)
    near = spread(
        kernel_call(
            functools.partial(first_wave_kernel, window, classes),
            "wave0",
            [(2 * share + 8, window)] * classes,
            scalars,
            [obj, ill, amps, table],
            roll + state + work,
            48 * window**3,
        )
    )
    with jax.named_scope("start"):
        probe, ordered, exits = kernel_call(
            functools.partial(second_start_kernel, window),
            "start1",
            [(2, window, window), (window, window), (2, window, window)],
            scalars,
            [obj, ill, amps],
            roll,
        )
    (acc,) = kernel_call(
        functools.partial(first_sum_kernel, window, classes), "sum0", [(2, 2, share, columns)], (), near
    )
    late = spread(
        kernel_call(
            functools.partial(second_wave_kernel, window, classes),
            "wave1",
            [(2 * share, window)] * classes,
            scalars,
            [probe, ordered, exits, table, rim],
            work,
            48 * window**3,
        )
    )
    sums = kernel_call(
        functools.partial(second_sum_kernel, window, classes),
        "sum1",
        [(2 * share, LANES)] * (6 * tiles),
        (),
        [acc, *near, *late],
    )
    is_upper = lax.axis_index("pos") >= classes
    kept, received = [], []
    for chunk in range(2 * tiles):
        top, middle, spilled = sums[3 * chunk : 3 * chunk + 3]
        with jax.named_scope("spill_" + str(chunk)):
            top = top + shifted(spilled, "tile", 1)
        outgoing = jnp.where(is_upper, top, middle)
        with jax.named_scope("halves_" + str(chunk)):
            received.append(exchanged(outgoing, "pos", classes))
        kept.append(jnp.where(is_upper, middle, top))
    result = pl.pallas_call(
        functools.partial(final_kernel, tiles, share),
        out_shape=jax.ShapeDtypeStruct((share * 4 * tiles, LANES), F32),
        in_specs=[pl.BlockSpec(memory_space=pltpu.VMEM)] * (4 * tiles),
        out_specs=pl.BlockSpec(memory_space=pltpu.VMEM),
        compiler_params=pltpu.CompilerParams(vmem_limit_bytes=16 << 20),
        name="final",
    )(*[in_vmem(array) for array in kept + received])
    return unlinear(result, share, columns)


def solution(mesh):
    in_specs = (
        P("tile", None, None),
        P(),
        P(("tile", "pos"), None, None),
        P(("tile", "pos")),
        P(("tile", "pos")),
    )
    out_specs = P(("tile", "pos"), None, None)
    return jax.shard_map(
        on_device, mesh=mesh, in_specs=in_specs, out_specs=out_specs, check_vma=False
    )
```

```python
import functools
import math

import jax
import jax.numpy as jnp
import numpy as np
from jax import lax
from jax.experimental import pallas as pl
from jax.experimental.pallas import tpu as pltpu
from jax.sharding import PartitionSpec as P

LANES = 128
F32 = jnp.float32
BF16 = jnp.bfloat16


def shifted(block, axis, distance):
    devices = lax.axis_size(axis)
    return lax.ppermute(block, axis, [((i - distance) % devices, i) for i in range(devices)])


def exchanged(block, axis, flip):
    return lax.ppermute(block, axis, [(i, i ^ flip) for i in range(lax.axis_size(axis))])


def split_tables(length):
    half = length // 2
    n = np.arange(half, dtype=np.int64)
    even = 2 * n[:, None] * n[None, :]
    odd = n[:, None] * (2 * n[None, :] + 1)
    rows = []
    for product in (even, odd, odd.T):
        angles = (product % length) * (2.0 * math.pi / length)
        real, imag = np.cos(angles) / math.sqrt(length), -np.sin(angles) / math.sqrt(length)
        whole = np.concatenate([real, imag, -imag], axis=1)
        high = whole.astype(BF16)
        rows += [high, (whole - high.astype(np.float64)).astype(BF16)]
    return jnp.asarray(np.concatenate(rows, axis=0))


def linear(array):
    rows, parts, columns = array.shape
    tiles = columns // LANES
    return array.reshape(rows, parts, tiles, LANES).transpose(0, 2, 1, 3).reshape(rows * tiles * parts, LANES)


def unlinear(array, rows, columns):
    tiles = columns // LANES
    return array.reshape(rows, tiles, 2, LANES).transpose(0, 2, 1, 3).reshape(rows, 2, columns)


def halves(value):
    high = value.astype(BF16)
    return high, (value - high.astype(F32)).astype(BF16)


def dot3(high_left, low_left, high_right, low_right):
    left = jnp.concatenate([low_left, high_left, high_left], axis=1)
    right = jnp.concatenate([high_right, low_right, high_right], axis=0)
    return jnp.dot(left, right, preferred_element_type=F32)


def in_vmem(array):
    return pltpu.with_memory_space_constraint(array, pltpu.VMEM)


def kernel_call(body, name, out_shapes, scalars, arrays, scratch=(), flops=0):
    smem = pl.BlockSpec(memory_space=pltpu.SMEM)
    vmem = pl.BlockSpec(memory_space=pltpu.VMEM)
    moved = sum(4 * math.prod(shape) for shape in out_shapes)
    return pl.pallas_call(
        body,
        out_shape=[pltpu.VMEM(shape, F32) for shape in out_shapes],
        in_specs=[smem] * len(scalars) + [vmem] * len(arrays),
        out_specs=[vmem] * len(out_shapes),
        scratch_shapes=scratch,
        cost_estimate=pl.CostEstimate(flops=flops, transcendentals=0, bytes_accessed=2 * moved),
        compiler_params=pltpu.CompilerParams(vmem_limit_bytes=16 << 20),
        name=name,
    )(*scalars, *[in_vmem(array) for array in arrays])


def chosen(slot, rows, cols, band_start, window):
    crossing = (rows[0] - band_start > window).astype(jnp.int32)
    index = crossing if slot == 0 else 1 - crossing
    return rows[index] - band_start, cols[index], index


def load_kernel(number, *refs):
    sources, targets, sem = refs[:number], refs[number : 2 * number], refs[2 * number]
    copies = [pltpu.make_async_copy(a, b, sem.at[i]) for i, (a, b) in enumerate(zip(sources, targets))]
    for copy in copies:
        copy.start()
    for copy in copies:
        copy.wait()


def loaded(arrays):
    return pl.pallas_call(
        functools.partial(load_kernel, len(arrays)),
        out_shape=[pltpu.VMEM(array.shape, array.dtype) for array in arrays],
        in_specs=[pl.BlockSpec(memory_space=pl.ANY)] * len(arrays),
        out_specs=[pl.BlockSpec(memory_space=pltpu.VMEM)] * len(arrays),
        scratch_shapes=[pltpu.SemaphoreType.DMA((len(arrays),))],
        compiler_params=pltpu.CompilerParams(vmem_limit_bytes=16 << 20),
        name="load",
    )(*[pltpu.with_memory_space_constraint(array, pltpu.HBM) for array in arrays])


def pick_kernel(window, rows, cols, out):
    _, column, _ = chosen(1, rows, cols, lax.axis_index("tile") * (2 * window), window)
    out[...] = jnp.broadcast_to(column.astype(F32), out.shape)


def rim_kernel(window, wanted, obj, out):
    offset = wanted[pl.ds(0, 1), :]
    tiles = window // LANES
    for tile in range(tiles):
        column = (lax.broadcasted_iota(jnp.int32, (window, LANES), 1) + tile * LANES).astype(F32)
        for part in range(2):
            near = obj[pl.ds(tile * 2 + part, window, stride=4 * tiles), :]
            beyond = obj[pl.ds((tiles + tile) * 2 + part, window, stride=4 * tiles), :]
            out[part, :, pl.ds(tile * LANES, LANES)] = jnp.where(column < offset, beyond, near)


def prepare(slot, window, rows, cols, obj, ill, amps, doubled, probe, ordered, emit):
    tiles = window // LANES
    half = window // 2
    row, column, index = chosen(slot, rows, cols, lax.axis_index("tile") * (2 * window), window)
    size = 32
    step = 2 * tiles
    whole = window * step
    doubled[pl.ds(0, whole), :] = ill[...]
    doubled[pl.ds(whole, size * step), :] = ill[pl.ds(0, size * step), :]
    turn = lax.rem(row, window)

    below = lax.broadcasted_iota(jnp.int32, (window, window), 0)
    beside = lax.broadcasted_iota(jnp.int32, (window, window), 1)

    def picks(frequency, place):
        wanted = jnp.where(place < half, 2 * place, 2 * (place - half) + 1)
        return jnp.where(frequency == wanted, 1.0, 0.0).astype(BF16)

    by_column = jnp.dot(amps[index], picks(below, beside), preferred_element_type=F32).astype(BF16)
    ordered[...] = jnp.dot(picks(beside, below), by_column, preferred_element_type=F32)

    for first in range(0, window, size):
        place = lax.broadcasted_iota(jnp.int32, (size, window), 0) + first
        across = lax.broadcasted_iota(jnp.int32, (size, window), 1)
        start = lax.rem(first + window - turn, window) * step
        pair = []
        for part in range(2):
            rolled = jnp.concatenate(
                [doubled[pl.ds(start + tile * 2 + part, size, stride=step), :] for tile in range(tiles)],
                axis=1,
            )
            rolled = pltpu.roll(rolled, column, 1)
            probe[part, pl.ds(first, size), :] = rolled

            def block(base):
                def tile_at(tile):
                    return obj[pl.ds((base + first) * 2 * step + tile * 2 + part, size, stride=2 * step), :]

                near = jnp.concatenate([tile_at(t) for t in range(tiles)], axis=1)
                beyond = jnp.concatenate([tile_at(t + tiles) for t in range(tiles)], axis=1)
                return jnp.where(across < column, beyond, near)

            pair.append((rolled, jnp.where(place < row, block(window), block(0))))
        emit(first, size, product(*pair))


def product(real_pair, imag_pair):
    (probe_real, obj_real), (probe_imag, obj_imag) = real_pair, imag_pair
    return (
        probe_real * obj_real - probe_imag * obj_imag,
        probe_real * obj_imag + probe_imag * obj_real,
    )


def keep(high_ref, low_ref, here, across, value):
    high, low = halves(value)
    high_ref[here, across] = high
    low_ref[here, across] = low


def keep_exit(xh, xl, first, size, exits):
    here = pl.ds(first, size)
    window = exits[0].shape[1]
    half = window // 2
    for part, value in enumerate(exits):
        left, right = value[:, :half], value[:, half:]
        keep(xh, xl, here, pl.ds(part * half, half), left + right)
        keep(xh, xl, here, pl.ds(window + part * half, half), left - right)


def transforms(window, classes, table, probe, ordered, xh, xl, yh, yl, far, outs):
    half = window // 2
    own = lax.rem(lax.axis_index("pos"), classes)
    size = 32

    def block_of(matrix, part, low):
        return table[pl.ds((2 * matrix + low) * half, half), pl.ds(part * half, half)]

    def factor(matrix, order):
        return [
            jnp.concatenate(
                [
                    jnp.concatenate([block_of(matrix, part, low) for part in line], axis=1)
                    for line in order
                ],
                axis=0,
            )
            for low in range(2)
        ]

    def from_right(first, matrix):
        across = pl.ds(first, window)
        return dot3(xh[:, across], xl[:, across], *factor(matrix, ((0, 1), (2, 0))))

    def from_left(matrix, first):
        down = pl.ds(first, window)
        return dot3(*factor(matrix, ((0, 2), (1, 0))), yh[down, :], yl[down, :])

    for parity in range(2):
        mid = from_right(parity * window, parity)
        across = pl.ds(parity * half, half)
        for first in range(0, half, size):
            top, bottom = mid[first : first + size], mid[half + first : half + first + size]
            for line, value in enumerate((top + bottom, top - bottom)):
                for part in range(2):
                    here = pl.ds((2 * line + part) * half + first, size)
                    keep(yh, yl, here, across, value[:, part * half : (part + 1) * half])
    far[pl.ds(0, window), :] = from_left(0, 0)
    far[pl.ds(window, window), :] = from_left(2, window)

    for parity in range(2):
        for first in range(0, half, size):
            real = far[pl.ds(parity * window + first, size), :]
            imag = far[pl.ds(parity * window + half + first, size), :]
            here = pl.ds(parity * half + first, size)
            inverse = jnp.minimum(lax.rsqrt(real * real + imag * imag), 4.0)
            scaled = ordered[here, :] * inverse
            for part, value in enumerate((real * (1.0 - scaled), imag * (scaled - 1.0))):
                for side in range(2):
                    across = pl.ds(side * window + part * half, half)
                    keep(xh, xl, here, across, value[:, side * half : (side + 1) * half])

    even, odd = from_right(0, 0), from_right(window, 2)
    for first in range(0, window, size):
        near, beyond = even[first : first + size], odd[first : first + size]
        parity, place = first // half, first % half
        for side, value in enumerate((near + beyond, near - beyond)):
            for part in range(2):
                here = pl.ds((2 * parity + part) * half + place, size)
                keep(yh, yl, here, pl.ds(side * half, half), value[:, part * half : (part + 1) * half])
    far[pl.ds(0, window), :] = from_left(0, 0)
    far[pl.ds(window, window), :] = from_left(1, window)

    share = window // classes
    for flip in range(classes):
        base = pl.multiple_of((own ^ flip) * share, share)
        place = pl.multiple_of(lax.rem(base, half), share)
        sign = jnp.where(base < half, 1.0, -1.0)
        real, imag = (
            far[pl.ds(part * half + place, share), :] + sign * far[pl.ds(window + part * half + place, share), :]
            for part in range(2)
        )
        here = pl.ds(base, share)
        probe_real = probe[0, here, :]
        probe_imag = probe[1, here, :]
        outs[flip][pl.ds(0, share), :] = probe_real * real - probe_imag * imag
        outs[flip][pl.ds(share, share), :] = -(probe_real * imag + probe_imag * real)


def first_wave_kernel(window, classes, rows, cols, obj, ill, amps, table, *refs):
    outs = refs[:classes]
    doubled, probe, ordered, xh, xl, yh, yl, far = refs[classes:]
    emit = functools.partial(keep_exit, xh, xl)
    prepare(0, window, rows, cols, obj, ill, amps, doubled, probe, ordered, emit)
    transforms(window, classes, table, probe, ordered, xh, xl, yh, yl, far, outs)
    share = window // classes
    line = lax.broadcasted_iota(jnp.int32, (8, window), 0)
    head = jnp.zeros((8, window), jnp.int32)
    for slot in range(2):
        row, column, _ = chosen(slot, rows, cols, lax.axis_index("tile") * (2 * window), window)
        head = jnp.where(line == 2 * slot, row, jnp.where(line == 2 * slot + 1, column, head))
    for out in outs:
        out[pl.ds(2 * share, 8), :] = head.astype(F32)


def second_start_kernel(window, rows, cols, obj, ill, amps, probe, ordered, exits, doubled):
    def emit(first, size, values):
        for part in range(2):
            exits[part, pl.ds(first, size), :] = values[part]

    prepare(1, window, rows, cols, obj, ill, amps, doubled, probe, ordered, emit)


def second_wave_kernel(window, classes, rows, cols, probe, ordered, exits, table, rim, *refs):
    outs = refs[:classes]
    xh, xl, yh, yl, far = refs[classes:]
    row, _, _ = chosen(1, rows, cols, lax.axis_index("tile") * (2 * window), window)
    size = 32
    for first in range(0, window, size):
        here = pl.ds(first, size)
        beyond = lax.broadcasted_iota(jnp.int32, (size, window), 0) + (first + window) < row
        edge = product(*[(probe[part, here, :], rim[part, here, :]) for part in range(2)])
        values = [jnp.where(beyond, edge[part], exits[part, here, :]) for part in range(2)]
        keep_exit(xh, xl, first, size, values)
    transforms(window, classes, table, probe, ordered, xh, xl, yh, yl, far, outs)


def scratch_of(window):
    tiles = window // LANES
    roll = [pltpu.VMEM(((window + 32) * 2 * tiles + 8, LANES), F32)]
    state = [pltpu.VMEM((2, window, window), F32), pltpu.VMEM((window, window), F32)]
    work = [
        pltpu.VMEM((window, 2 * window), BF16),
        pltpu.VMEM((window, 2 * window), BF16),
        pltpu.VMEM((2 * window, window), BF16),
        pltpu.VMEM((2 * window, window), BF16),
        pltpu.VMEM((2 * window, window), F32),
    ]
    return roll, state, work


def placed(slot, piece, own, share, window):
    row = piece[pl.ds(2 * share + 2 * slot, 1), :]
    column = piece[pl.ds(2 * share + 2 * slot + 1, 1), :]
    place = (lax.broadcasted_iota(jnp.int32, (share, window), 0) + own * share).astype(F32)
    across = lax.broadcasted_iota(jnp.int32, (share, window), 1).astype(F32)
    return across < column, place < row, place + float(window) < row


def first_sum_kernel(window, classes, *refs):
    pieces, acc = refs[:classes], refs[classes]
    share = window // classes
    own = lax.rem(lax.axis_index("pos"), classes)
    for part in range(2):
        total = [[jnp.zeros((share, window), F32) for _ in range(2)] for _ in range(2)]
        for piece in pieces:
            upper, below, _ = placed(0, piece, own, share, window)
            value = piece[pl.ds(part * share, share), :]
            for k, wanted in enumerate((~below, below)):
                kept = jnp.where(wanted, value, 0.0)
                total[k][0] += jnp.where(upper, 0.0, kept)
                total[k][1] += jnp.where(upper, kept, 0.0)
        for k in range(2):
            for half in range(2):
                acc[k, part, :, pl.ds(half * window, window)] = total[k][half]


def grouped(tiles):
    return [(1, 0)] + [(0, strip - 1) for strip in range(1, 2 * tiles)]


def second_sum_kernel(window, classes, acc, *refs):
    heads, pieces, outs = refs[:classes], refs[classes : 2 * classes], refs[2 * classes :]
    share = window // classes
    tiles = window // LANES
    own = lax.rem(lax.axis_index("pos"), classes)
    for part in range(2):
        total = [[acc[k, part, :, pl.ds(h * window, window)] for h in range(2)] for k in range(2)]
        total.append([jnp.zeros((share, window), F32) for _ in range(2)])
        for head, piece in zip(heads, pieces):
            upper, below, lowest = placed(1, head, own, share, window)
            value = piece[pl.ds(part * share, share), :]
            for k, wanted in enumerate((~below, below & ~lowest, lowest)):
                kept = jnp.where(wanted, value, 0.0)
                total[k][0] += jnp.where(upper, 0.0, kept)
                total[k][1] += jnp.where(upper, kept, 0.0)
        for k in range(3):
            for half in range(2):
                for tile in range(tiles):
                    group, place = grouped(tiles)[2 * tile + part]
                    here = pl.ds((2 * place + half) * share, share)
                    outs[3 * group + k][here, :] = total[k][half][:, tile * LANES : (tile + 1) * LANES]


def final_kernel(tiles, share, *refs):
    kept, received, out = refs[:2], refs[2:4], refs[4]
    for strip, (group, place) in enumerate(grouped(tiles)):
        for half in range(2):
            here = pl.ds((2 * place + half) * share, share)
            line = half * 2 * tiles + strip
            out[pl.ds(line, share, stride=4 * tiles), :] = kept[group][here, :] + received[group][here, :]


def on_device(object_field, illumination, amplitudes, row_offset, col_offset):
    band_rows, _, columns = object_field.shape
    window = illumination.shape[0]
    ways = lax.axis_size("pos")
    assert band_rows == 2 * window and columns == 2 * window and row_offset.shape[0] == 2
    classes = ways // 2
    share = window // classes
    tiles = window // LANES
    scalars = (row_offset, col_offset)

    arrays = [linear(object_field), linear(illumination), amplitudes, split_tables(window)]
    remote = tuple(pltpu.with_memory_space_constraint(scalar, pltpu.HBM) for scalar in scalars)
    (wanted,) = kernel_call(functools.partial(pick_kernel, window), "pick", [(8, LANES)], remote, [])
    wanted = shifted(wanted, "tile", 1)
    obj, ill, amps, table = loaded(arrays)
    (rim,) = kernel_call(functools.partial(rim_kernel, window), "rim", [(2, window, window)], (), [wanted, obj])
    rim = shifted(rim, "tile", -1)

    def spread(pieces):
        moved = {d: exchanged(pieces[d], "pos", d) for d in reversed(range(1, classes))}
        return [pieces[0]] + [moved[d] for d in range(1, classes)]

    roll, state, work = scratch_of(window)
    near = spread(
        kernel_call(
            functools.partial(first_wave_kernel, window, classes),
            "wave0",
            [(2 * share + 8, window)] * classes,
            scalars,
            [obj, ill, amps, table],
            roll + state + work,
            48 * window**3,
        )
    )
    with jax.named_scope("start"):
        probe, ordered, exits = kernel_call(
            functools.partial(second_start_kernel, window),
            "start1",
            [(2, window, window), (window, window), (2, window, window)],
            scalars,
            [obj, ill, amps],
            roll,
        )
    (acc,) = kernel_call(
        functools.partial(first_sum_kernel, window, classes), "sum0", [(2, 2, share, columns)], (), near
    )
    late = spread(
        kernel_call(
            functools.partial(second_wave_kernel, window, classes),
            "wave1",
            [(2 * share, window)] * classes,
            scalars,
            [probe, ordered, exits, table, rim],
            work,
            48 * window**3,
        )
    )
    sums = kernel_call(
        functools.partial(second_sum_kernel, window, classes),
        "sum1",
        [((2 * tiles - 1) * 2 * share, LANES)] * 3 + [(2 * share, LANES)] * 3,
        (),
        [acc, *near, *late],
    )
    is_upper = lax.axis_index("pos") >= classes
    kept, received = [], []
    for chunk in range(2):
        top, middle, spilled = sums[3 * chunk : 3 * chunk + 3]
        with jax.named_scope("spill_" + str(chunk)):
            top = top + shifted(spilled, "tile", 1)
        outgoing = jnp.where(is_upper, top, middle)
        with jax.named_scope("halves_" + str(chunk)):
            received.append(exchanged(outgoing, "pos", classes))
        kept.append(jnp.where(is_upper, middle, top))
    result = pl.pallas_call(
        functools.partial(final_kernel, tiles, share),
        out_shape=jax.ShapeDtypeStruct((share * 4 * tiles, LANES), F32),
        in_specs=[pl.BlockSpec(memory_space=pltpu.VMEM)] * 4,
        out_specs=pl.BlockSpec(memory_space=pltpu.VMEM),
        compiler_params=pltpu.CompilerParams(vmem_limit_bytes=16 << 20),
        name="final",
    )(*[in_vmem(array) for array in kept + received])
    return unlinear(result, share, columns)


def solution(mesh):
    in_specs = (
        P("tile", None, None),
        P(),
        P(("tile", "pos"), None, None),
        P(("tile", "pos")),
        P(("tile", "pos")),
    )
    out_specs = P(("tile", "pos"), None, None)
    return jax.shard_map(
        on_device, mesh=mesh, in_specs=in_specs, out_specs=out_specs, check_vma=False
    )
```

```python
import functools
import math

import jax
import jax.numpy as jnp
import numpy as np
from jax import lax
from jax.experimental import pallas as pl
from jax.experimental.pallas import tpu as pltpu
from jax.sharding import PartitionSpec as P


LANES = 128
F32 = jnp.float32
BF16 = jnp.bfloat16


def shifted(block, axis, distance):
    devices = lax.axis_size(axis)
    return lax.ppermute(block, axis, [((i - distance) % devices, i) for i in range(devices)])


def exchanged(block, axis, flip):
    return lax.ppermute(block, axis, [(i, i ^ flip) for i in range(lax.axis_size(axis))])


def split_tables(length):
    half = length // 2
    n = np.arange(half, dtype=np.int64)
    even = 2 * n[:, None] * n[None, :]
    odd = n[:, None] * (2 * n[None, :] + 1)
    rows = []
    for product in (even, odd, odd.T):
        angles = (product % length) * (2.0 * math.pi / length)
        real, imag = np.cos(angles) / math.sqrt(length), -np.sin(angles) / math.sqrt(length)
        whole = np.concatenate([real, imag, -imag], axis=1)
        high = whole.astype(BF16)
        rows += [high, (whole - high.astype(np.float64)).astype(BF16)]
    return jnp.asarray(np.concatenate(rows, axis=0))


def linear(array):
    rows, parts, columns = array.shape
    tiles = columns // LANES
    return array.reshape(rows, parts, tiles, LANES).transpose(0, 2, 1, 3).reshape(rows * tiles * parts, LANES)


def unlinear(array, rows, columns):
    tiles = columns // LANES
    return array.reshape(rows, tiles, 2, LANES).transpose(0, 2, 1, 3).reshape(rows, 2, columns)


def halves(value):
    high = value.astype(BF16)
    return high, (value - high.astype(F32)).astype(BF16)


def dot3(high_left, low_left, high_right, low_right):
    left = jnp.concatenate([low_left, high_left, high_left], axis=1)
    right = jnp.concatenate([high_right, low_right, high_right], axis=0)
    return jnp.dot(left, right, preferred_element_type=F32)


def in_vmem(array):
    return pltpu.with_memory_space_constraint(array, pltpu.VMEM)


def kernel_call(body, out_shapes, scalars, arrays, scratch=(), flops=0):
    smem = pl.BlockSpec(memory_space=pltpu.SMEM)
    vmem = pl.BlockSpec(memory_space=pltpu.VMEM)
    moved = sum(4 * math.prod(shape) for shape in out_shapes)
    return pl.pallas_call(
        body,
        out_shape=[pltpu.VMEM(shape, F32) for shape in out_shapes],
        in_specs=[smem] * len(scalars) + [vmem] * len(arrays),
        out_specs=[vmem] * len(out_shapes),
        scratch_shapes=scratch,
        cost_estimate=pl.CostEstimate(flops=flops, transcendentals=0, bytes_accessed=2 * moved),
        compiler_params=pltpu.CompilerParams(vmem_limit_bytes=16 << 20),
    )(*scalars, *[in_vmem(array) for array in arrays])


def chosen(slot, rows, cols, band_start, window):
    crossing = (rows[0] - band_start > window).astype(jnp.int32)
    index = crossing if slot == 0 else 1 - crossing
    return rows[index] - band_start, cols[index], index


def load_kernel(number, *refs):
    sources, targets, sem = refs[:number], refs[number : 2 * number], refs[2 * number]
    copies = [pltpu.make_async_copy(a, b, sem.at[i]) for i, (a, b) in enumerate(zip(sources, targets))]
    for copy in copies:
        copy.start()
    for copy in copies:
        copy.wait()


def loaded(arrays):
    return pl.pallas_call(
        functools.partial(load_kernel, len(arrays)),
        out_shape=[pltpu.VMEM(array.shape, array.dtype) for array in arrays],
        in_specs=[pl.BlockSpec(memory_space=pl.ANY)] * len(arrays),
        out_specs=[pl.BlockSpec(memory_space=pltpu.VMEM)] * len(arrays),
        scratch_shapes=[pltpu.SemaphoreType.DMA((len(arrays),))],
        compiler_params=pltpu.CompilerParams(vmem_limit_bytes=16 << 20),
        name="load",
    )(*[pltpu.with_memory_space_constraint(array, pltpu.HBM) for array in arrays])


def pick_kernel(window, rows, cols, out):
    _, column, _ = chosen(1, rows, cols, lax.axis_index("tile") * (2 * window), window)
    out[...] = jnp.broadcast_to(column.astype(F32), out.shape)


def rim_kernel(window, wanted, obj, out):
    offset = wanted[pl.ds(0, 1), :]
    tiles = window // LANES
    for tile in range(tiles):
        column = (lax.broadcasted_iota(jnp.int32, (window, LANES), 1) + tile * LANES).astype(F32)
        for part in range(2):
            near = obj[pl.ds(tile * 2 + part, window, stride=4 * tiles), :]
            beyond = obj[pl.ds((tiles + tile) * 2 + part, window, stride=4 * tiles), :]
            out[part, :, pl.ds(tile * LANES, LANES)] = jnp.where(column < offset, beyond, near)


def prepare(slot, window, rows, cols, obj, ill, amps, doubled, probe, ordered, emit):
    tiles = window // LANES
    half = window // 2
    row, column, index = chosen(slot, rows, cols, lax.axis_index("tile") * (2 * window), window)
    size = 32
    step = 2 * tiles
    whole = window * step
    doubled[pl.ds(0, whole), :] = ill[...]
    doubled[pl.ds(whole, size * step), :] = ill[pl.ds(0, size * step), :]
    turn = lax.rem(row, window)

    below = lax.broadcasted_iota(jnp.int32, (window, window), 0)
    beside = lax.broadcasted_iota(jnp.int32, (window, window), 1)

    def picks(frequency, place):
        wanted = jnp.where(place < half, 2 * place, 2 * (place - half) + 1)
        return jnp.where(frequency == wanted, 1.0, 0.0).astype(BF16)

    by_column = jnp.dot(amps[index], picks(below, beside), preferred_element_type=F32).astype(BF16)
    ordered[...] = jnp.dot(picks(beside, below), by_column, preferred_element_type=F32)

    for first in range(0, window, size):
        place = lax.broadcasted_iota(jnp.int32, (size, window), 0) + first
        across = lax.broadcasted_iota(jnp.int32, (size, window), 1)
        start = lax.rem(first + window - turn, window) * step
        pair = []
        for part in range(2):
            rolled = jnp.concatenate(
                [doubled[pl.ds(start + tile * 2 + part, size, stride=step), :] for tile in range(tiles)],
                axis=1,
            )
            rolled = pltpu.roll(rolled, column, 1)
            probe[part, pl.ds(first, size), :] = rolled

            def block(base):
                def tile_at(tile):
                    return obj[pl.ds((base + first) * 2 * step + tile * 2 + part, size, stride=2 * step), :]

                near = jnp.concatenate([tile_at(t) for t in range(tiles)], axis=1)
                beyond = jnp.concatenate([tile_at(t + tiles) for t in range(tiles)], axis=1)
                return jnp.where(across < column, beyond, near)

            pair.append((rolled, jnp.where(place < row, block(window), block(0))))
        emit(first, size, product(*pair))


def product(real_pair, imag_pair):
    (probe_real, obj_real), (probe_imag, obj_imag) = real_pair, imag_pair
    return (
        probe_real * obj_real - probe_imag * obj_imag,
        probe_real * obj_imag + probe_imag * obj_real,
    )


def keep(high_ref, low_ref, here, across, value):
    high, low = halves(value)
    high_ref[here, across] = high
    low_ref[here, across] = low


def keep_exit(xh, xl, first, size, exits):
    here = pl.ds(first, size)
    window = exits[0].shape[1]
    half = window // 2
    for part, value in enumerate(exits):
        left, right = value[:, :half], value[:, half:]
        keep(xh, xl, here, pl.ds(part * half, half), left + right)
        keep(xh, xl, here, pl.ds(window + part * half, half), left - right)


def transforms(window, classes, table, probe, ordered, xh, xl, yh, yl, far, outs):
    half = window // 2
    own = lax.rem(lax.axis_index("pos"), classes)
    size = 32

    def block_of(matrix, part, low):
        return table[pl.ds((2 * matrix + low) * half, half), pl.ds(part * half, half)]

    def factor(matrix, order):
        return [
            jnp.concatenate(
                [
                    jnp.concatenate([block_of(matrix, part, low) for part in line], axis=1)
                    for line in order
                ],
                axis=0,
            )
            for low in range(2)
        ]

    def from_right(first, matrix):
        across = pl.ds(first, window)
        return dot3(xh[:, across], xl[:, across], *factor(matrix, ((0, 1), (2, 0))))

    def from_left(matrix, first):
        down = pl.ds(first, window)
        return dot3(*factor(matrix, ((0, 2), (1, 0))), yh[down, :], yl[down, :])

    for parity in range(2):
        mid = from_right(parity * window, parity)
        across = pl.ds(parity * half, half)
        for first in range(0, half, size):
            top, bottom = mid[first : first + size], mid[half + first : half + first + size]
            for line, value in enumerate((top + bottom, top - bottom)):
                for part in range(2):
                    here = pl.ds((2 * line + part) * half + first, size)
                    keep(yh, yl, here, across, value[:, part * half : (part + 1) * half])
    far[pl.ds(0, window), :] = from_left(0, 0)
    far[pl.ds(window, window), :] = from_left(2, window)

    for parity in range(2):
        for first in range(0, half, size):
            real = far[pl.ds(parity * window + first, size), :]
            imag = far[pl.ds(parity * window + half + first, size), :]
            here = pl.ds(parity * half + first, size)
            inverse = jnp.minimum(lax.rsqrt(real * real + imag * imag), 4.0)
            scaled = ordered[here, :] * inverse
            for part, value in enumerate((real * (1.0 - scaled), imag * (scaled - 1.0))):
                for side in range(2):
                    across = pl.ds(side * window + part * half, half)
                    keep(xh, xl, here, across, value[:, side * half : (side + 1) * half])

    even, odd = from_right(0, 0), from_right(window, 2)
    for first in range(0, window, size):
        near, beyond = even[first : first + size], odd[first : first + size]
        parity, place = first // half, first % half
        for side, value in enumerate((near + beyond, near - beyond)):
            for part in range(2):
                here = pl.ds((2 * parity + part) * half + place, size)
                keep(yh, yl, here, pl.ds(side * half, half), value[:, part * half : (part + 1) * half])
    far[pl.ds(0, window), :] = from_left(0, 0)
    far[pl.ds(window, window), :] = from_left(1, window)

    share = window // classes
    for flip in range(classes):
        base = pl.multiple_of((own ^ flip) * share, share)
        place = pl.multiple_of(lax.rem(base, half), share)
        sign = jnp.where(base < half, 1.0, -1.0)
        real, imag = (
            far[pl.ds(part * half + place, share), :] + sign * far[pl.ds(window + part * half + place, share), :]
            for part in range(2)
        )
        here = pl.ds(base, share)
        probe_real = probe[0, here, :]
        probe_imag = probe[1, here, :]
        outs[flip][pl.ds(0, share), :] = probe_real * real - probe_imag * imag
        outs[flip][pl.ds(share, share), :] = -(probe_real * imag + probe_imag * real)


def first_wave_kernel(window, classes, rows, cols, obj, ill, amps, table, *refs):
    outs = refs[:classes]
    doubled, probe, ordered, xh, xl, yh, yl, far = refs[classes:]
    emit = functools.partial(keep_exit, xh, xl)
    prepare(0, window, rows, cols, obj, ill, amps, doubled, probe, ordered, emit)
    transforms(window, classes, table, probe, ordered, xh, xl, yh, yl, far, outs)
    share = window // classes
    line = lax.broadcasted_iota(jnp.int32, (8, window), 0)
    head = jnp.zeros((8, window), jnp.int32)
    for slot in range(2):
        row, column, _ = chosen(slot, rows, cols, lax.axis_index("tile") * (2 * window), window)
        head = jnp.where(line == 2 * slot, row, jnp.where(line == 2 * slot + 1, column, head))
    for out in outs:
        out[pl.ds(2 * share, 8), :] = head.astype(F32)


def second_start_kernel(window, rows, cols, obj, ill, amps, probe, ordered, exits, doubled):
    def emit(first, size, values):
        for part in range(2):
            exits[part, pl.ds(first, size), :] = values[part]

    prepare(1, window, rows, cols, obj, ill, amps, doubled, probe, ordered, emit)


def second_wave_kernel(window, classes, rows, cols, probe, ordered, exits, table, rim, *refs):
    outs = refs[:classes]
    xh, xl, yh, yl, far = refs[classes:]
    row, _, _ = chosen(1, rows, cols, lax.axis_index("tile") * (2 * window), window)
    size = 32
    for first in range(0, window, size):
        here = pl.ds(first, size)
        beyond = lax.broadcasted_iota(jnp.int32, (size, window), 0) + (first + window) < row
        edge = product(*[(probe[part, here, :], rim[part, here, :]) for part in range(2)])
        values = [jnp.where(beyond, edge[part], exits[part, here, :]) for part in range(2)]
        keep_exit(xh, xl, first, size, values)
    transforms(window, classes, table, probe, ordered, xh, xl, yh, yl, far, outs)


def scratch_of(window):
    tiles = window // LANES
    roll = [pltpu.VMEM(((window + 32) * 2 * tiles + 8, LANES), F32)]
    state = [pltpu.VMEM((2, window, window), F32), pltpu.VMEM((window, window), F32)]
    work = [
        pltpu.VMEM((window, 2 * window), BF16),
        pltpu.VMEM((window, 2 * window), BF16),
        pltpu.VMEM((2 * window, window), BF16),
        pltpu.VMEM((2 * window, window), BF16),
        pltpu.VMEM((2 * window, window), F32),
    ]
    return roll, state, work


def placed(slot, piece, own, share, window):
    row = piece[pl.ds(2 * share + 2 * slot, 1), :]
    column = piece[pl.ds(2 * share + 2 * slot + 1, 1), :]
    place = (lax.broadcasted_iota(jnp.int32, (share, window), 0) + own * share).astype(F32)
    across = lax.broadcasted_iota(jnp.int32, (share, window), 1).astype(F32)
    return across < column, place < row, place + float(window) < row


def first_sum_kernel(window, classes, *refs):
    pieces, acc = refs[:classes], refs[classes]
    share = window // classes
    own = lax.rem(lax.axis_index("pos"), classes)
    for part in range(2):
        total = [[jnp.zeros((share, window), F32) for _ in range(2)] for _ in range(2)]
        for piece in pieces:
            upper, below, _ = placed(0, piece, own, share, window)
            value = piece[pl.ds(part * share, share), :]
            for k, wanted in enumerate((~below, below)):
                kept = jnp.where(wanted, value, 0.0)
                total[k][0] += jnp.where(upper, 0.0, kept)
                total[k][1] += jnp.where(upper, kept, 0.0)
        for k in range(2):
            for half in range(2):
                acc[k, part, :, pl.ds(half * window, window)] = total[k][half]


def grouped(tiles):
    return [(1, 0)] + [(0, strip - 1) for strip in range(1, 2 * tiles)]


def second_sum_kernel(window, classes, acc, *refs):
    heads, pieces, outs = refs[:classes], refs[classes : 2 * classes], refs[2 * classes :]
    share = window // classes
    tiles = window // LANES
    own = lax.rem(lax.axis_index("pos"), classes)
    for part in range(2):
        total = [[acc[k, part, :, pl.ds(h * window, window)] for h in range(2)] for k in range(2)]
        total.append([jnp.zeros((share, window), F32) for _ in range(2)])
        for head, piece in zip(heads, pieces):
            upper, below, lowest = placed(1, head, own, share, window)
            value = piece[pl.ds(part * share, share), :]
            for k, wanted in enumerate((~below, below & ~lowest, lowest)):
                kept = jnp.where(wanted, value, 0.0)
                total[k][0] += jnp.where(upper, 0.0, kept)
                total[k][1] += jnp.where(upper, kept, 0.0)
        for k in range(3):
            for half in range(2):
                for tile in range(tiles):
                    group, place = grouped(tiles)[2 * tile + part]
                    here = pl.ds((2 * place + half) * share, share)
                    outs[3 * group + k][here, :] = total[k][half][:, tile * LANES : (tile + 1) * LANES]


def final_kernel(tiles, share, *refs):
    kept, received, out = refs[:2], refs[2:4], refs[4]
    for strip, (group, place) in enumerate(grouped(tiles)):
        for half in range(2):
            here = pl.ds((2 * place + half) * share, share)
            line = half * 2 * tiles + strip
            out[pl.ds(line, share, stride=4 * tiles), :] = kept[group][here, :] + received[group][here, :]


def on_device(object_field, illumination, amplitudes, row_offset, col_offset):
    band_rows, _, columns = object_field.shape
    window = illumination.shape[0]
    ways = lax.axis_size("pos")
    assert band_rows == 2 * window and columns == 2 * window and row_offset.shape[0] == 2
    classes = ways // 2
    share = window // classes
    tiles = window // LANES
    scalars = (row_offset, col_offset)

    arrays = [linear(object_field), linear(illumination), amplitudes, split_tables(window)]
    remote = tuple(pltpu.with_memory_space_constraint(scalar, pltpu.HBM) for scalar in scalars)
    (wanted,) = kernel_call(functools.partial(pick_kernel, window), [(8, LANES)], remote, [])
    wanted = shifted(wanted, "tile", 1)
    obj, ill, amps, table = loaded(arrays)
    (rim,) = kernel_call(functools.partial(rim_kernel, window), [(2, window, window)], (), [wanted, obj])
    rim = shifted(rim, "tile", -1)

    def spread(pieces):
        moved = {d: exchanged(pieces[d], "pos", d) for d in reversed(range(1, classes))}
        return [pieces[0]] + [moved[d] for d in range(1, classes)]

    roll, state, work = scratch_of(window)
    near = spread(
        kernel_call(
            functools.partial(first_wave_kernel, window, classes),
            [(2 * share + 8, window)] * classes,
            scalars,
            [obj, ill, amps, table],
            roll + state + work,
            48 * window**3,
        )
    )
    probe, ordered, exits = kernel_call(
        functools.partial(second_start_kernel, window),
        [(2, window, window), (window, window), (2, window, window)],
        scalars,
        [obj, ill, amps],
        roll,
    )
    (acc,) = kernel_call(functools.partial(first_sum_kernel, window, classes), [(2, 2, share, columns)], (), near)
    late = spread(
        kernel_call(
            functools.partial(second_wave_kernel, window, classes),
            [(2 * share, window)] * classes,
            scalars,
            [probe, ordered, exits, table, rim],
            work,
            48 * window**3,
        )
    )
    sums = kernel_call(
        functools.partial(second_sum_kernel, window, classes),
        [((2 * tiles - 1) * 2 * share, LANES)] * 3 + [(2 * share, LANES)] * 3,
        (),
        [acc, *near, *late],
    )
    is_upper = lax.axis_index("pos") >= classes
    kept, received = [], []
    for chunk in range(2):
        top, middle, spilled = sums[3 * chunk : 3 * chunk + 3]
        top = top + shifted(spilled, "tile", 1)
        outgoing = jnp.where(is_upper, top, middle)
        received.append(exchanged(outgoing, "pos", classes))
        kept.append(jnp.where(is_upper, middle, top))
    result = pl.pallas_call(
        functools.partial(final_kernel, tiles, share),
        out_shape=jax.ShapeDtypeStruct((share * 4 * tiles, LANES), F32),
        in_specs=[pl.BlockSpec(memory_space=pltpu.VMEM)] * 4,
        out_specs=pl.BlockSpec(memory_space=pltpu.VMEM),
        compiler_params=pltpu.CompilerParams(vmem_limit_bytes=16 << 20),
        name="final",
    )(*[in_vmem(array) for array in kept + received])
    return unlinear(result, share, columns)


def solution(mesh):
    in_specs = (
        P("tile", None, None),
        P(),
        P(("tile", "pos"), None, None),
        P(("tile", "pos")),
        P(("tile", "pos")),
    )
    out_specs = P(("tile", "pos"), None, None)

    return jax.shard_map(on_device, mesh=mesh, in_specs=in_specs, out_specs=out_specs, check_vma=False)
```

```python
import functools
import math

import jax
import jax.numpy as jnp
import numpy as np
from jax import lax
from jax.experimental import pallas as pl
from jax.experimental.pallas import tpu as pltpu
from jax.sharding import PartitionSpec as P

LANES = 128
F32 = jnp.float32
BF16 = jnp.bfloat16


def shifted(block, axis, distance):
    devices = lax.axis_size(axis)
    return lax.ppermute(block, axis, [((i - distance) % devices, i) for i in range(devices)])


def exchanged(block, axis, flip):
    return lax.ppermute(block, axis, [(i, i ^ flip) for i in range(lax.axis_size(axis))])


def split_tables(length):
    half = length // 2
    n = np.arange(half, dtype=np.int64)
    even = 2 * n[:, None] * n[None, :]
    odd = n[:, None] * (2 * n[None, :] + 1)
    rows = []
    for product in (even, odd, odd.T):
        angles = (product % length) * (2.0 * math.pi / length)
        real, imag = np.cos(angles) / math.sqrt(length), -np.sin(angles) / math.sqrt(length)
        whole = np.concatenate([real, imag, -imag], axis=1)
        high = whole.astype(BF16)
        rows += [high, (whole - high.astype(np.float64)).astype(BF16)]
    return jnp.asarray(np.concatenate(rows, axis=0))


def linear(array):
    rows, parts, columns = array.shape
    tiles = columns // LANES
    return array.reshape(rows, parts, tiles, LANES).transpose(0, 2, 1, 3).reshape(rows * tiles * parts, LANES)


def unlinear(array, rows, columns):
    tiles = columns // LANES
    return array.reshape(rows, tiles, 2, LANES).transpose(0, 2, 1, 3).reshape(rows, 2, columns)


def halves(value):
    high = value.astype(BF16)
    return high, (value - high.astype(F32)).astype(BF16)


def dot3(high_left, low_left, high_right, low_right):
    left = jnp.concatenate([low_left, high_left, high_left], axis=1)
    right = jnp.concatenate([high_right, low_right, high_right], axis=0)
    return jnp.dot(left, right, preferred_element_type=F32)


def in_vmem(array):
    return pltpu.with_memory_space_constraint(array, pltpu.VMEM)


def kernel_call(body, name, out_shapes, scalars, arrays, scratch=(), flops=0):
    smem = pl.BlockSpec(memory_space=pltpu.SMEM)
    vmem = pl.BlockSpec(memory_space=pltpu.VMEM)
    moved = sum(4 * math.prod(shape) for shape in out_shapes)
    return pl.pallas_call(
        body,
        out_shape=[pltpu.VMEM(shape, F32) for shape in out_shapes],
        in_specs=[smem] * len(scalars) + [vmem] * len(arrays),
        out_specs=[vmem] * len(out_shapes),
        scratch_shapes=scratch,
        cost_estimate=pl.CostEstimate(flops=flops, transcendentals=0, bytes_accessed=2 * moved),
        compiler_params=pltpu.CompilerParams(vmem_limit_bytes=16 << 20),
        name=name,
    )(*scalars, *[in_vmem(array) for array in arrays])


def chosen(slot, rows, cols, band_start, window):
    crossing = (rows[0] - band_start > window).astype(jnp.int32)
    index = crossing if slot == 0 else 1 - crossing
    return rows[index] - band_start, cols[index], index


def load_kernel(number, *refs):
    sources, targets, sem = refs[:number], refs[number : 2 * number], refs[2 * number]
    copies = [pltpu.make_async_copy(a, b, sem.at[i]) for i, (a, b) in enumerate(zip(sources, targets))]
    for copy in copies:
        copy.start()
    for copy in copies:
        copy.wait()


def loaded(arrays):
    return pl.pallas_call(
        functools.partial(load_kernel, len(arrays)),
        out_shape=[pltpu.VMEM(array.shape, array.dtype) for array in arrays],
        in_specs=[pl.BlockSpec(memory_space=pl.ANY)] * len(arrays),
        out_specs=[pl.BlockSpec(memory_space=pltpu.VMEM)] * len(arrays),
        scratch_shapes=[pltpu.SemaphoreType.DMA((len(arrays),))],
        compiler_params=pltpu.CompilerParams(vmem_limit_bytes=16 << 20),
        name="load",
    )(*[pltpu.with_memory_space_constraint(array, pltpu.HBM) for array in arrays])


def rim_kernel(window, rows, cols, obj, out):
    band_start = (lax.axis_index("tile") - 1) * (2 * window)
    crossing = rows[:, 0:1] - band_start > window
    offset = jnp.where(crossing, cols[:, 0:1], cols[:, 1:2])
    tiles = window // LANES
    for tile in range(tiles):
        column = lax.broadcasted_iota(jnp.int32, (window, LANES), 1) + tile * LANES
        for part in range(2):
            near = obj[pl.ds(tile * 2 + part, window, stride=4 * tiles), :]
            beyond = obj[pl.ds((tiles + tile) * 2 + part, window, stride=4 * tiles), :]
            out[part, :, pl.ds(tile * LANES, LANES)] = jnp.where(column < offset, beyond, near)


def prepare(slot, window, rows, cols, obj, ill, amps, doubled, probe, ordered, emit):
    tiles = window // LANES
    half = window // 2
    row, column, index = chosen(slot, rows, cols, lax.axis_index("tile") * (2 * window), window)
    size = 32
    step = 2 * tiles
    whole = window * step
    doubled[pl.ds(0, whole), :] = ill[...]
    doubled[pl.ds(whole, size * step), :] = ill[pl.ds(0, size * step), :]
    turn = lax.rem(row, window)

    below = lax.broadcasted_iota(jnp.int32, (window, window), 0)
    beside = lax.broadcasted_iota(jnp.int32, (window, window), 1)

    def picks(frequency, place):
        wanted = jnp.where(place < half, 2 * place, 2 * (place - half) + 1)
        return jnp.where(frequency == wanted, 1.0, 0.0).astype(BF16)

    by_column = jnp.dot(amps[index], picks(below, beside), preferred_element_type=F32).astype(BF16)
    ordered[...] = jnp.dot(picks(beside, below), by_column, preferred_element_type=F32)

    for first in range(0, window, size):
        place = lax.broadcasted_iota(jnp.int32, (size, window), 0) + first
        across = lax.broadcasted_iota(jnp.int32, (size, window), 1)
        start = lax.rem(first + window - turn, window) * step
        pair = []
        for part in range(2):
            rolled = jnp.concatenate(
                [doubled[pl.ds(start + tile * 2 + part, size, stride=step), :] for tile in range(tiles)],
                axis=1,
            )
            rolled = pltpu.roll(rolled, column, 1)
            probe[part, pl.ds(first, size), :] = rolled

            def block(base):
                def tile_at(tile):
                    return obj[pl.ds((base + first) * 2 * step + tile * 2 + part, size, stride=2 * step), :]

                near = jnp.concatenate([tile_at(t) for t in range(tiles)], axis=1)
                beyond = jnp.concatenate([tile_at(t + tiles) for t in range(tiles)], axis=1)
                return jnp.where(across < column, beyond, near)

            pair.append((rolled, jnp.where(place < row, block(window), block(0))))
        emit(first, size, product(*pair))


def product(real_pair, imag_pair):
    (probe_real, obj_real), (probe_imag, obj_imag) = real_pair, imag_pair
    return (
        probe_real * obj_real - probe_imag * obj_imag,
        probe_real * obj_imag + probe_imag * obj_real,
    )


def keep(high_ref, low_ref, here, across, value):
    high, low = halves(value)
    high_ref[here, across] = high
    low_ref[here, across] = low


def keep_exit(xh, xl, first, size, exits):
    here = pl.ds(first, size)
    window = exits[0].shape[1]
    half = window // 2
    for part, value in enumerate(exits):
        left, right = value[:, :half], value[:, half:]
        keep(xh, xl, here, pl.ds(part * half, half), left + right)
        keep(xh, xl, here, pl.ds(window + part * half, half), left - right)


def transforms(window, classes, table, probe, ordered, xh, xl, yh, yl, far, outs):
    half = window // 2
    own = lax.rem(lax.axis_index("pos"), classes)
    size = 32

    def block_of(matrix, part, low):
        return table[pl.ds((2 * matrix + low) * half, half), pl.ds(part * half, half)]

    def factor(matrix, order):
        return [
            jnp.concatenate(
                [
                    jnp.concatenate([block_of(matrix, part, low) for part in line], axis=1)
                    for line in order
                ],
                axis=0,
            )
            for low in range(2)
        ]

    def from_right(first, matrix):
        across = pl.ds(first, window)
        return dot3(xh[:, across], xl[:, across], *factor(matrix, ((0, 1), (2, 0))))

    def from_left(matrix, first):
        down = pl.ds(first, window)
        return dot3(*factor(matrix, ((0, 2), (1, 0))), yh[down, :], yl[down, :])

    for parity in range(2):
        mid = from_right(parity * window, parity)
        across = pl.ds(parity * half, half)
        for first in range(0, half, size):
            top, bottom = mid[first : first + size], mid[half + first : half + first + size]
            for line, value in enumerate((top + bottom, top - bottom)):
                for part in range(2):
                    here = pl.ds((2 * line + part) * half + first, size)
                    keep(yh, yl, here, across, value[:, part * half : (part + 1) * half])
    far[pl.ds(0, window), :] = from_left(0, 0)
    far[pl.ds(window, window), :] = from_left(2, window)

    for parity in range(2):
        for first in range(0, half, size):
            real = far[pl.ds(parity * window + first, size), :]
            imag = far[pl.ds(parity * window + half + first, size), :]
            here = pl.ds(parity * half + first, size)
            inverse = jnp.minimum(lax.rsqrt(real * real + imag * imag), 4.0)
            scaled = ordered[here, :] * inverse
            for part, value in enumerate((real * (1.0 - scaled), imag * (scaled - 1.0))):
                for side in range(2):
                    across = pl.ds(side * window + part * half, half)
                    keep(xh, xl, here, across, value[:, side * half : (side + 1) * half])

    even, odd = from_right(0, 0), from_right(window, 2)
    for first in range(0, window, size):
        near, beyond = even[first : first + size], odd[first : first + size]
        parity, place = first // half, first % half
        for side, value in enumerate((near + beyond, near - beyond)):
            for part in range(2):
                here = pl.ds((2 * parity + part) * half + place, size)
                keep(yh, yl, here, pl.ds(side * half, half), value[:, part * half : (part + 1) * half])
    far[pl.ds(0, window), :] = from_left(0, 0)
    far[pl.ds(window, window), :] = from_left(1, window)

    share = window // classes
    for flip in range(classes):
        base = pl.multiple_of((own ^ flip) * share, share)
        place = pl.multiple_of(lax.rem(base, half), share)
        sign = jnp.where(base < half, 1.0, -1.0)
        real, imag = (
            far[pl.ds(part * half + place, share), :] + sign * far[pl.ds(window + part * half + place, share), :]
            for part in range(2)
        )
        here = pl.ds(base, share)
        probe_real = probe[0, here, :]
        probe_imag = probe[1, here, :]
        outs[flip][pl.ds(0, share), :] = probe_real * real - probe_imag * imag
        outs[flip][pl.ds(share, share), :] = -(probe_real * imag + probe_imag * real)


def first_wave_kernel(window, classes, rows, cols, obj, ill, amps, table, *refs):
    outs = refs[:classes]
    doubled, probe, ordered, xh, xl, yh, yl, far = refs[classes:]
    emit = functools.partial(keep_exit, xh, xl)
    prepare(0, window, rows, cols, obj, ill, amps, doubled, probe, ordered, emit)
    transforms(window, classes, table, probe, ordered, xh, xl, yh, yl, far, outs)
    share = window // classes
    line = lax.broadcasted_iota(jnp.int32, (8, window), 0)
    head = jnp.zeros((8, window), jnp.int32)
    for slot in range(2):
        row, column, _ = chosen(slot, rows, cols, lax.axis_index("tile") * (2 * window), window)
        head = jnp.where(line == 2 * slot, row, jnp.where(line == 2 * slot + 1, column, head))
    for out in outs:
        out[pl.ds(2 * share, 8), :] = head.astype(F32)


def second_start_kernel(window, rows, cols, obj, ill, amps, probe, ordered, exits, doubled):
    def emit(first, size, values):
        for part in range(2):
            exits[part, pl.ds(first, size), :] = values[part]

    prepare(1, window, rows, cols, obj, ill, amps, doubled, probe, ordered, emit)


def second_wave_kernel(window, classes, rows, cols, probe, ordered, exits, table, rim, *refs):
    outs = refs[:classes]
    xh, xl, yh, yl, far = refs[classes:]
    row, _, _ = chosen(1, rows, cols, lax.axis_index("tile") * (2 * window), window)
    size = 32
    for first in range(0, window, size):
        here = pl.ds(first, size)
        beyond = lax.broadcasted_iota(jnp.int32, (size, window), 0) + (first + window) < row
        edge = product(*[(probe[part, here, :], rim[part, here, :]) for part in range(2)])
        values = [jnp.where(beyond, edge[part], exits[part, here, :]) for part in range(2)]
        keep_exit(xh, xl, first, size, values)
    transforms(window, classes, table, probe, ordered, xh, xl, yh, yl, far, outs)


def scratch_of(window):
    tiles = window // LANES
    roll = [pltpu.VMEM(((window + 32) * 2 * tiles + 8, LANES), F32)]
    state = [pltpu.VMEM((2, window, window), F32), pltpu.VMEM((window, window), F32)]
    work = [
        pltpu.VMEM((window, 2 * window), BF16),
        pltpu.VMEM((window, 2 * window), BF16),
        pltpu.VMEM((2 * window, window), BF16),
        pltpu.VMEM((2 * window, window), BF16),
        pltpu.VMEM((2 * window, window), F32),
    ]
    return roll, state, work


def placed(slot, piece, own, share, window):
    row = piece[pl.ds(2 * share + 2 * slot, 1), :]
    column = piece[pl.ds(2 * share + 2 * slot + 1, 1), :]
    place = (lax.broadcasted_iota(jnp.int32, (share, window), 0) + own * share).astype(F32)
    across = lax.broadcasted_iota(jnp.int32, (share, window), 1).astype(F32)
    return across < column, place < row, place + float(window) < row


def first_sum_kernel(window, classes, *refs):
    pieces, acc = refs[:classes], refs[classes]
    share = window // classes
    own = lax.rem(lax.axis_index("pos"), classes)
    for part in range(2):
        total = [[jnp.zeros((share, window), F32) for _ in range(2)] for _ in range(2)]
        for piece in pieces:
            upper, below, _ = placed(0, piece, own, share, window)
            value = piece[pl.ds(part * share, share), :]
            for k, wanted in enumerate((~below, below)):
                kept = jnp.where(wanted, value, 0.0)
                total[k][0] += jnp.where(upper, 0.0, kept)
                total[k][1] += jnp.where(upper, kept, 0.0)
        for k in range(2):
            for half in range(2):
                acc[k, part, :, pl.ds(half * window, window)] = total[k][half]


def second_sum_kernel(window, classes, acc, *refs):
    heads, pieces, outs = refs[:classes], refs[classes : 2 * classes], refs[2 * classes :]
    share = window // classes
    tiles = window // LANES
    own = lax.rem(lax.axis_index("pos"), classes)
    for part in range(2):
        total = [[acc[k, part, :, pl.ds(h * window, window)] for h in range(2)] for k in range(2)]
        total.append([jnp.zeros((share, window), F32) for _ in range(2)])
        for head, piece in zip(heads, pieces):
            upper, below, lowest = placed(1, head, own, share, window)
            value = piece[pl.ds(part * share, share), :]
            for k, wanted in enumerate((~below, below & ~lowest, lowest)):
                kept = jnp.where(wanted, value, 0.0)
                total[k][0] += jnp.where(upper, 0.0, kept)
                total[k][1] += jnp.where(upper, kept, 0.0)
        for k in range(3):
            for half in range(2):
                for tile in range(tiles):
                    outs[3 * tile + k][pl.ds((half * 2 + part) * share, share), :] = total[k][half][
                        :, tile * LANES : (tile + 1) * LANES
                    ]


def final_kernel(tiles, share, *refs):
    kept, received, out = refs[:tiles], refs[tiles : 2 * tiles], refs[2 * tiles]
    for tile in range(tiles):
        for half in range(2):
            for part in range(2):
                here = pl.ds((half * 2 + part) * share, share)
                line = (half * tiles + tile) * 2 + part
                out[pl.ds(line, share, stride=4 * tiles), :] = kept[tile][here, :] + received[tile][here, :]


def on_device(object_field, illumination, amplitudes, row_offset, col_offset):
    band_rows, _, columns = object_field.shape
    window = illumination.shape[0]
    ways = lax.axis_size("pos")
    assert band_rows == 2 * window and columns == 2 * window and row_offset.shape[0] == 2
    classes = ways // 2
    share = window // classes
    tiles = window // LANES
    scalars = (row_offset, col_offset)

    arrays = [linear(object_field), linear(illumination), amplitudes, split_tables(window)]
    wanted = [shifted(scalar, "tile", 1).reshape(1, 2) for scalar in scalars]
    obj, ill, amps, table = loaded(arrays)
    (rim,) = kernel_call(functools.partial(rim_kernel, window), "rim", [(2, window, window)], (), [*wanted, obj])
    rim = shifted(rim, "tile", -1)

    def spread(pieces):
        moved = {d: exchanged(pieces[d], "pos", d) for d in reversed(range(1, classes))}
        return [pieces[0]] + [moved[d] for d in range(1, classes)]

    roll, state, work = scratch_of(window)
    near = spread(
        kernel_call(
            functools.partial(first_wave_kernel, window, classes),
            "wave0",
            [(2 * share + 8, window)] * classes,
            scalars,
            [obj, ill, amps, table],
            roll + state + work,
            48 * window**3,
        )
    )
    with jax.named_scope("start"):
        probe, ordered, exits = kernel_call(
            functools.partial(second_start_kernel, window),
            "start1",
            [(2, window, window), (window, window), (2, window, window)],
            scalars,
            [obj, ill, amps],
            roll,
        )
    (acc,) = kernel_call(
        functools.partial(first_sum_kernel, window, classes), "sum0", [(2, 2, share, columns)], (), near
    )
    late = spread(
        kernel_call(
            functools.partial(second_wave_kernel, window, classes),
            "wave1",
            [(2 * share, window)] * classes,
            scalars,
            [probe, ordered, exits, table, rim],
            work,
            48 * window**3,
        )
    )
    sums = kernel_call(
        functools.partial(second_sum_kernel, window, classes),
        "sum1",
        [(4 * share, LANES)] * (3 * tiles),
        (),
        [acc, *near, *late],
    )
    is_upper = lax.axis_index("pos") >= classes
    kept, received = [], []
    for chunk in range(tiles):
        top, middle, spilled = sums[3 * chunk : 3 * chunk + 3]
        with jax.named_scope("spill_" + str(chunk)):
            top = top + shifted(spilled, "tile", 1)
        outgoing = jnp.where(is_upper, top, middle)
        with jax.named_scope("halves_" + str(chunk)):
            received.append(exchanged(outgoing, "pos", classes))
        kept.append(jnp.where(is_upper, middle, top))
    result = pl.pallas_call(
        functools.partial(final_kernel, tiles, share),
        out_shape=jax.ShapeDtypeStruct((share * 4 * tiles, LANES), F32),
        in_specs=[pl.BlockSpec(memory_space=pltpu.VMEM)] * (2 * tiles),
        out_specs=pl.BlockSpec(memory_space=pltpu.VMEM),
        compiler_params=pltpu.CompilerParams(vmem_limit_bytes=16 << 20),
        name="final",
    )(*[in_vmem(array) for array in kept + received])
    return unlinear(result, share, columns)


def solution(mesh):
    in_specs = (
        P("tile", None, None),
        P(),
        P(("tile", "pos"), None, None),
        P(("tile", "pos")),
        P(("tile", "pos")),
    )
    out_specs = P(("tile", "pos"), None, None)
    return jax.shard_map(
        on_device, mesh=mesh, in_specs=in_specs, out_specs=out_specs, check_vma=False
    )
```

```python
import functools
import math

import jax
import jax.numpy as jnp
import numpy as np
from jax import lax
from jax.experimental import pallas as pl
from jax.experimental.pallas import tpu as pltpu
from jax.sharding import PartitionSpec as P


LANES = 128
F32 = jnp.float32
BF16 = jnp.bfloat16


def shifted(block, axis, distance):
    devices = lax.axis_size(axis)
    return lax.ppermute(block, axis, [((i - distance) % devices, i) for i in range(devices)])


def exchanged(block, axis, flip):
    return lax.ppermute(block, axis, [(i, i ^ flip) for i in range(lax.axis_size(axis))])


def split_tables(length):
    half = length // 2
    n = np.arange(half, dtype=np.int64)
    even = 2 * n[:, None] * n[None, :]
    odd = n[:, None] * (2 * n[None, :] + 1)
    rows = []
    for product in (even, odd, odd.T):
        angles = (product % length) * (2.0 * math.pi / length)
        real, imag = np.cos(angles) / math.sqrt(length), -np.sin(angles) / math.sqrt(length)
        whole = np.concatenate([real, imag, -imag], axis=1)
        high = whole.astype(BF16)
        rows += [high, (whole - high.astype(np.float64)).astype(BF16)]
    return jnp.asarray(np.concatenate(rows, axis=0))


def linear(array):
    rows, parts, columns = array.shape
    tiles = columns // LANES
    return array.reshape(rows, parts, tiles, LANES).transpose(0, 2, 1, 3).reshape(rows * tiles * parts, LANES)


def unlinear(array, rows, columns):
    tiles = columns // LANES
    return array.reshape(rows, tiles, 2, LANES).transpose(0, 2, 1, 3).reshape(rows, 2, columns)


def halves(value):
    high = value.astype(BF16)
    return high, (value - high.astype(F32)).astype(BF16)


def dot3(high_left, low_left, high_right, low_right):
    left = jnp.concatenate([low_left, high_left, high_left], axis=1)
    right = jnp.concatenate([high_right, low_right, high_right], axis=0)
    return jnp.dot(left, right, preferred_element_type=F32)


def in_vmem(array):
    return pltpu.with_memory_space_constraint(array, pltpu.VMEM)


def kernel_call(body, out_shapes, scalars, arrays, scratch=(), flops=0):
    smem = pl.BlockSpec(memory_space=pltpu.SMEM)
    vmem = pl.BlockSpec(memory_space=pltpu.VMEM)
    moved = sum(4 * math.prod(shape) for shape in out_shapes)
    return pl.pallas_call(
        body,
        out_shape=[pltpu.VMEM(shape, F32) for shape in out_shapes],
        in_specs=[smem] * len(scalars) + [vmem] * len(arrays),
        out_specs=[vmem] * len(out_shapes),
        scratch_shapes=scratch,
        cost_estimate=pl.CostEstimate(flops=flops, transcendentals=0, bytes_accessed=2 * moved),
        compiler_params=pltpu.CompilerParams(vmem_limit_bytes=16 << 20),
    )(*scalars, *[in_vmem(array) for array in arrays])


def chosen(slot, rows, cols, band_start, window):
    crossing = (rows[0] - band_start > window).astype(jnp.int32)
    index = crossing if slot == 0 else 1 - crossing
    return rows[index] - band_start, cols[index], index


def load_kernel(number, *refs):
    sources, targets, sem = refs[:number], refs[number : 2 * number + 1], refs[2 * number + 1]
    strip = sources[0].at[pl.ds(0, targets[-1].shape[0])]
    copies = [pltpu.make_async_copy(a, b, sem.at[i]) for i, (a, b) in enumerate(zip((strip, *sources), (targets[-1], *targets)))]
    for copy in copies:
        copy.start()
    for copy in copies:
        copy.wait()


def loaded(arrays, strip_rows):
    outputs = [pltpu.VMEM(array.shape, array.dtype) for array in arrays] + [pltpu.VMEM((strip_rows, LANES), F32)]
    return pl.pallas_call(
        functools.partial(load_kernel, len(arrays)),
        out_shape=outputs,
        in_specs=[pl.BlockSpec(memory_space=pl.ANY)] * len(arrays),
        out_specs=[pl.BlockSpec(memory_space=pltpu.VMEM)] * len(outputs),
        scratch_shapes=[pltpu.SemaphoreType.DMA((len(outputs),))],
        compiler_params=pltpu.CompilerParams(vmem_limit_bytes=16 << 20),
        name="load",
    )(*[pltpu.with_memory_space_constraint(array, pltpu.HBM) for array in arrays])


def rim_kernel(window, skipped, rows, cols, obj, out):
    band_start = (lax.axis_index("tile") - 1) * (2 * window)
    crossing = rows[:, 0:1] - band_start > window
    offset = jnp.where(crossing, cols[:, 0:1], cols[:, 1:2])
    tiles = window // LANES
    number = window - skipped
    base = skipped * 4 * tiles
    for tile in range(tiles):
        column = lax.broadcasted_iota(jnp.int32, (number, LANES), 1) + tile * LANES
        for part in range(2):
            near = obj[pl.ds(base + tile * 2 + part, number, stride=4 * tiles), :]
            beyond = obj[pl.ds(base + (tiles + tile) * 2 + part, number, stride=4 * tiles), :]
            out[part, :, pl.ds(tile * LANES, LANES)] = jnp.where(column < offset, beyond, near)


def prepare(slot, window, rows, cols, obj, ill, amps, doubled, probe, ordered, emit):
    tiles = window // LANES
    half = window // 2
    row, column, index = chosen(slot, rows, cols, lax.axis_index("tile") * (2 * window), window)
    size = 32
    step = 2 * tiles
    whole = window * step
    doubled[pl.ds(0, whole), :] = ill[...]
    doubled[pl.ds(whole, size * step), :] = ill[pl.ds(0, size * step), :]
    turn = lax.rem(row, window)

    below = lax.broadcasted_iota(jnp.int32, (window, window), 0)
    beside = lax.broadcasted_iota(jnp.int32, (window, window), 1)

    def picks(frequency, place):
        wanted = jnp.where(place < half, 2 * place, 2 * (place - half) + 1)
        return jnp.where(frequency == wanted, 1.0, 0.0).astype(BF16)

    by_column = jnp.dot(amps[index], picks(below, beside), preferred_element_type=F32).astype(BF16)
    ordered[...] = jnp.dot(picks(beside, below), by_column, preferred_element_type=F32)

    for first in range(0, window, size):
        place = lax.broadcasted_iota(jnp.int32, (size, window), 0) + first
        across = lax.broadcasted_iota(jnp.int32, (size, window), 1)
        start = lax.rem(first + window - turn, window) * step
        pair = []
        for part in range(2):
            rolled = jnp.concatenate(
                [doubled[pl.ds(start + tile * 2 + part, size, stride=step), :] for tile in range(tiles)],
                axis=1,
            )
            rolled = pltpu.roll(rolled, column, 1)
            probe[part, pl.ds(first, size), :] = rolled

            def block(base):
                def tile_at(tile):
                    return obj[pl.ds((base + first) * 2 * step + tile * 2 + part, size, stride=2 * step), :]

                near = jnp.concatenate([tile_at(t) for t in range(tiles)], axis=1)
                beyond = jnp.concatenate([tile_at(t + tiles) for t in range(tiles)], axis=1)
                return jnp.where(across < column, beyond, near)

            pair.append((rolled, jnp.where(place < row, block(window), block(0))))
        emit(first, size, product(*pair))


def product(real_pair, imag_pair):
    (probe_real, obj_real), (probe_imag, obj_imag) = real_pair, imag_pair
    return (
        probe_real * obj_real - probe_imag * obj_imag,
        probe_real * obj_imag + probe_imag * obj_real,
    )


def keep(high_ref, low_ref, here, across, value):
    high, low = halves(value)
    high_ref[here, across] = high
    low_ref[here, across] = low


def keep_exit(xh, xl, first, size, exits):
    here = pl.ds(first, size)
    window = exits[0].shape[1]
    half = window // 2
    for part, value in enumerate(exits):
        left, right = value[:, :half], value[:, half:]
        keep(xh, xl, here, pl.ds(part * half, half), left + right)
        keep(xh, xl, here, pl.ds(window + part * half, half), left - right)


def transforms(window, classes, table, probe, ordered, xh, xl, yh, yl, far, outs):
    half = window // 2
    own = lax.rem(lax.axis_index("pos"), classes)
    size = 32

    def block_of(matrix, part, low):
        return table[pl.ds((2 * matrix + low) * half, half), pl.ds(part * half, half)]

    def factor(matrix, order):
        return [
            jnp.concatenate(
                [
                    jnp.concatenate([block_of(matrix, part, low) for part in line], axis=1)
                    for line in order
                ],
                axis=0,
            )
            for low in range(2)
        ]

    def from_right(first, matrix):
        across = pl.ds(first, window)
        return dot3(xh[:, across], xl[:, across], *factor(matrix, ((0, 1), (2, 0))))

    def from_left(matrix, first):
        down = pl.ds(first, window)
        return dot3(*factor(matrix, ((0, 2), (1, 0))), yh[down, :], yl[down, :])

    for parity in range(2):
        mid = from_right(parity * window, parity)
        across = pl.ds(parity * half, half)
        for first in range(0, half, size):
            top, bottom = mid[first : first + size], mid[half + first : half + first + size]
            for line, value in enumerate((top + bottom, top - bottom)):
                for part in range(2):
                    here = pl.ds((2 * line + part) * half + first, size)
                    keep(yh, yl, here, across, value[:, part * half : (part + 1) * half])
    far[pl.ds(0, window), :] = from_left(0, 0)
    far[pl.ds(window, window), :] = from_left(2, window)

    for parity in range(2):
        for first in range(0, half, size):
            real = far[pl.ds(parity * window + first, size), :]
            imag = far[pl.ds(parity * window + half + first, size), :]
            here = pl.ds(parity * half + first, size)
            inverse = jnp.minimum(lax.rsqrt(real * real + imag * imag), 4.0)
            scaled = ordered[here, :] * inverse
            for part, value in enumerate((real * (1.0 - scaled), imag * (scaled - 1.0))):
                for side in range(2):
                    across = pl.ds(side * window + part * half, half)
                    keep(xh, xl, here, across, value[:, side * half : (side + 1) * half])

    even, odd = from_right(0, 0), from_right(window, 2)
    for first in range(0, window, size):
        near, beyond = even[first : first + size], odd[first : first + size]
        parity, place = first // half, first % half
        for side, value in enumerate((near + beyond, near - beyond)):
            for part in range(2):
                here = pl.ds((2 * parity + part) * half + place, size)
                keep(yh, yl, here, pl.ds(side * half, half), value[:, part * half : (part + 1) * half])
    far[pl.ds(0, window), :] = from_left(0, 0)
    far[pl.ds(window, window), :] = from_left(1, window)

    share = window // classes
    for flip in range(classes):
        base = pl.multiple_of((own ^ flip) * share, share)
        place = pl.multiple_of(lax.rem(base, half), share)
        sign = jnp.where(base < half, 1.0, -1.0)
        real, imag = (
            far[pl.ds(part * half + place, share), :] + sign * far[pl.ds(window + part * half + place, share), :]
            for part in range(2)
        )
        here = pl.ds(base, share)
        probe_real = probe[0, here, :]
        probe_imag = probe[1, here, :]
        outs[flip][pl.ds(0, share), :] = probe_real * real - probe_imag * imag
        outs[flip][pl.ds(share, share), :] = -(probe_real * imag + probe_imag * real)


def first_wave_kernel(window, classes, rows, cols, obj, ill, amps, table, *refs):
    outs = refs[:classes]
    doubled, probe, ordered, xh, xl, yh, yl, far = refs[classes:]
    emit = functools.partial(keep_exit, xh, xl)
    prepare(0, window, rows, cols, obj, ill, amps, doubled, probe, ordered, emit)
    transforms(window, classes, table, probe, ordered, xh, xl, yh, yl, far, outs)
    share = window // classes
    line = lax.broadcasted_iota(jnp.int32, (8, window), 0)
    head = jnp.zeros((8, window), jnp.int32)
    for slot in range(2):
        row, column, _ = chosen(slot, rows, cols, lax.axis_index("tile") * (2 * window), window)
        head = jnp.where(line == 2 * slot, row, jnp.where(line == 2 * slot + 1, column, head))
    for out in outs:
        out[pl.ds(2 * share, 8), :] = head.astype(F32)


def second_start_kernel(window, rows, cols, obj, ill, amps, probe, ordered, exits, doubled):
    def emit(first, size, values):
        for part in range(2):
            exits[part, pl.ds(first, size), :] = values[part]

    prepare(1, window, rows, cols, obj, ill, amps, doubled, probe, ordered, emit)


def second_wave_kernel(window, classes, rows, cols, probe, ordered, exits, table, strip, rim, *refs):
    outs = refs[:classes]
    xh, xl, yh, yl, far = refs[classes:]
    row, column, _ = chosen(1, rows, cols, lax.axis_index("tile") * (2 * window), window)
    size = 32
    tiles = window // LANES
    skipped = window - rim.shape[1]
    across = lax.broadcasted_iota(jnp.int32, (size, window), 1)

    def rim_rows(first, part):
        if first >= skipped:
            return rim[part, pl.ds(first - skipped, size), :]

        def tile_at(tile):
            return strip[pl.ds(first * 4 * tiles + tile * 2 + part, size, stride=4 * tiles), :]

        near = jnp.concatenate([tile_at(t) for t in range(tiles)], axis=1)
        beyond = jnp.concatenate([tile_at(t + tiles) for t in range(tiles)], axis=1)
        return jnp.where(across < column, beyond, near)

    for first in range(0, window, size):
        here = pl.ds(first, size)
        beyond = lax.broadcasted_iota(jnp.int32, (size, window), 0) + (first + window) < row
        edge = product(*[(probe[part, here, :], rim_rows(first, part)) for part in range(2)])
        values = [jnp.where(beyond, edge[part], exits[part, here, :]) for part in range(2)]
        keep_exit(xh, xl, first, size, values)
    transforms(window, classes, table, probe, ordered, xh, xl, yh, yl, far, outs)


def scratch_of(window):
    tiles = window // LANES
    roll = [pltpu.VMEM(((window + 32) * 2 * tiles + 8, LANES), F32)]
    state = [pltpu.VMEM((2, window, window), F32), pltpu.VMEM((window, window), F32)]
    work = [
        pltpu.VMEM((window, 2 * window), BF16),
        pltpu.VMEM((window, 2 * window), BF16),
        pltpu.VMEM((2 * window, window), BF16),
        pltpu.VMEM((2 * window, window), BF16),
        pltpu.VMEM((2 * window, window), F32),
    ]
    return roll, state, work


def placed(slot, piece, own, share, window):
    row = piece[pl.ds(2 * share + 2 * slot, 1), :]
    column = piece[pl.ds(2 * share + 2 * slot + 1, 1), :]
    place = (lax.broadcasted_iota(jnp.int32, (share, window), 0) + own * share).astype(F32)
    across = lax.broadcasted_iota(jnp.int32, (share, window), 1).astype(F32)
    return across < column, place < row, place + float(window) < row


def first_sum_kernel(window, classes, *refs):
    pieces, acc = refs[:classes], refs[classes]
    share = window // classes
    own = lax.rem(lax.axis_index("pos"), classes)
    for part in range(2):
        total = [[jnp.zeros((share, window), F32) for _ in range(2)] for _ in range(2)]
        for piece in pieces:
            upper, below, _ = placed(0, piece, own, share, window)
            value = piece[pl.ds(part * share, share), :]
            for k, wanted in enumerate((~below, below)):
                kept = jnp.where(wanted, value, 0.0)
                total[k][0] += jnp.where(upper, 0.0, kept)
                total[k][1] += jnp.where(upper, kept, 0.0)
        for k in range(2):
            for half in range(2):
                acc[k, part, :, pl.ds(half * window, window)] = total[k][half]


def second_sum_kernel(window, classes, acc, *refs):
    heads, pieces, outs = refs[:classes], refs[classes : 2 * classes], refs[2 * classes :]
    share = window // classes
    tiles = window // LANES
    own = lax.rem(lax.axis_index("pos"), classes)
    for part in range(2):
        total = [[acc[k, part, :, pl.ds(h * window, window)] for h in range(2)] for k in range(2)]
        total.append([jnp.zeros((share, window), F32) for _ in range(2)])
        for head, piece in zip(heads, pieces):
            upper, below, lowest = placed(1, head, own, share, window)
            value = piece[pl.ds(part * share, share), :]
            for k, wanted in enumerate((~below, below & ~lowest, lowest)):
                kept = jnp.where(wanted, value, 0.0)
                total[k][0] += jnp.where(upper, 0.0, kept)
                total[k][1] += jnp.where(upper, kept, 0.0)
        for k in range(3):
            for half in range(2):
                for tile in range(tiles):
                    outs[3 * tile + k][pl.ds((half * 2 + part) * share, share), :] = total[k][half][
                        :, tile * LANES : (tile + 1) * LANES
                    ]


def final_kernel(tiles, share, *refs):
    kept, received, out = refs[:tiles], refs[tiles : 2 * tiles], refs[2 * tiles]
    for tile in range(tiles):
        for half in range(2):
            for part in range(2):
                here = pl.ds((half * 2 + part) * share, share)
                line = (half * tiles + tile) * 2 + part
                out[pl.ds(line, share, stride=4 * tiles), :] = kept[tile][here, :] + received[tile][here, :]


def on_device(object_field, illumination, amplitudes, row_offset, col_offset):
    band_rows, _, columns = object_field.shape
    window = illumination.shape[0]
    ways = lax.axis_size("pos")
    assert band_rows == 2 * window and columns == 2 * window and row_offset.shape[0] == 2
    classes = ways // 2
    share = window // classes
    tiles = window // LANES
    scalars = (row_offset, col_offset)

    arrays = [linear(object_field), linear(illumination), amplitudes, split_tables(window)]
    skipped = window // 4
    wanted = [shifted(scalar, "tile", 1).reshape(1, 2) for scalar in scalars]
    obj, ill, amps, table, strip = loaded(arrays, skipped * 4 * tiles)
    strip = shifted(strip, "tile", -1)
    rim_body = functools.partial(rim_kernel, window, skipped)
    (rim,) = kernel_call(rim_body, [(2, window - skipped, window)], (), [*wanted, obj])
    rim = shifted(rim, "tile", -1)

    def spread(pieces):
        moved = {d: exchanged(pieces[d], "pos", d) for d in reversed(range(1, classes))}
        return [pieces[0]] + [moved[d] for d in range(1, classes)]

    roll, state, work = scratch_of(window)
    near = spread(
        kernel_call(
            functools.partial(first_wave_kernel, window, classes),
            [(2 * share + 8, window)] * classes,
            scalars,
            [obj, ill, amps, table],
            roll + state + work,
            48 * window**3,
        )
    )
    probe, ordered, exits = kernel_call(
        functools.partial(second_start_kernel, window),
        [(2, window, window), (window, window), (2, window, window)],
        scalars,
        [obj, ill, amps],
        roll,
    )
    (acc,) = kernel_call(functools.partial(first_sum_kernel, window, classes), [(2, 2, share, columns)], (), near)
    late = spread(
        kernel_call(
            functools.partial(second_wave_kernel, window, classes),
            [(2 * share, window)] * classes,
            scalars,
            [probe, ordered, exits, table, strip, rim],
            work,
            48 * window**3,
        )
    )
    sums = kernel_call(
        functools.partial(second_sum_kernel, window, classes),
        [(4 * share, LANES)] * (3 * tiles),
        (),
        [acc, *near, *late],
    )
    is_upper = lax.axis_index("pos") >= classes
    kept, received = [], []
    for chunk in range(tiles):
        top, middle, spilled = sums[3 * chunk : 3 * chunk + 3]
        top = top + shifted(spilled, "tile", 1)
        outgoing = jnp.where(is_upper, top, middle)
        received.append(exchanged(outgoing, "pos", classes))
        kept.append(jnp.where(is_upper, middle, top))
    result = pl.pallas_call(
        functools.partial(final_kernel, tiles, share),
        out_shape=jax.ShapeDtypeStruct((share * 4 * tiles, LANES), F32),
        in_specs=[pl.BlockSpec(memory_space=pltpu.VMEM)] * (2 * tiles),
        out_specs=pl.BlockSpec(memory_space=pltpu.VMEM),
        compiler_params=pltpu.CompilerParams(vmem_limit_bytes=16 << 20),
        name="final",
    )(*[in_vmem(array) for array in kept + received])
    return unlinear(result, share, columns)


def solution(mesh):
    in_specs = (
        P("tile", None, None),
        P(),
        P(("tile", "pos"), None, None),
        P(("tile", "pos")),
        P(("tile", "pos")),
    )
    out_specs = P(("tile", "pos"), None, None)

    return jax.shard_map(on_device, mesh=mesh, in_specs=in_specs, out_specs=out_specs, check_vma=False)
```

```python
import functools
import math

import jax
import jax.numpy as jnp
import numpy as np
from jax import lax
from jax.experimental import pallas as pl
from jax.experimental.pallas import tpu as pltpu
from jax.sharding import PartitionSpec as P

LANES = 128
F32 = jnp.float32
BF16 = jnp.bfloat16


def shifted(block, axis, distance):
    devices = lax.axis_size(axis)
    return lax.ppermute(block, axis, [((i - distance) % devices, i) for i in range(devices)])


def exchanged(block, axis, flip):
    return lax.ppermute(block, axis, [(i, i ^ flip) for i in range(lax.axis_size(axis))])


def split_tables(length):
    half = length // 2
    n = np.arange(half, dtype=np.int64)
    even = 2 * n[:, None] * n[None, :]
    odd = n[:, None] * (2 * n[None, :] + 1)
    rows = []
    for product in (even, odd, odd.T):
        angles = (product % length) * (2.0 * math.pi / length)
        real, imag = np.cos(angles) / math.sqrt(length), -np.sin(angles) / math.sqrt(length)
        whole = np.concatenate([real, imag, -imag], axis=1)
        high = whole.astype(BF16)
        rows += [high, (whole - high.astype(np.float64)).astype(BF16)]
    return jnp.asarray(np.concatenate(rows, axis=0))


def linear(array):
    rows, parts, columns = array.shape
    tiles = columns // LANES
    return array.reshape(rows, parts, tiles, LANES).transpose(0, 2, 1, 3).reshape(rows * tiles * parts, LANES)


def unlinear(array, rows, columns):
    tiles = columns // LANES
    return array.reshape(rows, tiles, 2, LANES).transpose(0, 2, 1, 3).reshape(rows, 2, columns)


def halves(value):
    high = value.astype(BF16)
    return high, (value - high.astype(F32)).astype(BF16)


def dot3(high_left, low_left, high_right, low_right):
    left = jnp.concatenate([low_left, high_left, high_left], axis=1)
    right = jnp.concatenate([high_right, low_right, high_right], axis=0)
    return jnp.dot(left, right, preferred_element_type=F32)


def in_vmem(array):
    return pltpu.with_memory_space_constraint(array, pltpu.VMEM)


def kernel_call(body, name, out_shapes, scalars, arrays, scratch=(), flops=0):
    smem = pl.BlockSpec(memory_space=pltpu.SMEM)
    vmem = pl.BlockSpec(memory_space=pltpu.VMEM)
    moved = sum(4 * math.prod(shape) for shape in out_shapes)
    return pl.pallas_call(
        body,
        out_shape=[pltpu.VMEM(shape, F32) for shape in out_shapes],
        in_specs=[smem] * len(scalars) + [vmem] * len(arrays),
        out_specs=[vmem] * len(out_shapes),
        scratch_shapes=scratch,
        cost_estimate=pl.CostEstimate(flops=flops, transcendentals=0, bytes_accessed=2 * moved),
        compiler_params=pltpu.CompilerParams(vmem_limit_bytes=16 << 20),
        name=name,
    )(*scalars, *[in_vmem(array) for array in arrays])


def chosen(slot, rows, cols, band_start, window):
    crossing = (rows[0] - band_start > window).astype(jnp.int32)
    index = crossing if slot == 0 else 1 - crossing
    return rows[index] - band_start, cols[index], index


def load_kernel(number, *refs):
    sources, targets, sem = refs[:number], refs[number : 2 * number], refs[2 * number]
    copies = [pltpu.make_async_copy(a, b, sem.at[i]) for i, (a, b) in enumerate(zip(sources, targets))]
    for copy in copies:
        copy.start()
    for copy in copies:
        copy.wait()


def loaded(arrays):
    return pl.pallas_call(
        functools.partial(load_kernel, len(arrays)),
        out_shape=[pltpu.VMEM(array.shape, array.dtype) for array in arrays],
        in_specs=[pl.BlockSpec(memory_space=pl.ANY)] * len(arrays),
        out_specs=[pl.BlockSpec(memory_space=pltpu.VMEM)] * len(arrays),
        scratch_shapes=[pltpu.SemaphoreType.DMA((len(arrays),))],
        compiler_params=pltpu.CompilerParams(vmem_limit_bytes=16 << 20),
        name="load",
    )(*[pltpu.with_memory_space_constraint(array, pltpu.HBM) for array in arrays])


def rim_kernel(window, rows, cols, obj, out):
    band_start = (lax.axis_index("tile") - 1) * (2 * window)
    crossing = rows[:, 0:1] - band_start > window
    offset = jnp.where(crossing, cols[:, 0:1], cols[:, 1:2])
    tiles = window // LANES
    for tile in range(tiles):
        column = lax.broadcasted_iota(jnp.int32, (window, LANES), 1) + tile * LANES
        for part in range(2):
            near = obj[pl.ds(tile * 2 + part, window, stride=4 * tiles), :]
            beyond = obj[pl.ds((tiles + tile) * 2 + part, window, stride=4 * tiles), :]
            out[part, :, pl.ds(tile * LANES, LANES)] = jnp.where(column < offset, beyond, near)


def prepare(slot, window, rows, cols, obj, ill, amps, doubled, probe, ordered, emit):
    tiles = window // LANES
    half = window // 2
    row, column, index = chosen(slot, rows, cols, lax.axis_index("tile") * (2 * window), window)
    size = 32
    step = 2 * tiles
    whole = window * step
    doubled[pl.ds(0, whole), :] = ill[...]
    doubled[pl.ds(whole, size * step), :] = ill[pl.ds(0, size * step), :]
    turn = lax.rem(row, window)

    below = lax.broadcasted_iota(jnp.int32, (window, window), 0)
    beside = lax.broadcasted_iota(jnp.int32, (window, window), 1)

    def picks(frequency, place):
        wanted = jnp.where(place < half, 2 * place, 2 * (place - half) + 1)
        return jnp.where(frequency == wanted, 1.0, 0.0).astype(BF16)

    by_column = jnp.dot(amps[index], picks(below, beside), preferred_element_type=F32).astype(BF16)
    ordered[...] = jnp.dot(picks(beside, below), by_column, preferred_element_type=F32)

    for first in range(0, window, size):
        place = lax.broadcasted_iota(jnp.int32, (size, window), 0) + first
        across = lax.broadcasted_iota(jnp.int32, (size, window), 1)
        start = lax.rem(first + window - turn, window) * step
        pair = []
        for part in range(2):
            rolled = jnp.concatenate(
                [doubled[pl.ds(start + tile * 2 + part, size, stride=step), :] for tile in range(tiles)],
                axis=1,
            )
            rolled = pltpu.roll(rolled, column, 1)
            probe[part, pl.ds(first, size), :] = rolled

            def block(base):
                def tile_at(tile):
                    return obj[pl.ds((base + first) * 2 * step + tile * 2 + part, size, stride=2 * step), :]

                near = jnp.concatenate([tile_at(t) for t in range(tiles)], axis=1)
                beyond = jnp.concatenate([tile_at(t + tiles) for t in range(tiles)], axis=1)
                return jnp.where(across < column, beyond, near)

            pair.append((rolled, jnp.where(place < row, block(window), block(0))))
        emit(first, size, product(*pair))


def product(real_pair, imag_pair):
    (probe_real, obj_real), (probe_imag, obj_imag) = real_pair, imag_pair
    return (
        probe_real * obj_real - probe_imag * obj_imag,
        probe_real * obj_imag + probe_imag * obj_real,
    )


def keep(high_ref, low_ref, here, across, value):
    high, low = halves(value)
    high_ref[here, across] = high
    low_ref[here, across] = low


def keep_exit(xh, xl, first, size, exits):
    here = pl.ds(first, size)
    window = exits[0].shape[1]
    half = window // 2
    for part, value in enumerate(exits):
        left, right = value[:, :half], value[:, half:]
        keep(xh, xl, here, pl.ds(part * half, half), left + right)
        keep(xh, xl, here, pl.ds(window + part * half, half), left - right)


def transforms(window, classes, table, probe, ordered, xh, xl, yh, yl, far, outs):
    half = window // 2
    own = lax.rem(lax.axis_index("pos"), classes)
    size = 32

    def block_of(matrix, part, low):
        return table[pl.ds((2 * matrix + low) * half, half), pl.ds(part * half, half)]

    def factor(matrix, order):
        return [
            jnp.concatenate(
                [
                    jnp.concatenate([block_of(matrix, part, low) for part in line], axis=1)
                    for line in order
                ],
                axis=0,
            )
            for low in range(2)
        ]

    def from_right(first, matrix):
        across = pl.ds(first, window)
        return dot3(xh[:, across], xl[:, across], *factor(matrix, ((0, 1), (2, 0))))

    def from_left(matrix, first):
        down = pl.ds(first, window)
        return dot3(*factor(matrix, ((0, 2), (1, 0))), yh[down, :], yl[down, :])

    for parity in range(2):
        mid = from_right(parity * window, parity)
        across = pl.ds(parity * half, half)
        for first in range(0, half, size):
            top, bottom = mid[first : first + size], mid[half + first : half + first + size]
            for line, value in enumerate((top + bottom, top - bottom)):
                for part in range(2):
                    here = pl.ds((2 * line + part) * half + first, size)
                    keep(yh, yl, here, across, value[:, part * half : (part + 1) * half])
    far[pl.ds(0, window), :] = from_left(0, 0)
    far[pl.ds(window, window), :] = from_left(2, window)

    for parity in range(2):
        for first in range(0, half, size):
            real = far[pl.ds(parity * window + first, size), :]
            imag = far[pl.ds(parity * window + half + first, size), :]
            here = pl.ds(parity * half + first, size)
            inverse = jnp.minimum(lax.rsqrt(real * real + imag * imag), 4.0)
            scaled = ordered[here, :] * inverse
            for part, value in enumerate((real * (1.0 - scaled), imag * (scaled - 1.0))):
                for side in range(2):
                    across = pl.ds(side * window + part * half, half)
                    keep(xh, xl, here, across, value[:, side * half : (side + 1) * half])

    even, odd = from_right(0, 0), from_right(window, 2)
    for first in range(0, window, size):
        near, beyond = even[first : first + size], odd[first : first + size]
        parity, place = first // half, first % half
        for side, value in enumerate((near + beyond, near - beyond)):
            for part in range(2):
                here = pl.ds((2 * parity + part) * half + place, size)
                keep(yh, yl, here, pl.ds(side * half, half), value[:, part * half : (part + 1) * half])
    far[pl.ds(0, window), :] = from_left(0, 0)
    far[pl.ds(window, window), :] = from_left(1, window)

    share = window // classes
    for flip in range(classes):
        base = pl.multiple_of((own ^ flip) * share, share)
        place = pl.multiple_of(lax.rem(base, half), share)
        sign = jnp.where(base < half, 1.0, -1.0)
        real, imag = (
            far[pl.ds(part * half + place, share), :] + sign * far[pl.ds(window + part * half + place, share), :]
            for part in range(2)
        )
        here = pl.ds(base, share)
        probe_real = probe[0, here, :]
        probe_imag = probe[1, here, :]
        outs[flip][pl.ds(0, share), :] = probe_real * real - probe_imag * imag
        outs[flip][pl.ds(share, share), :] = -(probe_real * imag + probe_imag * real)


def first_wave_kernel(window, classes, rows, cols, obj, ill, amps, table, *refs):
    outs = refs[:classes]
    doubled, probe, ordered, xh, xl, yh, yl, far = refs[classes:]
    emit = functools.partial(keep_exit, xh, xl)
    prepare(0, window, rows, cols, obj, ill, amps, doubled, probe, ordered, emit)
    transforms(window, classes, table, probe, ordered, xh, xl, yh, yl, far, outs)
    share = window // classes
    line = lax.broadcasted_iota(jnp.int32, (8, window), 0)
    head = jnp.zeros((8, window), jnp.int32)
    for slot in range(2):
        row, column, _ = chosen(slot, rows, cols, lax.axis_index("tile") * (2 * window), window)
        head = jnp.where(line == 2 * slot, row, jnp.where(line == 2 * slot + 1, column, head))
    for out in outs:
        out[pl.ds(2 * share, 8), :] = head.astype(F32)


def second_start_kernel(window, rows, cols, obj, ill, amps, probe, ordered, exits, doubled):
    def emit(first, size, values):
        for part in range(2):
            exits[part, pl.ds(first, size), :] = values[part]

    prepare(1, window, rows, cols, obj, ill, amps, doubled, probe, ordered, emit)


def second_wave_kernel(window, classes, rows, cols, probe, ordered, exits, table, rim, *refs):
    outs = refs[:classes]
    xh, xl, yh, yl, far = refs[classes:]
    row, _, _ = chosen(1, rows, cols, lax.axis_index("tile") * (2 * window), window)
    size = 32
    for first in range(0, window, size):
        here = pl.ds(first, size)
        beyond = lax.broadcasted_iota(jnp.int32, (size, window), 0) + (first + window) < row
        edge = product(*[(probe[part, here, :], rim[part, here, :]) for part in range(2)])
        values = [jnp.where(beyond, edge[part], exits[part, here, :]) for part in range(2)]
        keep_exit(xh, xl, first, size, values)
    transforms(window, classes, table, probe, ordered, xh, xl, yh, yl, far, outs)


def scratch_of(window):
    tiles = window // LANES
    roll = [pltpu.VMEM(((window + 32) * 2 * tiles + 8, LANES), F32)]
    state = [pltpu.VMEM((2, window, window), F32), pltpu.VMEM((window, window), F32)]
    work = [
        pltpu.VMEM((window, 2 * window), BF16),
        pltpu.VMEM((window, 2 * window), BF16),
        pltpu.VMEM((2 * window, window), BF16),
        pltpu.VMEM((2 * window, window), BF16),
        pltpu.VMEM((2 * window, window), F32),
    ]
    return roll, state, work


def placed(slot, piece, own, share, window):
    row = piece[pl.ds(2 * share + 2 * slot, 1), :]
    column = piece[pl.ds(2 * share + 2 * slot + 1, 1), :]
    place = (lax.broadcasted_iota(jnp.int32, (share, window), 0) + own * share).astype(F32)
    across = lax.broadcasted_iota(jnp.int32, (share, window), 1).astype(F32)
    return across < column, place < row, place + float(window) < row


def first_sum_kernel(window, classes, *refs):
    pieces, acc = refs[:classes], refs[classes]
    share = window // classes
    own = lax.rem(lax.axis_index("pos"), classes)
    for part in range(2):
        total = [[jnp.zeros((share, window), F32) for _ in range(2)] for _ in range(2)]
        for piece in pieces:
            upper, below, _ = placed(0, piece, own, share, window)
            value = piece[pl.ds(part * share, share), :]
            for k, wanted in enumerate((~below, below)):
                kept = jnp.where(wanted, value, 0.0)
                total[k][0] += jnp.where(upper, 0.0, kept)
                total[k][1] += jnp.where(upper, kept, 0.0)
        for k in range(2):
            for half in range(2):
                acc[k, part, :, pl.ds(half * window, window)] = total[k][half]


def second_sum_kernel(window, classes, acc, *refs):
    heads, pieces, outs = refs[:classes], refs[classes : 2 * classes], refs[2 * classes :]
    share = window // classes
    tiles = window // LANES
    own = lax.rem(lax.axis_index("pos"), classes)
    for part in range(2):
        total = [[acc[k, part, :, pl.ds(h * window, window)] for h in range(2)] for k in range(2)]
        total.append([jnp.zeros((share, window), F32) for _ in range(2)])
        for head, piece in zip(heads, pieces):
            upper, below, lowest = placed(1, head, own, share, window)
            value = piece[pl.ds(part * share, share), :]
            for k, wanted in enumerate((~below, below & ~lowest, lowest)):
                kept = jnp.where(wanted, value, 0.0)
                total[k][0] += jnp.where(upper, 0.0, kept)
                total[k][1] += jnp.where(upper, kept, 0.0)
        for k in range(3):
            for half in range(2):
                for tile in range(tiles):
                    outs[3 * tile + k][pl.ds((half * 2 + part) * share, share), :] = total[k][half][
                        :, tile * LANES : (tile + 1) * LANES
                    ]


def final_kernel(tiles, share, *refs):
    kept, received, out = refs[:tiles], refs[tiles : 2 * tiles], refs[2 * tiles]
    for tile in range(tiles):
        for half in range(2):
            for part in range(2):
                here = pl.ds((half * 2 + part) * share, share)
                line = (half * tiles + tile) * 2 + part
                out[pl.ds(line, share, stride=4 * tiles), :] = kept[tile][here, :] + received[tile][here, :]


def on_device(object_field, illumination, amplitudes, row_offset, col_offset):
    band_rows, _, columns = object_field.shape
    window = illumination.shape[0]
    ways = lax.axis_size("pos")
    assert band_rows == 2 * window and columns == 2 * window and row_offset.shape[0] == 2
    classes = ways // 2
    share = window // classes
    tiles = window // LANES
    scalars = (row_offset, col_offset)

    arrays = [linear(object_field), linear(illumination), amplitudes, split_tables(window)]
    wanted = [shifted(scalar, "tile", 1).reshape(1, 2) for scalar in scalars]
    obj, ill, amps, table = loaded(arrays)
    (rim,) = kernel_call(functools.partial(rim_kernel, window), "rim", [(2, window, window)], (), [*wanted, obj])
    rim = shifted(rim, "tile", -1)

    def spread(pieces):
        moved = {d: exchanged(pieces[d], "pos", d) for d in range(1, classes)}
        return [pieces[0]] + [moved[d] for d in range(1, classes)]

    roll, state, work = scratch_of(window)
    near = spread(
        kernel_call(
            functools.partial(first_wave_kernel, window, classes),
            "wave0",
            [(2 * share + 8, window)] * classes,
            scalars,
            [obj, ill, amps, table],
            roll + state + work,
            48 * window**3,
        )
    )
    with jax.named_scope("start"):
        probe, ordered, exits = kernel_call(
            functools.partial(second_start_kernel, window),
            "start1",
            [(2, window, window), (window, window), (2, window, window)],
            scalars,
            [obj, ill, amps],
            roll,
        )
    (acc,) = kernel_call(
        functools.partial(first_sum_kernel, window, classes), "sum0", [(2, 2, share, columns)], (), near
    )
    late = spread(
        kernel_call(
            functools.partial(second_wave_kernel, window, classes),
            "wave1",
            [(2 * share, window)] * classes,
            scalars,
            [probe, ordered, exits, table, rim],
            work,
            48 * window**3,
        )
    )
    sums = kernel_call(
        functools.partial(second_sum_kernel, window, classes),
        "sum1",
        [(4 * share, LANES)] * (3 * tiles),
        (),
        [acc, *near, *late],
    )
    is_upper = lax.axis_index("pos") >= classes
    kept, received = [], []
    for chunk in range(tiles):
        top, middle, spilled = sums[3 * chunk : 3 * chunk + 3]
        with jax.named_scope("spill_" + str(chunk)):
            top = top + shifted(spilled, "tile", 1)
        outgoing = jnp.where(is_upper, top, middle)
        with jax.named_scope("halves_" + str(chunk)):
            received.append(exchanged(outgoing, "pos", classes))
        kept.append(jnp.where(is_upper, middle, top))
    result = pl.pallas_call(
        functools.partial(final_kernel, tiles, share),
        out_shape=jax.ShapeDtypeStruct((share * 4 * tiles, LANES), F32),
        in_specs=[pl.BlockSpec(memory_space=pltpu.VMEM)] * (2 * tiles),
        out_specs=pl.BlockSpec(memory_space=pltpu.VMEM),
        compiler_params=pltpu.CompilerParams(vmem_limit_bytes=16 << 20),
        name="final",
    )(*[in_vmem(array) for array in kept + received])
    return unlinear(result, share, columns)


def solution(mesh):
    in_specs = (
        P("tile", None, None),
        P(),
        P(("tile", "pos"), None, None),
        P(("tile", "pos")),
        P(("tile", "pos")),
    )
    out_specs = P(("tile", "pos"), None, None)
    return jax.shard_map(
        on_device, mesh=mesh, in_specs=in_specs, out_specs=out_specs, check_vma=False
    )
```

```python
import functools
import math

import jax
import jax.numpy as jnp
import numpy as np
from jax import lax
from jax.experimental import pallas as pl
from jax.experimental.pallas import tpu as pltpu
from jax.sharding import PartitionSpec as P

LANES = 128
F32 = jnp.float32
BF16 = jnp.bfloat16


def shifted(block, axis, distance):
    devices = lax.axis_size(axis)
    return lax.ppermute(block, axis, [((i - distance) % devices, i) for i in range(devices)])


def exchanged(block, axis, flip):
    return lax.ppermute(block, axis, [(i, i ^ flip) for i in range(lax.axis_size(axis))])


def split_tables(length):
    half = length // 2
    n = np.arange(half, dtype=np.int64)
    even = 2 * n[:, None] * n[None, :]
    odd = n[:, None] * (2 * n[None, :] + 1)
    rows = []
    for product in (even, odd, odd.T):
        angles = (product % length) * (2.0 * math.pi / length)
        real, imag = np.cos(angles) / math.sqrt(length), -np.sin(angles) / math.sqrt(length)
        whole = np.concatenate([real, imag, -imag], axis=1)
        high = whole.astype(BF16)
        rows += [high, (whole - high.astype(np.float64)).astype(BF16)]
    return jnp.asarray(np.concatenate(rows, axis=0))


def linear(array):
    rows, parts, columns = array.shape
    tiles = columns // LANES
    return array.reshape(rows, parts, tiles, LANES).transpose(0, 2, 1, 3).reshape(rows * tiles * parts, LANES)


def unlinear(array, rows, columns):
    tiles = columns // LANES
    return array.reshape(rows, tiles, 2, LANES).transpose(0, 2, 1, 3).reshape(rows, 2, columns)


def halves(value):
    high = value.astype(BF16)
    return high, (value - high.astype(F32)).astype(BF16)


def dot3(high_left, low_left, high_right, low_right):
    left = jnp.concatenate([low_left, high_left, high_left], axis=1)
    right = jnp.concatenate([high_right, low_right, high_right], axis=0)
    return jnp.dot(left, right, preferred_element_type=F32)


def in_vmem(array):
    return pltpu.with_memory_space_constraint(array, pltpu.VMEM)


def kernel_call(body, name, out_shapes, scalars, arrays, scratch=(), flops=0):
    smem = pl.BlockSpec(memory_space=pltpu.SMEM)
    vmem = pl.BlockSpec(memory_space=pltpu.VMEM)
    moved = sum(4 * math.prod(shape) for shape in out_shapes)
    return pl.pallas_call(
        body,
        out_shape=[pltpu.VMEM(shape, F32) for shape in out_shapes],
        in_specs=[smem] * len(scalars) + [vmem] * len(arrays),
        out_specs=[vmem] * len(out_shapes),
        scratch_shapes=scratch,
        cost_estimate=pl.CostEstimate(flops=flops, transcendentals=0, bytes_accessed=2 * moved),
        compiler_params=pltpu.CompilerParams(vmem_limit_bytes=16 << 20),
        name=name,
    )(*[pltpu.with_memory_space_constraint(scalar, pltpu.HBM) for scalar in scalars], *[in_vmem(array) for array in arrays])


def chosen(slot, rows, cols, band_start, window):
    crossing = (rows[0] - band_start > window).astype(jnp.int32)
    index = crossing if slot == 0 else 1 - crossing
    return rows[index] - band_start, cols[index], index


def load_kernel(number, *refs):
    sources, targets, sem = refs[:number], refs[number : 2 * number], refs[2 * number]
    copies = [pltpu.make_async_copy(a, b, sem.at[i]) for i, (a, b) in enumerate(zip(sources, targets))]
    for copy in copies:
        copy.start()
    for copy in copies:
        copy.wait()


def loaded(arrays):
    return pl.pallas_call(
        functools.partial(load_kernel, len(arrays)),
        out_shape=[pltpu.VMEM(array.shape, array.dtype) for array in arrays],
        in_specs=[pl.BlockSpec(memory_space=pl.ANY)] * len(arrays),
        out_specs=[pl.BlockSpec(memory_space=pltpu.VMEM)] * len(arrays),
        scratch_shapes=[pltpu.SemaphoreType.DMA((len(arrays),))],
        compiler_params=pltpu.CompilerParams(vmem_limit_bytes=16 << 20),
        name="load",
    )(*[pltpu.with_memory_space_constraint(array, pltpu.HBM) for array in arrays])


def rim_kernel(window, rows, cols, obj, out):
    band_start = (lax.axis_index("tile") - 1) * (2 * window)
    crossing = rows[:, 0:1] - band_start > window
    offset = jnp.where(crossing, cols[:, 0:1], cols[:, 1:2])
    tiles = window // LANES
    for tile in range(tiles):
        column = lax.broadcasted_iota(jnp.int32, (window, LANES), 1) + tile * LANES
        for part in range(2):
            near = obj[pl.ds(tile * 2 + part, window, stride=4 * tiles), :]
            beyond = obj[pl.ds((tiles + tile) * 2 + part, window, stride=4 * tiles), :]
            out[part, :, pl.ds(tile * LANES, LANES)] = jnp.where(column < offset, beyond, near)


def prepare(slot, window, rows, cols, obj, ill, amps, doubled, probe, ordered, emit):
    tiles = window // LANES
    half = window // 2
    row, column, index = chosen(slot, rows, cols, lax.axis_index("tile") * (2 * window), window)
    size = 32
    step = 2 * tiles
    whole = window * step
    doubled[pl.ds(0, whole), :] = ill[...]
    doubled[pl.ds(whole, size * step), :] = ill[pl.ds(0, size * step), :]
    turn = lax.rem(row, window)

    below = lax.broadcasted_iota(jnp.int32, (window, window), 0)
    beside = lax.broadcasted_iota(jnp.int32, (window, window), 1)

    def picks(frequency, place):
        wanted = jnp.where(place < half, 2 * place, 2 * (place - half) + 1)
        return jnp.where(frequency == wanted, 1.0, 0.0).astype(BF16)

    by_column = jnp.dot(amps[index], picks(below, beside), preferred_element_type=F32).astype(BF16)
    ordered[...] = jnp.dot(picks(beside, below), by_column, preferred_element_type=F32)

    for first in range(0, window, size):
        place = lax.broadcasted_iota(jnp.int32, (size, window), 0) + first
        across = lax.broadcasted_iota(jnp.int32, (size, window), 1)
        start = lax.rem(first + window - turn, window) * step
        pair = []
        for part in range(2):
            rolled = jnp.concatenate(
                [doubled[pl.ds(start + tile * 2 + part, size, stride=step), :] for tile in range(tiles)],
                axis=1,
            )
            rolled = pltpu.roll(rolled, column, 1)
            probe[part, pl.ds(first, size), :] = rolled

            def block(base):
                def tile_at(tile):
                    return obj[pl.ds((base + first) * 2 * step + tile * 2 + part, size, stride=2 * step), :]

                near = jnp.concatenate([tile_at(t) for t in range(tiles)], axis=1)
                beyond = jnp.concatenate([tile_at(t + tiles) for t in range(tiles)], axis=1)
                return jnp.where(across < column, beyond, near)

            pair.append((rolled, jnp.where(place < row, block(window), block(0))))
        emit(first, size, product(*pair))


def product(real_pair, imag_pair):
    (probe_real, obj_real), (probe_imag, obj_imag) = real_pair, imag_pair
    return (
        probe_real * obj_real - probe_imag * obj_imag,
        probe_real * obj_imag + probe_imag * obj_real,
    )


def keep(high_ref, low_ref, here, across, value):
    high, low = halves(value)
    high_ref[here, across] = high
    low_ref[here, across] = low


def keep_exit(xh, xl, first, size, exits):
    here = pl.ds(first, size)
    window = exits[0].shape[1]
    half = window // 2
    for part, value in enumerate(exits):
        left, right = value[:, :half], value[:, half:]
        keep(xh, xl, here, pl.ds(part * half, half), left + right)
        keep(xh, xl, here, pl.ds(window + part * half, half), left - right)


def transforms(window, classes, table, probe, ordered, xh, xl, yh, yl, far, outs):
    half = window // 2
    own = lax.rem(lax.axis_index("pos"), classes)
    size = 32

    def block_of(matrix, part, low):
        return table[pl.ds((2 * matrix + low) * half, half), pl.ds(part * half, half)]

    def factor(matrix, order):
        return [
            jnp.concatenate(
                [
                    jnp.concatenate([block_of(matrix, part, low) for part in line], axis=1)
                    for line in order
                ],
                axis=0,
            )
            for low in range(2)
        ]

    def from_right(first, matrix):
        across = pl.ds(first, window)
        return dot3(xh[:, across], xl[:, across], *factor(matrix, ((0, 1), (2, 0))))

    def from_left(matrix, first):
        down = pl.ds(first, window)
        return dot3(*factor(matrix, ((0, 2), (1, 0))), yh[down, :], yl[down, :])

    for parity in range(2):
        mid = from_right(parity * window, parity)
        across = pl.ds(parity * half, half)
        for first in range(0, half, size):
            top, bottom = mid[first : first + size], mid[half + first : half + first + size]
            for line, value in enumerate((top + bottom, top - bottom)):
                for part in range(2):
                    here = pl.ds((2 * line + part) * half + first, size)
                    keep(yh, yl, here, across, value[:, part * half : (part + 1) * half])
    far[pl.ds(0, window), :] = from_left(0, 0)
    far[pl.ds(window, window), :] = from_left(2, window)

    for parity in range(2):
        for first in range(0, half, size):
            real = far[pl.ds(parity * window + first, size), :]
            imag = far[pl.ds(parity * window + half + first, size), :]
            here = pl.ds(parity * half + first, size)
            inverse = jnp.minimum(lax.rsqrt(real * real + imag * imag), 4.0)
            scaled = ordered[here, :] * inverse
            for part, value in enumerate((real * (1.0 - scaled), imag * (scaled - 1.0))):
                for side in range(2):
                    across = pl.ds(side * window + part * half, half)
                    keep(xh, xl, here, across, value[:, side * half : (side + 1) * half])

    even, odd = from_right(0, 0), from_right(window, 2)
    for first in range(0, window, size):
        near, beyond = even[first : first + size], odd[first : first + size]
        parity, place = first // half, first % half
        for side, value in enumerate((near + beyond, near - beyond)):
            for part in range(2):
                here = pl.ds((2 * parity + part) * half + place, size)
                keep(yh, yl, here, pl.ds(side * half, half), value[:, part * half : (part + 1) * half])
    far[pl.ds(0, window), :] = from_left(0, 0)
    far[pl.ds(window, window), :] = from_left(1, window)

    share = window // classes
    for flip in range(classes):
        base = pl.multiple_of((own ^ flip) * share, share)
        place = pl.multiple_of(lax.rem(base, half), share)
        sign = jnp.where(base < half, 1.0, -1.0)
        real, imag = (
            far[pl.ds(part * half + place, share), :] + sign * far[pl.ds(window + part * half + place, share), :]
            for part in range(2)
        )
        here = pl.ds(base, share)
        probe_real = probe[0, here, :]
        probe_imag = probe[1, here, :]
        outs[flip][pl.ds(0, share), :] = probe_real * real - probe_imag * imag
        outs[flip][pl.ds(share, share), :] = -(probe_real * imag + probe_imag * real)


def first_wave_kernel(window, classes, rows, cols, obj, ill, amps, table, *refs):
    outs = refs[:classes]
    doubled, probe, ordered, xh, xl, yh, yl, far = refs[classes:]
    emit = functools.partial(keep_exit, xh, xl)
    prepare(0, window, rows, cols, obj, ill, amps, doubled, probe, ordered, emit)
    transforms(window, classes, table, probe, ordered, xh, xl, yh, yl, far, outs)
    share = window // classes
    line = lax.broadcasted_iota(jnp.int32, (8, window), 0)
    head = jnp.zeros((8, window), jnp.int32)
    for slot in range(2):
        row, column, _ = chosen(slot, rows, cols, lax.axis_index("tile") * (2 * window), window)
        head = jnp.where(line == 2 * slot, row, jnp.where(line == 2 * slot + 1, column, head))
    for out in outs:
        out[pl.ds(2 * share, 8), :] = head.astype(F32)


def second_start_kernel(window, rows, cols, obj, ill, amps, probe, ordered, exits, doubled):
    def emit(first, size, values):
        for part in range(2):
            exits[part, pl.ds(first, size), :] = values[part]

    prepare(1, window, rows, cols, obj, ill, amps, doubled, probe, ordered, emit)


def second_wave_kernel(window, classes, rows, cols, probe, ordered, exits, table, rim, *refs):
    outs = refs[:classes]
    xh, xl, yh, yl, far = refs[classes:]
    row, _, _ = chosen(1, rows, cols, lax.axis_index("tile") * (2 * window), window)
    size = 32
    for first in range(0, window, size):
        here = pl.ds(first, size)
        beyond = lax.broadcasted_iota(jnp.int32, (size, window), 0) + (first + window) < row
        edge = product(*[(probe[part, here, :], rim[part, here, :]) for part in range(2)])
        values = [jnp.where(beyond, edge[part], exits[part, here, :]) for part in range(2)]
        keep_exit(xh, xl, first, size, values)
    transforms(window, classes, table, probe, ordered, xh, xl, yh, yl, far, outs)


def scratch_of(window):
    tiles = window // LANES
    roll = [pltpu.VMEM(((window + 32) * 2 * tiles + 8, LANES), F32)]
    state = [pltpu.VMEM((2, window, window), F32), pltpu.VMEM((window, window), F32)]
    work = [
        pltpu.VMEM((window, 2 * window), BF16),
        pltpu.VMEM((window, 2 * window), BF16),
        pltpu.VMEM((2 * window, window), BF16),
        pltpu.VMEM((2 * window, window), BF16),
        pltpu.VMEM((2 * window, window), F32),
    ]
    return roll, state, work


def placed(slot, piece, own, share, window):
    row = piece[pl.ds(2 * share + 2 * slot, 1), :]
    column = piece[pl.ds(2 * share + 2 * slot + 1, 1), :]
    place = (lax.broadcasted_iota(jnp.int32, (share, window), 0) + own * share).astype(F32)
    across = lax.broadcasted_iota(jnp.int32, (share, window), 1).astype(F32)
    return across < column, place < row, place + float(window) < row


def first_sum_kernel(window, classes, *refs):
    pieces, acc = refs[:classes], refs[classes]
    share = window // classes
    own = lax.rem(lax.axis_index("pos"), classes)
    for part in range(2):
        total = [[jnp.zeros((share, window), F32) for _ in range(2)] for _ in range(2)]
        for piece in pieces:
            upper, below, _ = placed(0, piece, own, share, window)
            value = piece[pl.ds(part * share, share), :]
            for k, wanted in enumerate((~below, below)):
                kept = jnp.where(wanted, value, 0.0)
                total[k][0] += jnp.where(upper, 0.0, kept)
                total[k][1] += jnp.where(upper, kept, 0.0)
        for k in range(2):
            for half in range(2):
                acc[k, part, :, pl.ds(half * window, window)] = total[k][half]


def second_sum_kernel(window, classes, acc, *refs):
    heads, pieces, outs = refs[:classes], refs[classes : 2 * classes], refs[2 * classes :]
    share = window // classes
    tiles = window // LANES
    own = lax.rem(lax.axis_index("pos"), classes)
    for part in range(2):
        total = [[acc[k, part, :, pl.ds(h * window, window)] for h in range(2)] for k in range(2)]
        total.append([jnp.zeros((share, window), F32) for _ in range(2)])
        for head, piece in zip(heads, pieces):
            upper, below, lowest = placed(1, head, own, share, window)
            value = piece[pl.ds(part * share, share), :]
            for k, wanted in enumerate((~below, below & ~lowest, lowest)):
                kept = jnp.where(wanted, value, 0.0)
                total[k][0] += jnp.where(upper, 0.0, kept)
                total[k][1] += jnp.where(upper, kept, 0.0)
        for k in range(3):
            for half in range(2):
                for tile in range(tiles):
                    outs[3 * tile + k][pl.ds((half * 2 + part) * share, share), :] = total[k][half][
                        :, tile * LANES : (tile + 1) * LANES
                    ]


def final_kernel(tiles, share, *refs):
    kept, received, out = refs[:tiles], refs[tiles : 2 * tiles], refs[2 * tiles]
    for tile in range(tiles):
        for half in range(2):
            for part in range(2):
                here = pl.ds((half * 2 + part) * share, share)
                line = (half * tiles + tile) * 2 + part
                out[pl.ds(line, share, stride=4 * tiles), :] = kept[tile][here, :] + received[tile][here, :]


def on_device(object_field, illumination, amplitudes, row_offset, col_offset):
    band_rows, _, columns = object_field.shape
    window = illumination.shape[0]
    ways = lax.axis_size("pos")
    assert band_rows == 2 * window and columns == 2 * window and row_offset.shape[0] == 2
    classes = ways // 2
    share = window // classes
    tiles = window // LANES
    scalars = (row_offset, col_offset)

    arrays = [linear(object_field), linear(illumination), amplitudes, split_tables(window)]
    wanted = [shifted(scalar, "tile", 1).reshape(1, 2) for scalar in scalars]
    obj, ill, amps, table = loaded(arrays)
    (rim,) = kernel_call(functools.partial(rim_kernel, window), "rim", [(2, window, window)], (), [*wanted, obj])
    rim = shifted(rim, "tile", -1)

    def spread(pieces):
        moved = {d: exchanged(pieces[d], "pos", d) for d in range(1, classes)}
        return [pieces[0]] + [moved[d] for d in range(1, classes)]

    roll, state, work = scratch_of(window)
    near = spread(
        kernel_call(
            functools.partial(first_wave_kernel, window, classes),
            "wave0",
            [(2 * share + 8, window)] * classes,
            scalars,
            [obj, ill, amps, table],
            roll + state + work,
            48 * window**3,
        )
    )
    with jax.named_scope("start"):
        probe, ordered, exits = kernel_call(
            functools.partial(second_start_kernel, window),
            "start1",
            [(2, window, window), (window, window), (2, window, window)],
            scalars,
            [obj, ill, amps],
            roll,
        )
    (acc,) = kernel_call(
        functools.partial(first_sum_kernel, window, classes), "sum0", [(2, 2, share, columns)], (), near
    )
    late = spread(
        kernel_call(
            functools.partial(second_wave_kernel, window, classes),
            "wave1",
            [(2 * share, window)] * classes,
            scalars,
            [probe, ordered, exits, table, rim],
            work,
            48 * window**3,
        )
    )
    sums = kernel_call(
        functools.partial(second_sum_kernel, window, classes),
        "sum1",
        [(4 * share, LANES)] * (3 * tiles),
        (),
        [acc, *near, *late],
    )
    is_upper = lax.axis_index("pos") >= classes
    kept, received = [], []
    for chunk in range(tiles):
        top, middle, spilled = sums[3 * chunk : 3 * chunk + 3]
        with jax.named_scope("spill_" + str(chunk)):
            top = top + shifted(spilled, "tile", 1)
        outgoing = jnp.where(is_upper, top, middle)
        with jax.named_scope("halves_" + str(chunk)):
            received.append(exchanged(outgoing, "pos", classes))
        kept.append(jnp.where(is_upper, middle, top))
    result = pl.pallas_call(
        functools.partial(final_kernel, tiles, share),
        out_shape=jax.ShapeDtypeStruct((share * 4 * tiles, LANES), F32),
        in_specs=[pl.BlockSpec(memory_space=pltpu.VMEM)] * (2 * tiles),
        out_specs=pl.BlockSpec(memory_space=pltpu.VMEM),
        compiler_params=pltpu.CompilerParams(vmem_limit_bytes=16 << 20),
        name="final",
    )(*[in_vmem(array) for array in kept + received])
    return unlinear(result, share, columns)


def solution(mesh):
    in_specs = (
        P("tile", None, None),
        P(),
        P(("tile", "pos"), None, None),
        P(("tile", "pos")),
        P(("tile", "pos")),
    )
    out_specs = P(("tile", "pos"), None, None)
    return jax.shard_map(
        on_device, mesh=mesh, in_specs=in_specs, out_specs=out_specs, check_vma=False
    )
```

```python
import functools
import math

import jax
import jax.numpy as jnp
import numpy as np
from jax import lax
from jax.experimental import pallas as pl
from jax.experimental.pallas import tpu as pltpu
from jax.sharding import PartitionSpec as P

LANES = 128
F32 = jnp.float32
BF16 = jnp.bfloat16


def shifted(block, axis, distance):
    devices = lax.axis_size(axis)
    return lax.ppermute(block, axis, [((i - distance) % devices, i) for i in range(devices)])


def exchanged(block, axis, flip):
    return lax.ppermute(block, axis, [(i, i ^ flip) for i in range(lax.axis_size(axis))])


def split_tables(length):
    half = length // 2
    n = np.arange(half, dtype=np.int64)
    even = 2 * n[:, None] * n[None, :]
    odd = n[:, None] * (2 * n[None, :] + 1)
    rows = []
    for product in (even, odd, odd.T):
        angles = (product % length) * (2.0 * math.pi / length)
        real, imag = np.cos(angles) / math.sqrt(length), -np.sin(angles) / math.sqrt(length)
        whole = np.concatenate([real, imag, -imag], axis=1)
        high = whole.astype(BF16)
        rows += [high, (whole - high.astype(np.float64)).astype(BF16)]
    return jnp.asarray(np.concatenate(rows, axis=0))


def linear(array):
    rows, parts, columns = array.shape
    tiles = columns // LANES
    return array.reshape(rows, parts, tiles, LANES).transpose(0, 2, 1, 3).reshape(rows * tiles * parts, LANES)


def unlinear(array, rows, columns):
    tiles = columns // LANES
    return array.reshape(rows, tiles, 2, LANES).transpose(0, 2, 1, 3).reshape(rows, 2, columns)


def halves(value):
    high = value.astype(BF16)
    return high, (value - high.astype(F32)).astype(BF16)


def dot3(high_left, low_left, high_right, low_right):
    left = jnp.concatenate([low_left, high_left, high_left], axis=1)
    right = jnp.concatenate([high_right, low_right, high_right], axis=0)
    return jnp.dot(left, right, preferred_element_type=F32)


def in_vmem(array):
    return pltpu.with_memory_space_constraint(array, pltpu.VMEM)


def kernel_call(body, name, out_shapes, scalars, arrays, scratch=(), flops=0):
    smem = pl.BlockSpec(memory_space=pltpu.SMEM)
    vmem = pl.BlockSpec(memory_space=pltpu.VMEM)
    moved = sum(4 * math.prod(shape) for shape in out_shapes)
    return pl.pallas_call(
        body,
        out_shape=[pltpu.VMEM(shape, F32) for shape in out_shapes],
        in_specs=[smem] * len(scalars) + [vmem] * len(arrays),
        out_specs=[vmem] * len(out_shapes),
        scratch_shapes=scratch,
        cost_estimate=pl.CostEstimate(flops=flops, transcendentals=0, bytes_accessed=2 * moved),
        compiler_params=pltpu.CompilerParams(vmem_limit_bytes=16 << 20),
        name=name,
    )(*scalars, *[in_vmem(array) for array in arrays])


def chosen(slot, rows, cols, band_start, window):
    crossing = (rows[0] - band_start > window).astype(jnp.int32)
    index = crossing if slot == 0 else 1 - crossing
    return rows[index] - band_start, cols[index], index


def load_kernel(number, *refs):
    sources, targets, sem = refs[:number], refs[number : 2 * number], refs[2 * number]
    copies = [pltpu.make_async_copy(a, b, sem.at[i]) for i, (a, b) in enumerate(zip(sources, targets))]
    for copy in copies:
        copy.start()
    for copy in copies:
        copy.wait()


def loaded(arrays):
    return pl.pallas_call(
        functools.partial(load_kernel, len(arrays)),
        out_shape=[pltpu.VMEM(array.shape, array.dtype) for array in arrays],
        in_specs=[pl.BlockSpec(memory_space=pl.ANY)] * len(arrays),
        out_specs=[pl.BlockSpec(memory_space=pltpu.VMEM)] * len(arrays),
        scratch_shapes=[pltpu.SemaphoreType.DMA((len(arrays),))],
        compiler_params=pltpu.CompilerParams(vmem_limit_bytes=16 << 20),
        name="load",
    )(*[pltpu.with_memory_space_constraint(array, pltpu.HBM) for array in arrays])


def rim_kernel(window, rows, cols, obj, out):
    band_start = (lax.axis_index("tile") - 1) * (2 * window)
    crossing = rows[:, 0:1] - band_start > window
    offset = jnp.where(crossing, cols[:, 0:1], cols[:, 1:2])
    tiles = window // LANES
    for tile in range(tiles):
        column = lax.broadcasted_iota(jnp.int32, (window, LANES), 1) + tile * LANES
        for part in range(2):
            near = obj[pl.ds(tile * 2 + part, window, stride=4 * tiles), :]
            beyond = obj[pl.ds((tiles + tile) * 2 + part, window, stride=4 * tiles), :]
            out[part, :, pl.ds(tile * LANES, LANES)] = jnp.where(column < offset, beyond, near)


def prepare(slot, window, rows, cols, obj, ill, amps, doubled, probe, ordered, emit):
    tiles = window // LANES
    half = window // 2
    row, column, index = chosen(slot, rows, cols, lax.axis_index("tile") * (2 * window), window)
    size = 32
    step = 2 * tiles
    whole = window * step
    doubled[pl.ds(0, whole), :] = ill[...]
    doubled[pl.ds(whole, size * step), :] = ill[pl.ds(0, size * step), :]
    turn = lax.rem(row, window)

    below = lax.broadcasted_iota(jnp.int32, (window, window), 0)
    beside = lax.broadcasted_iota(jnp.int32, (window, window), 1)

    def picks(frequency, place):
        wanted = jnp.where(place < half, 2 * place, 2 * (place - half) + 1)
        return jnp.where(frequency == wanted, 1.0, 0.0).astype(BF16)

    by_column = jnp.dot(amps[index], picks(below, beside), preferred_element_type=F32).astype(BF16)
    ordered[...] = jnp.dot(picks(beside, below), by_column, preferred_element_type=F32)

    for first in range(0, window, size):
        place = lax.broadcasted_iota(jnp.int32, (size, window), 0) + first
        across = lax.broadcasted_iota(jnp.int32, (size, window), 1)
        start = lax.rem(first + window - turn, window) * step
        pair = []
        for part in range(2):
            rolled = jnp.concatenate(
                [doubled[pl.ds(start + tile * 2 + part, size, stride=step), :] for tile in range(tiles)],
                axis=1,
            )
            rolled = pltpu.roll(rolled, column, 1)
            probe[part, pl.ds(first, size), :] = rolled

            def block(base):
                def tile_at(tile):
                    return obj[pl.ds((base + first) * 2 * step + tile * 2 + part, size, stride=2 * step), :]

                near = jnp.concatenate([tile_at(t) for t in range(tiles)], axis=1)
                beyond = jnp.concatenate([tile_at(t + tiles) for t in range(tiles)], axis=1)
                return jnp.where(across < column, beyond, near)

            pair.append((rolled, jnp.where(place < row, block(window), block(0))))
        emit(first, size, product(*pair))


def product(real_pair, imag_pair):
    (probe_real, obj_real), (probe_imag, obj_imag) = real_pair, imag_pair
    return (
        probe_real * obj_real - probe_imag * obj_imag,
        probe_real * obj_imag + probe_imag * obj_real,
    )


def keep(high_ref, low_ref, here, across, value):
    high, low = halves(value)
    high_ref[here, across] = high
    low_ref[here, across] = low


def keep_exit(xh, xl, first, size, exits):
    here = pl.ds(first, size)
    window = exits[0].shape[1]
    half = window // 2
    for part, value in enumerate(exits):
        left, right = value[:, :half], value[:, half:]
        keep(xh, xl, here, pl.ds(part * half, half), left + right)
        keep(xh, xl, here, pl.ds(window + part * half, half), left - right)


def transforms(window, classes, table, probe, ordered, xh, xl, yh, yl, far, outs):
    half = window // 2
    own = lax.rem(lax.axis_index("pos"), classes)
    size = 32

    def block_of(matrix, part, low):
        return table[pl.ds((2 * matrix + low) * half, half), pl.ds(part * half, half)]

    def factor(matrix, order):
        return [
            jnp.concatenate(
                [
                    jnp.concatenate([block_of(matrix, part, low) for part in line], axis=1)
                    for line in order
                ],
                axis=0,
            )
            for low in range(2)
        ]

    def from_right(first, matrix):
        across = pl.ds(first, window)
        return dot3(xh[:, across], xl[:, across], *factor(matrix, ((0, 1), (2, 0))))

    def from_left(matrix, first):
        down = pl.ds(first, window)
        return dot3(*factor(matrix, ((0, 2), (1, 0))), yh[down, :], yl[down, :])

    for parity in range(2):
        mid = from_right(parity * window, parity)
        across = pl.ds(parity * half, half)
        for first in range(0, half, size):
            top, bottom = mid[first : first + size], mid[half + first : half + first + size]
            for line, value in enumerate((top + bottom, top - bottom)):
                for part in range(2):
                    here = pl.ds((2 * line + part) * half + first, size)
                    keep(yh, yl, here, across, value[:, part * half : (part + 1) * half])
    far[pl.ds(0, window), :] = from_left(0, 0)
    far[pl.ds(window, window), :] = from_left(2, window)

    for parity in range(2):
        for first in range(0, half, size):
            real = far[pl.ds(parity * window + first, size), :]
            imag = far[pl.ds(parity * window + half + first, size), :]
            here = pl.ds(parity * half + first, size)
            inverse = jnp.minimum(lax.rsqrt(real * real + imag * imag), 4.0)
            scaled = ordered[here, :] * inverse
            for part, value in enumerate((real * (1.0 - scaled), imag * (scaled - 1.0))):
                for side in range(2):
                    across = pl.ds(side * window + part * half, half)
                    keep(xh, xl, here, across, value[:, side * half : (side + 1) * half])

    even, odd = from_right(0, 0), from_right(window, 2)
    for first in range(0, window, size):
        near, beyond = even[first : first + size], odd[first : first + size]
        parity, place = first // half, first % half
        for side, value in enumerate((near + beyond, near - beyond)):
            for part in range(2):
                here = pl.ds((2 * parity + part) * half + place, size)
                keep(yh, yl, here, pl.ds(side * half, half), value[:, part * half : (part + 1) * half])
    far[pl.ds(0, window), :] = from_left(0, 0)
    far[pl.ds(window, window), :] = from_left(1, window)

    share = window // classes
    for flip in range(classes):
        base = pl.multiple_of((own ^ flip) * share, share)
        place = pl.multiple_of(lax.rem(base, half), share)
        sign = jnp.where(base < half, 1.0, -1.0)
        real, imag = (
            far[pl.ds(part * half + place, share), :] + sign * far[pl.ds(window + part * half + place, share), :]
            for part in range(2)
        )
        here = pl.ds(base, share)
        probe_real = probe[0, here, :]
        probe_imag = probe[1, here, :]
        outs[flip][pl.ds(0, share), :] = probe_real * real - probe_imag * imag
        outs[flip][pl.ds(share, share), :] = -(probe_real * imag + probe_imag * real)


def first_wave_kernel(window, classes, rows, cols, obj, ill, amps, table, *refs):
    outs = refs[:classes]
    doubled, probe, ordered, xh, xl, yh, yl, far = refs[classes:]
    emit = functools.partial(keep_exit, xh, xl)
    prepare(0, window, rows, cols, obj, ill, amps, doubled, probe, ordered, emit)
    transforms(window, classes, table, probe, ordered, xh, xl, yh, yl, far, outs)
    share = window // classes
    line = lax.broadcasted_iota(jnp.int32, (8, window), 0)
    head = jnp.zeros((8, window), jnp.int32)
    for slot in range(2):
        row, column, _ = chosen(slot, rows, cols, lax.axis_index("tile") * (2 * window), window)
        head = jnp.where(line == 2 * slot, row, jnp.where(line == 2 * slot + 1, column, head))
    for out in outs:
        out[pl.ds(2 * share, 8), :] = head.astype(F32)


def second_start_kernel(window, rows, cols, obj, ill, amps, probe, ordered, exits, doubled):
    def emit(first, size, values):
        for part in range(2):
            exits[part, pl.ds(first, size), :] = values[part]

    prepare(1, window, rows, cols, obj, ill, amps, doubled, probe, ordered, emit)


def second_wave_kernel(window, classes, rows, cols, probe, ordered, exits, table, rim, *refs):
    outs = refs[:classes]
    xh, xl, yh, yl, far = refs[classes:]
    row, _, _ = chosen(1, rows, cols, lax.axis_index("tile") * (2 * window), window)
    size = 32
    for first in range(0, window, size):
        here = pl.ds(first, size)
        beyond = lax.broadcasted_iota(jnp.int32, (size, window), 0) + (first + window) < row
        edge = product(*[(probe[part, here, :], rim[part, here, :]) for part in range(2)])
        values = [jnp.where(beyond, edge[part], exits[part, here, :]) for part in range(2)]
        keep_exit(xh, xl, first, size, values)
    transforms(window, classes, table, probe, ordered, xh, xl, yh, yl, far, outs)


def scratch_of(window):
    tiles = window // LANES
    roll = [pltpu.VMEM(((window + 32) * 2 * tiles + 8, LANES), F32)]
    state = [pltpu.VMEM((2, window, window), F32), pltpu.VMEM((window, window), F32)]
    work = [
        pltpu.VMEM((window, 2 * window), BF16),
        pltpu.VMEM((window, 2 * window), BF16),
        pltpu.VMEM((2 * window, window), BF16),
        pltpu.VMEM((2 * window, window), BF16),
        pltpu.VMEM((2 * window, window), F32),
    ]
    return roll, state, work


def placed(slot, piece, own, share, window):
    row = piece[pl.ds(2 * share + 2 * slot, 1), :]
    column = piece[pl.ds(2 * share + 2 * slot + 1, 1), :]
    place = (lax.broadcasted_iota(jnp.int32, (share, window), 0) + own * share).astype(F32)
    across = lax.broadcasted_iota(jnp.int32, (share, window), 1).astype(F32)
    return across < column, place < row, place + float(window) < row


def first_sum_kernel(window, classes, *refs):
    pieces, acc = refs[:classes], refs[classes]
    share = window // classes
    own = lax.rem(lax.axis_index("pos"), classes)
    for part in range(2):
        total = [[jnp.zeros((share, window), F32) for _ in range(2)] for _ in range(2)]
        for piece in pieces:
            upper, below, _ = placed(0, piece, own, share, window)
            value = piece[pl.ds(part * share, share), :]
            for k, wanted in enumerate((~below, below)):
                kept = jnp.where(wanted, value, 0.0)
                total[k][0] += jnp.where(upper, 0.0, kept)
                total[k][1] += jnp.where(upper, kept, 0.0)
        for k in range(2):
            for half in range(2):
                acc[k, part, :, pl.ds(half * window, window)] = total[k][half]


def second_sum_kernel(window, classes, acc, *refs):
    heads, pieces, outs = refs[:classes], refs[classes : 2 * classes], refs[2 * classes :]
    share = window // classes
    tiles = window // LANES
    own = lax.rem(lax.axis_index("pos"), classes)
    for part in range(2):
        total = [[acc[k, part, :, pl.ds(h * window, window)] for h in range(2)] for k in range(2)]
        total.append([jnp.zeros((share, window), F32) for _ in range(2)])
        for head, piece in zip(heads, pieces):
            upper, below, lowest = placed(1, head, own, share, window)
            value = piece[pl.ds(part * share, share), :]
            for k, wanted in enumerate((~below, below & ~lowest, lowest)):
                kept = jnp.where(wanted, value, 0.0)
                total[k][0] += jnp.where(upper, 0.0, kept)
                total[k][1] += jnp.where(upper, kept, 0.0)
        for k in range(3):
            for half in range(2):
                for tile in range(tiles):
                    outs[3 * tile + k][pl.ds((half * 2 + part) * share, share), :] = total[k][half][
                        :, tile * LANES : (tile + 1) * LANES
                    ]


def final_kernel(tiles, share, *refs):
    kept, received, out = refs[:tiles], refs[tiles : 2 * tiles], refs[2 * tiles]
    for tile in range(tiles):
        for half in range(2):
            for part in range(2):
                here = pl.ds((half * 2 + part) * share, share)
                line = (half * tiles + tile) * 2 + part
                out[pl.ds(line, share, stride=4 * tiles), :] = kept[tile][here, :] + received[tile][here, :]


def on_device(object_field, illumination, amplitudes, row_offset, col_offset):
    band_rows, _, columns = object_field.shape
    window = illumination.shape[0]
    ways = lax.axis_size("pos")
    assert band_rows == 2 * window and columns == 2 * window and row_offset.shape[0] == 2
    classes = ways // 2
    share = window // classes
    tiles = window // LANES
    scalars = (row_offset, col_offset)

    arrays = [linear(object_field), linear(illumination), amplitudes, split_tables(window)]
    wanted = [shifted(scalar, "tile", 1).reshape(1, 2) for scalar in scalars]
    obj, ill, amps, table = loaded(arrays)
    (rim,) = kernel_call(functools.partial(rim_kernel, window), "rim", [(2, window, window)], (), [*wanted, obj])
    rim = shifted(rim, "tile", -1)

    def spread(pieces):
        moved = {d: exchanged(pieces[d], "pos", d) for d in (*range(1, classes, 2), *range(2, classes, 2))}
        return [pieces[0]] + [moved[d] for d in range(1, classes)]

    roll, state, work = scratch_of(window)
    near = spread(
        kernel_call(
            functools.partial(first_wave_kernel, window, classes),
            "wave0",
            [(2 * share + 8, window)] * classes,
            scalars,
            [obj, ill, amps, table],
            roll + state + work,
            48 * window**3,
        )
    )
    with jax.named_scope("start"):
        probe, ordered, exits = kernel_call(
            functools.partial(second_start_kernel, window),
            "start1",
            [(2, window, window), (window, window), (2, window, window)],
            scalars,
            [obj, ill, amps],
            roll,
        )
    (acc,) = kernel_call(
        functools.partial(first_sum_kernel, window, classes), "sum0", [(2, 2, share, columns)], (), near
    )
    late = spread(
        kernel_call(
            functools.partial(second_wave_kernel, window, classes),
            "wave1",
            [(2 * share, window)] * classes,
            scalars,
            [probe, ordered, exits, table, rim],
            work,
            48 * window**3,
        )
    )
    sums = kernel_call(
        functools.partial(second_sum_kernel, window, classes),
        "sum1",
        [(4 * share, LANES)] * (3 * tiles),
        (),
        [acc, *near, *late],
    )
    is_upper = lax.axis_index("pos") >= classes
    kept, received = [], []
    for chunk in range(tiles):
        top, middle, spilled = sums[3 * chunk : 3 * chunk + 3]
        with jax.named_scope("spill_" + str(chunk)):
            top = top + shifted(spilled, "tile", 1)
        outgoing = jnp.where(is_upper, top, middle)
        with jax.named_scope("halves_" + str(chunk)):
            received.append(exchanged(outgoing, "pos", classes))
        kept.append(jnp.where(is_upper, middle, top))
    result = pl.pallas_call(
        functools.partial(final_kernel, tiles, share),
        out_shape=jax.ShapeDtypeStruct((share * 4 * tiles, LANES), F32),
        in_specs=[pl.BlockSpec(memory_space=pltpu.VMEM)] * (2 * tiles),
        out_specs=pl.BlockSpec(memory_space=pltpu.VMEM),
        compiler_params=pltpu.CompilerParams(vmem_limit_bytes=16 << 20),
        name="final",
    )(*[in_vmem(array) for array in kept + received])
    return unlinear(result, share, columns)


def solution(mesh):
    in_specs = (
        P("tile", None, None),
        P(),
        P(("tile", "pos"), None, None),
        P(("tile", "pos")),
        P(("tile", "pos")),
    )
    out_specs = P(("tile", "pos"), None, None)
    return jax.shard_map(
        on_device, mesh=mesh, in_specs=in_specs, out_specs=out_specs, check_vma=False
    )
```
